256 devices in a mesh: roll: 64 (over z, y_lo, x), tp: 4 (over y_hi, core).
Axes of the slice: x: 4, y: 4 (y_hi: 2, y_lo: 2; y = y_hi * 2 + y_lo), z: 8, core: 2. Of those that a mesh axis runs over, the one named last changes fastest.
Arguments:
- hidden_in: bfloat16 [8192, 5120], P('roll', 'tp'), may hold values from -480 to 480
- qkv_weight: bfloat16 [5120, 3584], P('roll', 'tp'), may hold values from -1 to 1
- sample_group: int32 [8192], P('roll'), may hold values from 0 to 127, as said below
- prefix_blocks: int32 [128], P('roll'), may hold values from 1 to 4, as said below
- prefix_kv: bfloat16 [128, 512, 1024], P('roll', None, 'tp'), may hold values from -24 to 24
- page_table: int32 [8192, 2], P('roll'), may hold values from 0 to 255, as said below
- suffix_pool: bfloat16 [16384, 16, 1024], P('roll', None, 'tp'), may hold values from -24 to 24
Outputs:
- attended: bfloat16 [8192, 2560], P('roll', 'tp')
The draws below stay inside these ranges and needn't reach their ends.
Inputs may be any that keep to these rules, and one draw needn't show every extreme that they name: `sample_group`: on each index of roll the 128 entries name every group exactly once. `prefix_blocks`: some group has exactly 4 blocks. `page_table`: on each index of roll the entries are a permutation of 0 to 255.
All inputs are finite; a program needn't handle non-finite values.
Results may differ from the reference program's by a relative error of at most 0.0096.
Values may be sent and summed in bfloat16 or wider, within the bound.
A program may use at most 64 MiB of HBM per device.

```python
import math
import jax
import jax.numpy as jnp
from jax import lax

D = 5120
HEADS = 20
KV_HEADS = 4
HD = 128
GROUP = 64
BLOCK = 128
MAXB = 4
PAGE = 16
SPAGES = 2
S_DEV = 128
SAMPLES = 8192
GROUPS = 128
POOL_DEV = 256
POOL = 16384
QKV = 3584
N_ROLL = 64


def kv_values(base_key, salt, shape):
    key = jax.random.fold_in(base_key, salt)
    return jnp.clip(2.0 * jax.random.normal(key, shape, jnp.float32), -12.0, 12.0).astype(jnp.bfloat16)


def draw_prefix_kv(key, part):
    return kv_values(key, 1, (GROUPS, MAXB * BLOCK, KV_HEADS * 2 * HD))


def draw_suffix_pool(key, part):
    return kv_values(key, 2, (POOL, PAGE, KV_HEADS * 2 * HD))


def draw_hidden_in(key, part):
    own = jax.random.fold_in(key, 6)
    return jnp.clip(jax.random.normal(own, (SAMPLES, D), jnp.float32), -6.0, 6.0).astype(jnp.bfloat16)


def draw_qkv_weight(key, part):
    own = jax.random.fold_in(key, 7)
    repeat = HEADS // KV_HEADS
    normal_draw = jnp.clip(jax.random.normal(own, (D, KV_HEADS, repeat + 2, HD), jnp.float32), -6.0, 6.0)
    summed = normal_draw[:, :, 0]
    for index in range(1, repeat):
        summed = summed + normal_draw[:, :, index]
    key_block = 0.6 * summed + normal_draw[:, :, repeat]
    joined = jnp.concatenate([normal_draw[:, :, :repeat], key_block[:, :, None], normal_draw[:, :, repeat + 1:]], axis=2)
    base_draw = jnp.clip(joined * D ** (-0.5), -1.0, 1.0).reshape(D, QKV)
    return base_draw.astype(jnp.bfloat16)


def draw_sample_group(key, part):
    base_ids = jnp.arange(S_DEV, dtype=jnp.int32) % GROUPS
    device_keys = jax.random.split(jax.random.fold_in(key, 3), N_ROLL)
    return jax.vmap(lambda k: jax.random.permutation(k, base_ids))(device_keys).reshape(-1).astype(jnp.int32)


def draw_prefix_blocks(key, part):
    own = jax.random.fold_in(key, 4)
    lengths = jax.random.randint(own, (GROUPS,), 1, MAXB + 1).astype(jnp.int32)
    longest = jax.random.randint(jax.random.fold_in(own, 3), (), 0, GROUPS)
    return lengths.at[longest].set(MAXB).astype(jnp.int32)


def draw_page_table(key, part):
    base_ids = jnp.arange(POOL_DEV, dtype=jnp.int32)
    device_keys = jax.random.split(jax.random.fold_in(key, 5), N_ROLL)
    tables = jax.vmap(lambda k: jax.random.permutation(k, base_ids))(device_keys)
    return tables.reshape(N_ROLL * S_DEV, SPAGES).astype(jnp.int32)


def setup_inputs(seed: int = 0) -> dict:
    key_of = jax.random.split(jax.random.key(seed), 8)
    hidden_in = draw_hidden_in(jax.random.fold_in(key_of[7], 71), 0)
    qkv_weight = draw_qkv_weight(jax.random.fold_in(key_of[7], 71), 0)
    sample_group = draw_sample_group(jax.random.fold_in(key_of[7], 71), 0)
    prefix_blocks = draw_prefix_blocks(jax.random.fold_in(key_of[7], 71), 0)
    prefix_kv = draw_prefix_kv(jax.random.fold_in(key_of[7], 71), 0)
    page_table = draw_page_table(jax.random.fold_in(key_of[7], 71), 0)
    suffix_pool = draw_suffix_pool(jax.random.fold_in(key_of[7], 71), 0)
    return {"hidden_in": hidden_in, "qkv_weight": qkv_weight, "sample_group": sample_group, "prefix_blocks": prefix_blocks, "prefix_kv": prefix_kv, "page_table": page_table, "suffix_pool": suffix_pool}


MASKED = -1e+30

def reference(hidden_in, qkv_weight, sample_group, prefix_blocks, prefix_kv, page_table, suffix_pool):
    repeat = HEADS // KV_HEADS
    score_scale = 1.0 / math.sqrt(HD)
    float_in = hidden_in.astype(jnp.float32)
    normed = (float_in * lax.rsqrt(lax.optimization_barrier(jnp.mean(float_in * float_in, axis=-1, keepdims=True)) + 1e-06)).astype(jnp.bfloat16)
    united_proj = jnp.dot(normed, qkv_weight, preferred_element_type=jnp.float32).astype(jnp.bfloat16)
    united_proj = lax.optimization_barrier(united_proj).astype(jnp.float32)
    united_proj = united_proj.reshape(SAMPLES, KV_HEADS, repeat + 2, HD)
    queries = united_proj[:, :, :repeat]
    own_key = united_proj[:, :, repeat]
    own_value = united_proj[:, :, repeat + 1]
    sort_order = jnp.argsort(sample_group, stable=True).astype(jnp.int32)
    members = sort_order.reshape(GROUPS, GROUP)

    def prefix_group(inputs):
        member_rows, kv_cache, blocks_live = inputs
        group_q = queries[member_rows]
        kv_cache = kv_cache.reshape(MAXB * BLOCK, KV_HEADS, 2, HD).astype(jnp.float32)
        scores = jnp.einsum('qjrd,tjd->qjrt', group_q, kv_cache[:, :, 0]) * score_scale
        live_mask = jnp.arange(MAXB * BLOCK) < blocks_live * BLOCK
        scores = jnp.where(live_mask, scores, MASKED)
        row_max = lax.optimization_barrier(jnp.max(scores, axis=-1))
        exponent = jnp.where(live_mask, jnp.exp(scores - row_max[..., None]), 0.0)
        row_sum = lax.optimization_barrier(jnp.sum(exponent, axis=-1))
        weights = lax.optimization_barrier((exponent / row_sum[..., None]).astype(jnp.bfloat16)).astype(jnp.float32)
        result = jnp.einsum('qjrt,tjd->qjrd', weights, kv_cache[:, :, 1])
        return (result, row_max + jnp.log(row_sum))
    group_out, group_lse = lax.map(prefix_group, (members, prefix_kv, prefix_blocks))
    prefix_out = jnp.zeros((SAMPLES, KV_HEADS, repeat, HD), jnp.float32).at[sort_order].set(group_out.reshape(SAMPLES, KV_HEADS, repeat, HD))
    prefix_lse = jnp.zeros((SAMPLES, KV_HEADS, repeat), jnp.float32).at[sort_order].set(group_lse.reshape(SAMPLES, KV_HEADS, repeat))

    def suffix_block(inputs):
        block_q, block_key, block_value, table, kv_pool = inputs
        page_rows = kv_pool[table].reshape(S_DEV, SPAGES * PAGE, KV_HEADS, 2, HD).astype(jnp.float32)
        key_rows = jnp.concatenate([page_rows[:, :, :, 0], block_key[:, None]], axis=1)
        value_rows = jnp.concatenate([page_rows[:, :, :, 1], block_value[:, None]], axis=1)
        scores = jnp.einsum('sjrd,stjd->sjrt', block_q, key_rows) * score_scale
        row_max = lax.optimization_barrier(jnp.max(scores, axis=-1))
        exponent = jnp.exp(scores - row_max[..., None])
        row_sum = lax.optimization_barrier(jnp.sum(exponent, axis=-1))
        weights = lax.optimization_barrier((exponent / row_sum[..., None]).astype(jnp.bfloat16)).astype(jnp.float32)
        result = jnp.einsum('sjrt,stjd->sjrd', weights, value_rows)
        return (result, row_max + jnp.log(row_sum))
    local_out, local_lse = lax.map(suffix_block, (queries.reshape(N_ROLL, S_DEV, KV_HEADS, repeat, HD), own_key.reshape(N_ROLL, S_DEV, KV_HEADS, HD), own_value.reshape(N_ROLL, S_DEV, KV_HEADS, HD), page_table.reshape(N_ROLL, S_DEV, SPAGES), suffix_pool.reshape(N_ROLL, POOL_DEV, PAGE, KV_HEADS * 2 * HD)))
    local_out = local_out.reshape(SAMPLES, KV_HEADS, repeat, HD)
    local_lse = local_lse.reshape(SAMPLES, KV_HEADS, repeat)
    combined = jnp.logaddexp(prefix_lse, local_lse)
    attended = jnp.exp(prefix_lse - combined)[..., None] * prefix_out + jnp.exp(local_lse - combined)[..., None] * local_out
    return attended.astype(jnp.bfloat16).reshape(SAMPLES, HEADS * HD)
```

```python
import functools
import math

import jax
import jax.numpy as jnp
from jax import lax
from jax.experimental import pallas as pl
from jax.experimental.pallas import tpu as pltpu
from jax.sharding import PartitionSpec as P

HEADS = 20
KV_HEADS = 4
HD = 128
BLOCK = 128
PAGE = 16
SPAGES = 2
D = 5120
NX, NY, NZ = 4, 2, 8
ROWS = 128
SHARD = 80
XC, ZC = 512, 384
MESH = pl.DeviceIdType.MESH


MASKED = -1e30


def softmax_parts(scores):
    row_max = jnp.max(scores, axis=-1)
    exponent = jnp.exp(scores - row_max[..., None])
    row_sum = jnp.sum(exponent, axis=-1)
    return (exponent, row_max, row_sum)


def merge_parts(first_out, first_lse, second_out, second_lse):
    combined = jnp.logaddexp(first_lse, second_lse)
    mixed = (
        jnp.exp(first_lse - combined)[..., None] * first_out
        + jnp.exp(second_lse - combined)[..., None] * second_out
    )
    return mixed.astype(jnp.bfloat16)


class Place:
    def __init__(self):
        self.r = lax.axis_index("roll")
        self.t = lax.axis_index("tp")
        self.x = lax.rem(self.r, NX)
        self.y = lax.rem(lax.div(self.r, NX), NY)
        self.z = lax.div(self.r, NX * NY)
        self.t1 = self.t + 1 - 2 * lax.rem(self.t, 2)
        self.t2 = lax.rem(self.t + 2, 4)
        self.t3 = lax.rem(self.t1 + 2, 4)
        self.ty = 1 - self.y

    def roll(self, z, y, x):
        return (z * NY + y) * NX + x

    def zn(self, k):
        return lax.rem(self.z + k + NZ, NZ)

    def xn(self, k):
        return lax.rem(self.x + k + NX, NX)

    def at_z(self, k):
        return {"roll": self.roll(self.zn(k), self.y, self.x), "tp": self.t}

    def at_x(self, k):
        return {"roll": self.roll(self.z, self.y, self.xn(k)), "tp": self.t}

    def other(self, flip_y, tp):
        y = self.ty if flip_y else self.y
        return {"roll": self.roll(self.z, y, self.x), "tp": tp}


class Sends:
    def __init__(self):
        self.copies = []

    def __call__(self, src, dst, send, recv, device):
        copy = pltpu.make_async_remote_copy(
            src_ref=src, dst_ref=dst, send_sem=send, recv_sem=recv,
            device_id=device, device_id_type=MESH,
        )
        copy.start()
        self.copies.append(copy)

    def finish(self):
        for copy in self.copies:
            copy.wait_send()


def arrived(ref, sem):
    pltpu.make_async_copy(ref, ref, sem).wait()


CHUNKS = ((0, 256), (256, 256), (512, 256), (768, 128))


def project_kernel(
    hp, w, out,
    wx, wz, ab, nb, ssq_s, ssq_r, cs, cr,
    s_ss, r_ss, s_a, r_a, s_b, r_b, s_c, r_c,
    s_xz, r_xz, s_zx, r_zx, s_xx, r_xx, s_zz, r_zz,
):
    me = Place()
    send = Sends()
    x, y, z, t = me.x, me.y, me.z, me.t
    barrier = pltpu.get_barrier_semaphore()
    peers = [
        me.at_z(1), me.at_z(-1), me.at_x(1), me.at_x(-1),
        me.other(True, t), me.other(False, me.t2), me.other(True, me.t2),
        me.other(False, me.t1), me.other(False, me.t3),
    ]
    for peer in peers:
        pl.semaphore_signal(barrier, inc=1, device_id=peer, device_id_type=MESH)

    wx[z, x] = w[:, :XC]
    wz[z, x] = w[:, XC:]
    total = jnp.zeros((ROWS, 1), jnp.float32)
    for side in range(2):
        part = hp[side].astype(jnp.float32)
        total += jnp.sum(part * part, axis=-1, keepdims=True)
    flat = jnp.broadcast_to(total, (ROWS, ROWS)).T[:8]
    ssq_s[...] = flat
    pl.semaphore_wait(barrier, len(peers))

    for k, tp in ((1, me.t1), (2, me.t2), (3, me.t3)):
        send(ssq_s, ssq_r.at[k], s_ss.at[k], r_ss.at[k], me.other(False, tp))

    XH = XC // 2
    ZH = 256
    full_x, half_x = pl.ds(0, XC), (pl.ds(0, XH), pl.ds(XH, XC - XH))
    full_z, half_z = pl.ds(0, ZC), (pl.ds(0, ZH), pl.ds(ZH, ZC - ZH))

    def xz_send(step, way):
        sign = 1 - 2 * way
        cols = full_x if step < 4 else half_x[way]
        ref = wx.at[me.zn(-sign * (step - 1)), x, :, cols]
        i = way * 4 + step - 1
        send(ref, ref, s_xz.at[i], r_xz.at[i], me.at_z(sign))

    def xz_wait(step, way):
        sign = 1 - 2 * way
        cols = full_x if step < 4 else half_x[way]
        arrived(wx.at[me.zn(-sign * step), x, :, cols], r_xz.at[way * 4 + step - 1])

    def xx_send(d, step, way):
        sign = 1 - 2 * way
        cols = full_x if step == 1 else half_x[way]
        ref = wx.at[me.zn(d), me.xn(-sign * (step - 1)), :, cols]
        i = way * 2 + step - 1
        send(ref, ref, s_xx.at[d, i], r_xx.at[d, i], me.at_x(sign))

    def xx_wait(d, step, way):
        sign = 1 - 2 * way
        cols = full_x if step == 1 else half_x[way]
        arrived(wx.at[me.zn(d), me.xn(-sign * step), :, cols], r_xx.at[d, way * 2 + step - 1])

    def zx_send(step, way):
        sign = 1 - 2 * way
        cols = full_z if step == 1 else half_z[way]
        ref = wz.at[z, me.xn(-sign * (step - 1)), :, cols]
        i = way * 2 + step - 1
        send(ref, ref, s_zx.at[i], r_zx.at[i], me.at_x(sign))

    def zx_wait(step, way):
        sign = 1 - 2 * way
        cols = full_z if step == 1 else half_z[way]
        arrived(wz.at[z, me.xn(-sign * step), :, cols], r_zx.at[way * 2 + step - 1])

    def zz_send(j, step, way):
        sign = 1 - 2 * way
        cols = full_z if step < 4 else half_z[way]
        ref = wz.at[me.zn(-sign * (step - 1)), me.xn(j), :, cols]
        i = way * 4 + step - 1
        send(ref, ref, s_zz.at[j, i], r_zz.at[j, i], me.at_z(sign))

    def zz_wait(j, step, way):
        sign = 1 - 2 * way
        cols = full_z if step < 4 else half_z[way]
        arrived(wz.at[me.zn(-sign * step), me.xn(j), :, cols], r_zz.at[j, way * 4 + step - 1])

    both = (0, 1)
    for way in both:
        xz_send(1, way)
        zx_send(1, way)
    for way in both:
        xx_send(0, 1, way)
        zz_send(0, 1, way)

    ssum = flat
    for k in (1, 2, 3):
        arrived(ssq_r.at[k], r_ss.at[k])
        ssum += ssq_r[k]
    scale = lax.rsqrt(ssum / D + 1e-06)
    scale = jnp.broadcast_to(scale[:1], (ROWS, ROWS)).T
    for side in range(2):
        for b in range(5):
            cols = slice(b * 128, b * 128 + 128)
            nb[side, :, cols] = (hp[side, :, cols].astype(jnp.float32) * scale).astype(jnp.bfloat16)
    ab[t, y] = nb[y]
    send(nb.at[me.ty], ab.at[t, y], s_a.at[0], r_a.at[0], me.other(True, t))
    send(nb.at[y], ab.at[t, y], s_a.at[1], r_a.at[1], me.other(False, me.t2))
    send(nb.at[me.ty], ab.at[t, y], s_a.at[2], r_a.at[2], me.other(True, me.t2))
    sibling = me.other(False, me.t1)
    send(nb.at[y], ab.at[t, y], s_b.at[3], r_b.at[3], sibling)

    def x_first():
        for way in both:
            zx_wait(1, way)
            zx_send(2, way)
        for j in (3, 1):
            for way in both:
                zz_send(j, 1, way)

    def xz_round(step):
        for way in both:
            xz_wait(step, way)
            if step < 4:
                xz_send(step + 1, way)
        if step < 4:
            for d in (NZ - step, step):
                for way in both:
                    xx_send(d, 1, way)
        else:
            for way in both:
                xx_send(4, 1, way)

    def zz_round(j, step):
        for way in both:
            zz_wait(j, step, way)
            if step < 4:
                zz_send(j, step + 1, way)

    def xx_round(d):
        for way in both:
            xx_wait(d, 1, way)
            xx_send(d, 2, way)

    x_first()
    xz_round(1)
    for way in both:
        zx_wait(2, way)
    for way in both:
        zz_send(2, 1, way)
    xz_round(2)
    xx_round(0)
    zz_round(0, 1)
    for i, (tp, yy) in enumerate(((t, me.ty), (me.t2, y), (me.t2, me.ty))):
        arrived(ab.at[tp, yy], r_a.at[i])
        send(ab.at[tp, yy], ab.at[tp, yy], s_b.at[i], r_b.at[i], sibling)
    xz_round(3)
    zz_round(3, 1)
    zz_round(1, 1)
    xx_round(7)
    xx_round(1)
    xz_round(4)
    zz_round(2, 1)
    zz_round(0, 2)
    xx_round(6)
    xx_round(2)
    zz_round(3, 2)
    zz_round(1, 2)
    zz_round(2, 2)
    xx_round(5)
    xx_round(3)
    zz_round(0, 3)
    zz_round(3, 3)
    zz_round(1, 3)
    zz_round(2, 3)
    xx_round(4)
    for i, (tp, yy) in enumerate(
        ((me.t1, me.ty), (me.t3, y), (me.t3, me.ty), (me.t1, y))
    ):
        arrived(ab.at[tp, yy], r_b.at[i])
    for d in range(NZ):
        for way in both:
            xx_wait(d, 2, way)
    for j in range(NX):
        zz_round(j, 4)

    partner = me.other(True, t)
    for i, (start, width) in enumerate(CHUNKS):
        src, at = (wx, start) if start < XC else (wz, start - XC)
        acc = jnp.zeros((2 * ROWS, width), jnp.float32)
        for tp in range(4):
            acc += jnp.dot(
                ab[tp].reshape(2 * ROWS, 640),
                src[2 * tp : 2 * tp + 2, :, :, at : at + width].reshape(640, width),
                preferred_element_type=jnp.float32,
            )
        cs[i, :, :, :width] = acc.reshape(2, ROWS, width)
        send(
            cs.at[i, me.ty, :, pl.ds(0, width)], cr.at[i, :, pl.ds(0, width)],
            s_c.at[i], r_c.at[i], partner,
        )
    for i, (start, width) in enumerate(CHUNKS):
        arrived(cr.at[i, :, pl.ds(0, width)], r_c.at[i])
        out[:, start : start + width] = (cs[i, y, :, :width] + cr[i, :, :width]).astype(jnp.bfloat16)
    send.finish()


def project(hidden_in, qkv_weight):
    hp = hidden_in.reshape(ROWS, 2, 2, 320).transpose(2, 0, 1, 3).reshape(2, ROWS, 640)
    dma = pltpu.SemaphoreType.DMA
    vmem = pl.BlockSpec(memory_space=pltpu.VMEM)
    sems = []
    for shape in ((4,), (3,), (4,), (4,), (8,), (4,), (8, 4), (4, 8)):
        sems += [dma(shape), dma(shape)]
    return pl.pallas_call(
        project_kernel,
        out_shape=jax.ShapeDtypeStruct((ROWS, XC + ZC), jnp.bfloat16),
        in_specs=[vmem, vmem],
        out_specs=vmem,
        scratch_shapes=[
            pltpu.VMEM((NZ, NX, SHARD, XC), jnp.bfloat16),
            pltpu.VMEM((NZ, NX, SHARD, ZC), jnp.bfloat16),
            pltpu.VMEM((4, 2, ROWS, 640), jnp.bfloat16),
            pltpu.VMEM((2, ROWS, 640), jnp.bfloat16),
            pltpu.VMEM((8, ROWS), jnp.float32),
            pltpu.VMEM((4, 8, ROWS), jnp.float32),
            pltpu.VMEM((4, 2, ROWS, 256), jnp.float32),
            pltpu.VMEM((4, ROWS, 256), jnp.float32),
            *sems,
        ],
        compiler_params=pltpu.CompilerParams(
            collective_id=0, has_side_effects=True, vmem_limit_bytes=40 * 1024 * 1024
        ),
    )(hp, qkv_weight)


def per_device(
    hidden_in, qkv_weight, sample_group, prefix_blocks, prefix_kv, page_table, suffix_pool
):
    row_count = hidden_in.shape[0]
    kv_heads_dev = prefix_kv.shape[2] // (2 * HD)
    repeat = HEADS // KV_HEADS
    q_width = kv_heads_dev * repeat * HD
    head_count = kv_heads_dev * repeat
    owned_groups = prefix_kv.shape[0]
    roll_count = lax.axis_size("roll")
    per_group = row_count // (roll_count * owned_groups)
    owner_rows = roll_count * per_group
    prefix_span = prefix_kv.shape[1]
    score_scale = 1.0 / math.sqrt(HD)
    united_proj = project(hidden_in, qkv_weight)
    united_proj = united_proj.astype(jnp.bfloat16).reshape(row_count, kv_heads_dev, repeat + 2, HD)
    queries = united_proj[:, :, :repeat]
    own_key = united_proj[:, :, repeat]
    own_value = united_proj[:, :, repeat + 1]
    sort_order = jnp.argsort(sample_group, stable=True)

    def sample_layout(arrived, width, dtype):
        return (
            jnp.zeros((row_count, width), dtype)
            .at[sort_order]
            .set(arrived.reshape(row_count, width))
        )

    page_rows = suffix_pool[page_table].reshape(row_count, SPAGES * PAGE, kv_heads_dev, 2, HD)
    key_rows = jnp.concatenate([page_rows[:, :, :, 0], own_key[:, None]], axis=1)
    value_rows = jnp.concatenate([page_rows[:, :, :, 1], own_value[:, None]], axis=1)
    scores = (
        jnp.einsum("sjrd,stjd->sjrt", queries, key_rows, preferred_element_type=jnp.float32)
        * score_scale
    )
    exponent, row_max, row_sum = softmax_parts(scores)
    weights = (exponent / row_sum[..., None]).astype(jnp.bfloat16)
    result = jnp.einsum("sjrt,stjd->sjrd", weights, value_rows, preferred_element_type=jnp.float32)
    local_out = result
    local_lse = row_max + jnp.log(row_sum)
    incoming = lax.all_to_all(
        queries.reshape(row_count, q_width)[sort_order].reshape(
            roll_count, owned_groups, per_group, q_width
        ),
        "roll",
        split_axis=0,
        concat_axis=2,
        tiled=True,
    )
    kv_cache = prefix_kv.reshape(owned_groups, prefix_span, kv_heads_dev, 2, HD)
    scores = (
        jnp.einsum(
            "gqjrd,gtjd->gqjrt",
            incoming.reshape(owned_groups, owner_rows, kv_heads_dev, repeat, HD),
            kv_cache[:, :, :, 0],
            preferred_element_type=jnp.float32,
        )
        * score_scale
    )
    live_mask = (jnp.arange(prefix_span)[None, :] < prefix_blocks[:, None] * BLOCK)[
        :, None, None, None, :
    ]
    scores = jnp.where(live_mask, scores, MASKED)
    row_max = jnp.max(scores, axis=-1)
    exponent = jnp.where(live_mask, jnp.exp(scores - row_max[..., None]), 0.0)
    row_sum = jnp.sum(exponent, axis=-1)
    weights = (exponent / row_sum[..., None]).astype(jnp.bfloat16)
    result = jnp.einsum(
        "gqjrt,gtjd->gqjrd", weights, kv_cache[:, :, :, 1], preferred_element_type=jnp.float32
    )
    result, result_lse = (result, row_max + jnp.log(row_sum))
    back_out = lax.all_to_all(
        result.reshape(1, owned_groups, owner_rows, q_width),
        "roll",
        split_axis=2,
        concat_axis=0,
        tiled=True,
    )
    back_lse = lax.all_to_all(
        result_lse.reshape(1, owned_groups, owner_rows, head_count),
        "roll",
        split_axis=2,
        concat_axis=0,
        tiled=True,
    )
    prefix_out = sample_layout(back_out, q_width, jnp.float32)
    prefix_lse = sample_layout(back_lse, head_count, jnp.float32)
    prefix_out, prefix_lse = (
        prefix_out.reshape(row_count, kv_heads_dev, repeat, HD),
        prefix_lse.reshape(row_count, kv_heads_dev, repeat),
    )
    return merge_parts(prefix_out, prefix_lse, local_out, local_lse).reshape(row_count, q_width)


def solution(mesh):
    in_specs = (
        P("roll", "tp"),
        P("roll", "tp"),
        P("roll"),
        P("roll"),
        P("roll", None, "tp"),
        P("roll", None),
        P("roll", None, "tp"),
    )
    out_specs = P("roll", "tp")
    return jax.shard_map(
        per_device, mesh=mesh, in_specs=in_specs, out_specs=out_specs, check_vma=False
    )
```

```python
import math

import jax
import jax.numpy as jnp
from jax import lax
from jax.experimental import pallas as pl
from jax.experimental.pallas import tpu as pltpu
from jax.sharding import PartitionSpec as P

HEADS = 20
KV_HEADS = 4
HD = 128
BLOCK = 128
PAGE = 16
SPAGES = 2
D = 5120
NX, NY, NZ = 4, 2, 8
ROWS = 128
SHARD = 80
XC, ZC = 512, 384
N_ROLL = NX * NY * NZ
REPEAT = HEADS // KV_HEADS
TILE = 16
SB = 16
KEYS = SPAGES * PAGE
SCALE = 1.0 / math.sqrt(HD)
MASKED = -1e30
MESH = pl.DeviceIdType.MESH


class Place:
    def __init__(self):
        self.r = lax.axis_index("roll")
        self.t = lax.axis_index("tp")
        self.x = lax.rem(self.r, NX)
        self.y = lax.rem(lax.div(self.r, NX), NY)
        self.z = lax.div(self.r, NX * NY)
        self.t1 = self.t + 1 - 2 * lax.rem(self.t, 2)
        self.t2 = lax.rem(self.t + 2, 4)
        self.t3 = lax.rem(self.t1 + 2, 4)
        self.ty = 1 - self.y

    def roll(self, z, y, x):
        return (z * NY + y) * NX + x

    def zn(self, k):
        return lax.rem(self.z + k + NZ, NZ)

    def xn(self, k):
        return lax.rem(self.x + k + NX, NX)

    def at_z(self, k):
        return {"roll": self.roll(self.zn(k), self.y, self.x), "tp": self.t}

    def at_x(self, k):
        return {"roll": self.roll(self.z, self.y, self.xn(k)), "tp": self.t}

    def other(self, flip_y, tp):
        y = self.ty if flip_y else self.y
        return {"roll": self.roll(self.z, y, self.x), "tp": tp}


class Sends:
    def __init__(self):
        self.copies = []

    def __call__(self, src, dst, send, recv, device):
        copy = pltpu.make_async_remote_copy(
            src_ref=src, dst_ref=dst, send_sem=send, recv_sem=recv,
            device_id=device, device_id_type=MESH,
        )
        copy.start()
        self.copies.append(copy)

    def finish(self):
        for copy in self.copies:
            copy.wait_send()


def arrived(ref, sem):
    pltpu.make_async_copy(ref, ref, sem).wait()


CHUNKS = ((0, 256), (256, 256), (512, 256), (768, 128))


def onehot(hit):
    return jnp.where(hit, 1.0, 0.0).astype(jnp.bfloat16)


def iota(shape, axis):
    return lax.broadcasted_iota(jnp.int32, shape, axis)


def attend_kernel(
    hp, w, group, blocks, prefix, table, pool, out,
    wx, wz, ab, nb, ssq_s, ssq_r, cs, cr,
    un, pref, pages, pick_send, pick_in, pick_out, pick_home,
    q_send, q_recv, o_send, o_recv, local_out, local_lse, gathered,
    s_ss, r_ss, s_a, r_a, s_b, r_b, s_c, r_c,
    s_xz, r_xz, s_zx, r_zx, s_xx, r_xx, s_zz, r_zz,
    load_sem, s_q, r_q, s_o, r_o,
):
    me = Place()
    send = Sends()
    x, y, z, t = me.x, me.y, me.z, me.t
    barrier = pltpu.get_barrier_semaphore()
    peers = [
        me.other(False, me.t2), me.other(True, me.t2),
        me.other(False, me.t1), me.other(False, me.t3),
    ]
    for peer in peers:
        pl.semaphore_signal(barrier, inc=1, device_id=peer, device_id_type=MESH)

    def greet(i, carry):
        peer = {"roll": lax.rem(me.r + i, N_ROLL), "tp": t}
        pl.semaphore_signal(barrier, inc=1, device_id=peer, device_id_type=MESH)
        return carry

    lax.fori_loop(1, N_ROLL, greet, 0)
    load_prefix = pltpu.make_async_copy(prefix, pref, load_sem.at[0])
    load_pages = pltpu.make_async_copy(pool, pages, load_sem.at[1])
    load_prefix.start()
    load_pages.start()

    wx[z, x] = w[:, :XC]
    wz[z, x] = w[:, XC:]
    total = jnp.zeros((ROWS, 1), jnp.float32)
    for side in range(2):
        part = hp[side].astype(jnp.float32)
        total += jnp.sum(part * part, axis=-1, keepdims=True)
    flat = jnp.broadcast_to(total, (ROWS, ROWS)).T[:8]
    ssq_s[...] = flat
    pl.semaphore_wait(barrier, len(peers) + N_ROLL - 1)

    for k, tp in ((1, me.t1), (2, me.t2), (3, me.t3)):
        send(ssq_s, ssq_r.at[k], s_ss.at[k], r_ss.at[k], me.other(False, tp))

    XH = XC // 2
    ZH = 256
    full_x, half_x = pl.ds(0, XC), (pl.ds(0, XH), pl.ds(XH, XC - XH))
    full_z, half_z = pl.ds(0, ZC), (pl.ds(0, ZH), pl.ds(ZH, ZC - ZH))

    def xz_send(step, way):
        sign = 1 - 2 * way
        cols = full_x if step < 4 else half_x[way]
        ref = wx.at[me.zn(-sign * (step - 1)), x, :, cols]
        i = way * 4 + step - 1
        send(ref, ref, s_xz.at[i], r_xz.at[i], me.at_z(sign))

    def xz_wait(step, way):
        sign = 1 - 2 * way
        cols = full_x if step < 4 else half_x[way]
        arrived(wx.at[me.zn(-sign * step), x, :, cols], r_xz.at[way * 4 + step - 1])

    def xx_send(d, step, way):
        sign = 1 - 2 * way
        cols = full_x if step == 1 else half_x[way]
        ref = wx.at[me.zn(d), me.xn(-sign * (step - 1)), :, cols]
        i = way * 2 + step - 1
        send(ref, ref, s_xx.at[d, i], r_xx.at[d, i], me.at_x(sign))

    def xx_wait(d, step, way):
        sign = 1 - 2 * way
        cols = full_x if step == 1 else half_x[way]
        arrived(wx.at[me.zn(d), me.xn(-sign * step), :, cols], r_xx.at[d, way * 2 + step - 1])

    def zx_send(step, way):
        sign = 1 - 2 * way
        cols = full_z if step == 1 else half_z[way]
        ref = wz.at[z, me.xn(-sign * (step - 1)), :, cols]
        i = way * 2 + step - 1
        send(ref, ref, s_zx.at[i], r_zx.at[i], me.at_x(sign))

    def zx_wait(step, way):
        sign = 1 - 2 * way
        cols = full_z if step == 1 else half_z[way]
        arrived(wz.at[z, me.xn(-sign * step), :, cols], r_zx.at[way * 2 + step - 1])

    def zz_send(j, step, way):
        sign = 1 - 2 * way
        cols = full_z if step < 4 else half_z[way]
        ref = wz.at[me.zn(-sign * (step - 1)), me.xn(j), :, cols]
        i = way * 4 + step - 1
        send(ref, ref, s_zz.at[j, i], r_zz.at[j, i], me.at_z(sign))

    def zz_wait(j, step, way):
        sign = 1 - 2 * way
        cols = full_z if step < 4 else half_z[way]
        arrived(wz.at[me.zn(-sign * step), me.xn(j), :, cols], r_zz.at[j, way * 4 + step - 1])

    both = (0, 1)
    for way in both:
        xz_send(1, way)
        zx_send(1, way)
    for way in both:
        xx_send(0, 1, way)
        zz_send(0, 1, way)

    ssum = flat
    for k in (1, 2, 3):
        arrived(ssq_r.at[k], r_ss.at[k])
        ssum += ssq_r[k]
    scale = lax.rsqrt(ssum / D + 1e-06)
    scale = jnp.broadcast_to(scale[:1], (ROWS, ROWS)).T
    for side in range(2):
        for b in range(5):
            cols = slice(b * 128, b * 128 + 128)
            nb[side, :, cols] = (hp[side, :, cols].astype(jnp.float32) * scale).astype(jnp.bfloat16)
    ab[t, y] = nb[y]
    send(nb.at[me.ty], ab.at[t, y], s_a.at[0], r_a.at[0], me.other(True, t))
    send(nb.at[y], ab.at[t, y], s_a.at[1], r_a.at[1], me.other(False, me.t2))
    send(nb.at[me.ty], ab.at[t, y], s_a.at[2], r_a.at[2], me.other(True, me.t2))
    sibling = me.other(False, me.t1)
    send(nb.at[y], ab.at[t, y], s_b.at[3], r_b.at[3], sibling)

    def x_first():
        for way in both:
            zx_wait(1, way)
            zx_send(2, way)
        for j in (3, 1):
            for way in both:
                zz_send(j, 1, way)

    def xz_round(step):
        for way in both:
            xz_wait(step, way)
            if step < 4:
                xz_send(step + 1, way)
        if step < 4:
            for d in (NZ - step, step):
                for way in both:
                    xx_send(d, 1, way)
        else:
            for way in both:
                xx_send(4, 1, way)

    def zz_round(j, step):
        for way in both:
            zz_wait(j, step, way)
            if step < 4:
                zz_send(j, step + 1, way)

    def xx_round(d):
        for way in both:
            xx_wait(d, 1, way)
            xx_send(d, 2, way)

    slot = lax.shift_right_logical(group[...], 1) * TILE + jnp.bitwise_and(group[...], 1) * REPEAT
    slot_rows = jnp.broadcast_to(slot, (ROWS, ROWS)).T
    group_rows = jnp.broadcast_to(group[...], (ROWS, ROWS)).T

    def build_send():
        for h in range(REPEAT):
            pick_send[:, h * ROWS : (h + 1) * ROWS] = onehot(iota((N_ROLL * TILE, ROWS), 0) == slot + h)

    def build_in():
        for i in range(2 * REPEAT):
            target = iota((N_ROLL, N_ROLL * TILE), 0) * TILE + i
            pick_in[i * N_ROLL : (i + 1) * N_ROLL, :] = onehot(iota((N_ROLL, N_ROLL * TILE), 1) == target)

    def build_out():
        for i in range(2 * REPEAT):
            lane = iota((N_ROLL * TILE, ROWS), 1) + (i % REPEAT) * ROWS
            row = lax.shift_right_logical(lane, 6) if i < REPEAT else 2 * REPEAT
            target = jnp.bitwise_and(lane, N_ROLL - 1) * TILE + row
            pick_out[:, i * ROWS : (i + 1) * ROWS] = onehot(iota((N_ROLL * TILE, ROWS), 0) == target)

    def build_home():
        for b in range(N_ROLL * TILE // ROWS):
            column = iota((ROWS, ROWS), 1) + b * ROWS
            for h in range(REPEAT):
                pick_home[h * ROWS : (h + 1) * ROWS, b * ROWS : (b + 1) * ROWS] = onehot(column == slot_rows + h)
            target = lax.shift_right_logical(group_rows, 1) * TILE + 2 * REPEAT
            pick_home[REPEAT * ROWS :, b * ROWS : (b + 1) * ROWS] = onehot(column == target)

    def gather_pages():
        load_pages.wait()

        def one(s, carry):
            for j in range(SPAGES):
                gathered[s, j] = pages[table[s, j]]
            return carry

        lax.fori_loop(0, ROWS, one, 0, unroll=8)

    x_first()
    xz_round(1)
    for way in both:
        zx_wait(2, way)
    for way in both:
        zz_send(2, 1, way)
    xz_round(2)
    xx_round(0)
    zz_round(0, 1)
    for i, (tp, yy) in enumerate(((t, me.ty), (me.t2, y), (me.t2, me.ty))):
        arrived(ab.at[tp, yy], r_a.at[i])
        send(ab.at[tp, yy], ab.at[tp, yy], s_b.at[i], r_b.at[i], sibling)
    build_send()
    xz_round(3)
    zz_round(3, 1)
    zz_round(1, 1)
    xx_round(7)
    xx_round(1)
    build_in()
    xz_round(4)
    zz_round(2, 1)
    zz_round(0, 2)
    xx_round(6)
    xx_round(2)
    build_out()
    zz_round(3, 2)
    zz_round(1, 2)
    zz_round(2, 2)
    xx_round(5)
    xx_round(3)
    build_home()
    zz_round(0, 3)
    zz_round(3, 3)
    zz_round(1, 3)
    zz_round(2, 3)
    xx_round(4)
    gather_pages()
    for i, (tp, yy) in enumerate(
        ((me.t1, me.ty), (me.t3, y), (me.t3, me.ty), (me.t1, y))
    ):
        arrived(ab.at[tp, yy], r_b.at[i])
    for d in range(NZ):
        for way in both:
            xx_wait(d, 2, way)
    for j in range(NX):
        zz_round(j, 4)

    partner = me.other(True, t)
    for i, (start, width) in enumerate(CHUNKS):
        src, at = (wx, start) if start < XC else (wz, start - XC)
        acc = jnp.zeros((2 * ROWS, width), jnp.float32)
        for tp in range(4):
            acc += jnp.dot(
                ab[tp].reshape(2 * ROWS, 640),
                src[2 * tp : 2 * tp + 2, :, :, at : at + width].reshape(640, width),
                preferred_element_type=jnp.float32,
            )
        cs[i, :, :, :width] = acc.reshape(2, ROWS, width)
        send(
            cs.at[i, me.ty, :, pl.ds(0, width)], cr.at[i, :, pl.ds(0, width)],
            s_c.at[i], r_c.at[i], partner,
        )
    for i, (start, width) in enumerate(CHUNKS):
        arrived(cr.at[i, :, pl.ds(0, width)], r_c.at[i])
        un[:, start : start + width] = (cs[i, y, :, :width] + cr[i, :, :width]).astype(jnp.bfloat16)

    rows = jnp.concatenate([un[:, h * HD : (h + 1) * HD] for h in range(REPEAT)], axis=0)
    q_send[...] = jnp.dot(pick_send[...], rows, preferred_element_type=jnp.float32).astype(
        jnp.bfloat16
    ).reshape(N_ROLL, TILE, HD)

    def exchange(src, dst, s_sem, r_sem):
        def one(i, carry):
            peer = lax.rem(me.r + i, N_ROLL)
            pltpu.make_async_remote_copy(
                src_ref=src.at[peer], dst_ref=dst.at[me.r], send_sem=s_sem, recv_sem=r_sem,
                device_id={"roll": peer, "tp": t}, device_id_type=MESH,
            ).start()
            return carry

        lax.fori_loop(1, N_ROLL, one, 0)
        dst[me.r] = src[me.r]

    exchange(q_send, q_recv, s_q, r_q)

    def local_block(b, carry):
        at = pl.ds(pl.multiple_of(b * SB, SB), SB)
        queries = jnp.concatenate([un[at, h * HD : (h + 1) * HD] for h in range(REPEAT)], axis=0)
        own_k = un[at, REPEAT * HD : (REPEAT + 1) * HD].astype(jnp.float32)
        own_v = un[at, (REPEAT + 1) * HD :].astype(jnp.float32)
        own_k = jnp.concatenate([own_k] * REPEAT, axis=0)
        own_v = jnp.concatenate([own_v] * REPEAT, axis=0)
        keys = gathered[at, :, :, :HD].reshape(SB * KEYS, HD)
        values = gathered[at, :, :, HD:].reshape(SB * KEYS, HD)
        scores = lax.dot_general(
            queries, keys, (((1,), (1,)), ((), ())), preferred_element_type=jnp.float32
        ) * SCALE
        shape = (REPEAT * SB, SB * KEYS)
        mine = jnp.bitwise_and(iota(shape, 0), SB - 1) == lax.shift_right_logical(iota(shape, 1), 5)
        scores = jnp.where(mine, scores, MASKED)
        own = jnp.sum(queries.astype(jnp.float32) * own_k, axis=-1, keepdims=True) * SCALE
        top = jnp.maximum(jnp.max(scores, axis=-1, keepdims=True), own)
        e = jnp.exp(scores - top)
        e_own = jnp.exp(own - top)
        total = jnp.sum(e, axis=-1, keepdims=True) + e_own
        weights = (e / total).astype(jnp.bfloat16)
        w_own = (e_own / total).astype(jnp.bfloat16).astype(jnp.float32)
        res = jnp.dot(weights, values, preferred_element_type=jnp.float32) + w_own * own_v
        lse = jnp.broadcast_to(top + jnp.log(total), (REPEAT * SB, HD))
        for h in range(REPEAT):
            local_out[h, at, :] = res[h * SB : (h + 1) * SB]
            local_lse[h, at, :] = lse[h * SB : (h + 1) * SB]
        return carry

    lax.fori_loop(0, ROWS // SB, local_block, 0)

    load_prefix.wait()
    arrived(q_recv.at[pl.ds(0, N_ROLL - 1)], r_q)
    came = q_recv[...].reshape(N_ROLL * TILE, HD)
    outs, marks = [], []
    per = REPEAT * N_ROLL
    for j in range(2):
        queries = jnp.dot(
            pick_in[j * per : (j + 1) * per, :], came, preferred_element_type=jnp.float32
        ).astype(jnp.bfloat16)
        scores = lax.dot_general(
            queries, pref[j, :, :HD], (((1,), (1,)), ((), ())), preferred_element_type=jnp.float32
        ) * SCALE
        scores = jnp.where(iota(scores.shape, 1) < blocks[j] * BLOCK, scores, MASKED)
        top = jnp.max(scores, axis=-1, keepdims=True)
        e = jnp.exp(scores - top)
        total = jnp.sum(e, axis=-1, keepdims=True)
        weights = (e / total).astype(jnp.bfloat16)
        res = jnp.dot(weights, pref[j, :, HD:], preferred_element_type=jnp.float32)
        outs.append(res.astype(jnp.bfloat16))
        lse = jnp.broadcast_to(top + jnp.log(total), (per, HD))
        hi = lse.astype(jnp.bfloat16).astype(jnp.float32)
        mid = (lse - hi).astype(jnp.bfloat16).astype(jnp.float32)
        low = lse - hi - mid
        lane = iota((per, HD), 1)
        first = (lax.shift_right_logical(iota((per, HD), 0), 6) + j * REPEAT) * 3
        mark = jnp.where(lane == first, hi, jnp.where(lane == first + 1, mid, jnp.where(lane == first + 2, low, 0.0)))
        marks.append(mark.astype(jnp.bfloat16))
    stacked = jnp.concatenate(outs + marks, axis=0)
    o_send[...] = jnp.dot(pick_out[...], stacked, preferred_element_type=jnp.float32).astype(
        jnp.bfloat16
    ).reshape(N_ROLL, TILE, HD)
    exchange(o_send, o_recv, s_o, r_o)

    arrived(o_recv.at[pl.ds(0, N_ROLL - 1)], r_o)
    back = jnp.dot(
        pick_home[...], o_recv[...].reshape(N_ROLL * TILE, HD), preferred_element_type=jnp.float32
    )
    terms = back[REPEAT * ROWS :]
    second = jnp.bitwise_and(group_rows, 1) * REPEAT
    lane = iota((ROWS, HD), 1)
    for h in range(REPEAT):
        first = (second + h) * 3
        mine = jnp.where((lane >= first) & (lane < first + 3), terms, 0.0)
        p_lse = jnp.broadcast_to(jnp.sum(mine, axis=-1, keepdims=True), (ROWS, HD))
        l_lse = local_lse[h]
        top = jnp.maximum(p_lse, l_lse)
        ep = jnp.exp(p_lse - top)
        el = jnp.exp(l_lse - top)
        mixed = (ep * back[h * ROWS : (h + 1) * ROWS] + el * local_out[h]) / (ep + el)
        out[:, h * HD : (h + 1) * HD] = mixed.astype(jnp.bfloat16)

    arrived(q_send.at[pl.ds(0, N_ROLL - 1)], s_q)
    arrived(o_send.at[pl.ds(0, N_ROLL - 1)], s_o)
    send.finish()


def per_device(
    hidden_in, qkv_weight, sample_group, prefix_blocks, prefix_kv, page_table, suffix_pool
):
    hp = hidden_in.reshape(ROWS, 2, 2, 320).transpose(2, 0, 1, 3).reshape(2, ROWS, 640)
    dma = pltpu.SemaphoreType.DMA
    vmem = pl.BlockSpec(memory_space=pltpu.VMEM)
    smem = pl.BlockSpec(memory_space=pltpu.SMEM)
    hbm = pl.BlockSpec(memory_space=pl.ANY)
    bf16, f32 = jnp.bfloat16, jnp.float32
    sems = []
    for shape in ((4,), (3,), (4,), (4,), (8,), (4,), (8, 4), (4, 8)):
        sems += [dma(shape), dma(shape)]
    tiles = pltpu.VMEM((N_ROLL, TILE, HD), bf16)
    return pl.pallas_call(
        attend_kernel,
        out_shape=jax.ShapeDtypeStruct((ROWS, REPEAT * HD), bf16),
        in_specs=[vmem, vmem, vmem, smem, hbm, smem, hbm],
        out_specs=vmem,
        scratch_shapes=[
            pltpu.VMEM((NZ, NX, SHARD, XC), bf16),
            pltpu.VMEM((NZ, NX, SHARD, ZC), bf16),
            pltpu.VMEM((4, 2, ROWS, 640), bf16),
            pltpu.VMEM((2, ROWS, 640), bf16),
            pltpu.VMEM((8, ROWS), f32),
            pltpu.VMEM((4, 8, ROWS), f32),
            pltpu.VMEM((4, 2, ROWS, 256), f32),
            pltpu.VMEM((4, ROWS, 256), f32),
            pltpu.VMEM((ROWS, XC + ZC), bf16),
            pltpu.VMEM(prefix_kv.shape, bf16),
            pltpu.VMEM(suffix_pool.shape, bf16),
            pltpu.VMEM((N_ROLL * TILE, REPEAT * ROWS), bf16),
            pltpu.VMEM((2 * REPEAT * N_ROLL, N_ROLL * TILE), bf16),
            pltpu.VMEM((N_ROLL * TILE, 2 * REPEAT * ROWS), bf16),
            pltpu.VMEM(((REPEAT + 1) * ROWS, N_ROLL * TILE), bf16),
            tiles, tiles, tiles, tiles,
            pltpu.VMEM((REPEAT, ROWS, HD), f32),
            pltpu.VMEM((REPEAT, ROWS, HD), f32),
            pltpu.VMEM((ROWS, SPAGES, PAGE, 2 * HD), bf16),
            *sems,
            dma((2,)), dma, dma, dma, dma,
        ],
        compiler_params=pltpu.CompilerParams(
            collective_id=0, has_side_effects=True, vmem_limit_bytes=48 * 1024 * 1024
        ),
    )(hp, qkv_weight, sample_group.reshape(1, ROWS), prefix_blocks, prefix_kv, page_table, suffix_pool)


def solution(mesh):
    in_specs = (
        P("roll", "tp"),
        P("roll", "tp"),
        P("roll"),
        P("roll"),
        P("roll", None, "tp"),
        P("roll", None),
        P("roll", None, "tp"),
    )
    out_specs = P("roll", "tp")
    return jax.shard_map(
        per_device, mesh=mesh, in_specs=in_specs, out_specs=out_specs, check_vma=False
    )
```

```python
import math

import jax
import jax.numpy as jnp
from jax import lax
from jax.experimental import pallas as pl
from jax.experimental.pallas import tpu as pltpu
from jax.sharding import PartitionSpec as P

HEADS = 20
KV_HEADS = 4
HD = 128
BLOCK = 128
PAGE = 16
SPAGES = 2
D = 5120
NX, NY, NZ = 4, 2, 8
ROWS = 128
SHARD = 80
XC, ZC = 512, 384
N_ROLL = NX * NY * NZ
REPEAT = HEADS // KV_HEADS
TILE = 16
SB = 16
KEYS = SPAGES * PAGE
SCALE = 1.0 / math.sqrt(HD)
MASKED = -1e30
MESH = pl.DeviceIdType.MESH


class Place:
    def __init__(self):
        self.r = lax.axis_index("roll")
        self.t = lax.axis_index("tp")
        self.x = lax.rem(self.r, NX)
        self.y = lax.rem(lax.div(self.r, NX), NY)
        self.z = lax.div(self.r, NX * NY)
        self.t1 = self.t + 1 - 2 * lax.rem(self.t, 2)
        self.t2 = lax.rem(self.t + 2, 4)
        self.t3 = lax.rem(self.t1 + 2, 4)
        self.ty = 1 - self.y

    def roll(self, z, y, x):
        return (z * NY + y) * NX + x

    def zn(self, k):
        return lax.rem(self.z + k + NZ, NZ)

    def xn(self, k):
        return lax.rem(self.x + k + NX, NX)

    def at_z(self, k):
        return {"roll": self.roll(self.zn(k), self.y, self.x), "tp": self.t}

    def at_x(self, k):
        return {"roll": self.roll(self.z, self.y, self.xn(k)), "tp": self.t}

    def other(self, flip_y, tp):
        y = self.ty if flip_y else self.y
        return {"roll": self.roll(self.z, y, self.x), "tp": tp}


class Sends:
    def __init__(self):
        self.copies = []

    def __call__(self, src, dst, send, recv, device):
        copy = pltpu.make_async_remote_copy(
            src_ref=src, dst_ref=dst, send_sem=send, recv_sem=recv,
            device_id=device, device_id_type=MESH,
        )
        copy.start()
        self.copies.append(copy)

    def finish(self):
        for copy in self.copies:
            copy.wait_send()


def arrived(ref, sem):
    pltpu.make_async_copy(ref, ref, sem).wait()


CHUNKS = ((0, 256), (256, 256), (512, 256), (768, 128))


def onehot(hit):
    return jnp.where(hit, 1.0, 0.0).astype(jnp.bfloat16)


def iota(shape, axis):
    return lax.broadcasted_iota(jnp.int32, shape, axis)


def attend_kernel(
    hidden_hbm, w_hbm, group_hbm, blocks, prefix, table_hbm, pool, out,
    hidden, w, group, table,
    wx, wz, ab, nb, ssq_s, ssq_r, cs, cr,
    un, pref, pages, pick_send, pick_in, pick_out, pick_home,
    q_send, q_recv, o_send, o_recv, local_out, local_lse, gathered,
    s_ss, r_ss, s_a, r_a, s_b, r_b, s_c, r_c,
    s_xz, r_xz, s_zx, r_zx, s_xx, r_xx, s_zz, r_zz,
    load_sem, s_q, r_q, s_o, r_o,
):
    me = Place()
    send = Sends()
    x, y, z, t = me.x, me.y, me.z, me.t
    barrier = pltpu.get_barrier_semaphore()
    peers = [
        me.at_z(1), me.at_z(-1), me.at_x(1), me.at_x(-1),
        me.other(True, t), me.other(False, me.t2), me.other(True, me.t2),
        me.other(False, me.t1), me.other(False, me.t3),
    ]
    for peer in peers:
        pl.semaphore_signal(barrier, inc=1, device_id=peer, device_id_type=MESH)
    load_hidden = pltpu.make_async_copy(hidden_hbm, hidden, load_sem.at[2])
    load_w = pltpu.make_async_copy(w_hbm, w, load_sem.at[3])
    load_group = pltpu.make_async_copy(group_hbm, group, load_sem.at[4])
    load_table = pltpu.make_async_copy(table_hbm, table, load_sem.at[5])
    load_hidden.start()
    load_w.start()
    load_group.start()
    load_table.start()
    load_prefix = pltpu.make_async_copy(prefix, pref, load_sem.at[0])
    load_pages = pltpu.make_async_copy(pool, pages, load_sem.at[1])
    load_prefix.start()
    load_pages.start()

    load_w.wait()
    wx[z, x] = w[:, :XC]
    wz[z, x] = w[:, XC:]
    load_hidden.wait()
    total = jnp.zeros((ROWS, HD), jnp.float32)
    for b in range(10):
        part = hidden[:, b * HD : (b + 1) * HD].astype(jnp.float32)
        total += part * part
    total = jnp.sum(total, axis=-1, keepdims=True)
    flat = jnp.broadcast_to(total, (ROWS, ROWS)).T[:8]
    ssq_s[...] = flat
    load_group.wait()
    load_table.wait()
    slot = lax.shift_right_logical(group[...], 1) * TILE + jnp.bitwise_and(group[...], 1) * REPEAT
    slot_rows = jnp.broadcast_to(slot, (ROWS, ROWS)).T
    group_rows = jnp.broadcast_to(group[...], (ROWS, ROWS)).T

    def build_send():
        for h in range(REPEAT):
            pick_send[:, h * ROWS : (h + 1) * ROWS] = onehot(iota((N_ROLL * TILE, ROWS), 0) == slot + h)

    def build_in():
        for i in range(2 * REPEAT):
            target = iota((N_ROLL, N_ROLL * TILE), 0) * TILE + i
            pick_in[i * N_ROLL : (i + 1) * N_ROLL, :] = onehot(iota((N_ROLL, N_ROLL * TILE), 1) == target)

    def build_out():
        for i in range(2 * REPEAT):
            lane = iota((N_ROLL * TILE, ROWS), 1) + (i % REPEAT) * ROWS
            row = lax.shift_right_logical(lane, 6) if i < REPEAT else 2 * REPEAT
            target = jnp.bitwise_and(lane, N_ROLL - 1) * TILE + row
            pick_out[:, i * ROWS : (i + 1) * ROWS] = onehot(iota((N_ROLL * TILE, ROWS), 0) == target)

    def build_home():
        for b in range(N_ROLL * TILE // ROWS):
            column = iota((ROWS, ROWS), 1) + b * ROWS
            for h in range(REPEAT):
                pick_home[h * ROWS : (h + 1) * ROWS, b * ROWS : (b + 1) * ROWS] = onehot(column == slot_rows + h)
            target = lax.shift_right_logical(group_rows, 1) * TILE + 2 * REPEAT
            pick_home[REPEAT * ROWS :, b * ROWS : (b + 1) * ROWS] = onehot(column == target)

    def gather_pages():
        load_pages.wait()

        def one(s, carry):
            for j in range(SPAGES):
                gathered[s, j] = pages[table[j, s]]
            return carry

        lax.fori_loop(0, ROWS, one, 0, unroll=8)

    pl.semaphore_wait(barrier, len(peers))

    for k, tp in ((1, me.t1), (2, me.t2), (3, me.t3)):
        send(ssq_s, ssq_r.at[k], s_ss.at[k], r_ss.at[k], me.other(False, tp))

    XH = XC // 2
    ZH = 256
    full_x, half_x = pl.ds(0, XC), (pl.ds(0, XH), pl.ds(XH, XC - XH))
    full_z, half_z = pl.ds(0, ZC), (pl.ds(0, ZH), pl.ds(ZH, ZC - ZH))

    def xz_send(step, way):
        sign = 1 - 2 * way
        cols = full_x if step < 4 else half_x[way]
        ref = wx.at[me.zn(-sign * (step - 1)), x, :, cols]
        i = way * 4 + step - 1
        send(ref, ref, s_xz.at[i], r_xz.at[i], me.at_z(sign))

    def xz_wait(step, way):
        sign = 1 - 2 * way
        cols = full_x if step < 4 else half_x[way]
        arrived(wx.at[me.zn(-sign * step), x, :, cols], r_xz.at[way * 4 + step - 1])

    def xx_send(d, step, way):
        sign = 1 - 2 * way
        cols = full_x if step == 1 else half_x[way]
        ref = wx.at[me.zn(d), me.xn(-sign * (step - 1)), :, cols]
        i = way * 2 + step - 1
        send(ref, ref, s_xx.at[d, i], r_xx.at[d, i], me.at_x(sign))

    def xx_wait(d, step, way):
        sign = 1 - 2 * way
        cols = full_x if step == 1 else half_x[way]
        arrived(wx.at[me.zn(d), me.xn(-sign * step), :, cols], r_xx.at[d, way * 2 + step - 1])

    def zx_send(step, way):
        sign = 1 - 2 * way
        cols = full_z if step == 1 else half_z[way]
        ref = wz.at[z, me.xn(-sign * (step - 1)), :, cols]
        i = way * 2 + step - 1
        send(ref, ref, s_zx.at[i], r_zx.at[i], me.at_x(sign))

    def zx_wait(step, way):
        sign = 1 - 2 * way
        cols = full_z if step == 1 else half_z[way]
        arrived(wz.at[z, me.xn(-sign * step), :, cols], r_zx.at[way * 2 + step - 1])

    def zz_send(j, step, way):
        sign = 1 - 2 * way
        cols = full_z if step < 4 else half_z[way]
        ref = wz.at[me.zn(-sign * (step - 1)), me.xn(j), :, cols]
        i = way * 4 + step - 1
        send(ref, ref, s_zz.at[j, i], r_zz.at[j, i], me.at_z(sign))

    def zz_wait(j, step, way):
        sign = 1 - 2 * way
        cols = full_z if step < 4 else half_z[way]
        arrived(wz.at[me.zn(-sign * step), me.xn(j), :, cols], r_zz.at[j, way * 4 + step - 1])

    both = (0, 1)
    for way in both:
        xz_send(1, way)
        zx_send(1, way)
    for way in both:
        xx_send(0, 1, way)
        zz_send(0, 1, way)

    ssum = flat
    for k in (1, 2, 3):
        arrived(ssq_r.at[k], r_ss.at[k])
        ssum += ssq_r[k]
    scale = lax.rsqrt(ssum / D + 1e-06)
    scale = jnp.broadcast_to(scale[:1], (ROWS, ROWS)).T
    tiles = [hidden[:, b * HD : (b + 1) * HD].astype(jnp.float32) * scale for b in range(10)]
    turned = {b: pltpu.roll(tiles[b], HD // 2, 1) for b in range(2, 8)}
    low_half = iota((ROWS, HD), 1) < HD // 2

    def halves(first, second):
        return jnp.where(low_half, first, second)

    sides = (
        (tiles[0], tiles[1], halves(tiles[2], turned[5]), halves(turned[5], turned[6]), halves(turned[6], turned[7])),
        (halves(turned[2], turned[3]), halves(turned[3], turned[4]), halves(turned[4], tiles[7]), tiles[8], tiles[9]),
    )
    for side in range(2):
        for b in range(5):
            nb[side, :, b * HD : (b + 1) * HD] = sides[side][b].astype(jnp.bfloat16)
    ab[t, y] = nb[y]
    send(nb.at[me.ty], ab.at[t, y], s_a.at[0], r_a.at[0], me.other(True, t))
    send(nb.at[y], ab.at[t, y], s_a.at[1], r_a.at[1], me.other(False, me.t2))
    send(nb.at[me.ty], ab.at[t, y], s_a.at[2], r_a.at[2], me.other(True, me.t2))
    sibling = me.other(False, me.t1)
    send(nb.at[y], ab.at[t, y], s_b.at[3], r_b.at[3], sibling)

    def x_first():
        for way in both:
            zx_wait(1, way)
            zx_send(2, way)
        for j in (3, 1):
            for way in both:
                zz_send(j, 1, way)

    def xz_round(step):
        for way in both:
            xz_wait(step, way)
            if step < 4:
                xz_send(step + 1, way)
        if step < 4:
            for d in (NZ - step, step):
                for way in both:
                    xx_send(d, 1, way)
        else:
            for way in both:
                xx_send(4, 1, way)

    def zz_round(j, step):
        for way in both:
            zz_wait(j, step, way)
            if step < 4:
                zz_send(j, step + 1, way)

    def xx_round(d):
        for way in both:
            xx_wait(d, 1, way)
            xx_send(d, 2, way)

    build_send()
    x_first()
    xz_round(1)
    build_in()
    for way in both:
        zx_wait(2, way)
    for way in both:
        zz_send(2, 1, way)
    xz_round(2)
    xx_round(0)
    zz_round(0, 1)
    for i, (tp, yy) in enumerate(((t, me.ty), (me.t2, y), (me.t2, me.ty))):
        arrived(ab.at[tp, yy], r_a.at[i])
        send(ab.at[tp, yy], ab.at[tp, yy], s_b.at[i], r_b.at[i], sibling)
    build_out()
    xz_round(3)
    zz_round(3, 1)
    zz_round(1, 1)
    xx_round(7)
    xx_round(1)
    xz_round(4)
    zz_round(2, 1)
    zz_round(0, 2)
    xx_round(6)
    xx_round(2)
    build_home()
    zz_round(3, 2)
    zz_round(1, 2)
    zz_round(2, 2)
    xx_round(5)
    xx_round(3)
    zz_round(0, 3)
    zz_round(3, 3)
    zz_round(1, 3)
    zz_round(2, 3)
    xx_round(4)
    gather_pages()
    for i, (tp, yy) in enumerate(
        ((me.t1, me.ty), (me.t3, y), (me.t3, me.ty), (me.t1, y))
    ):
        arrived(ab.at[tp, yy], r_b.at[i])
    for d in range(NZ):
        for way in both:
            xx_wait(d, 2, way)
    for j in range(NX):
        zz_round(j, 4)

    partner = me.other(True, t)
    for i, (start, width) in enumerate(CHUNKS):
        src, at = (wx, start) if start < XC else (wz, start - XC)
        acc = jnp.zeros((2 * ROWS, width), jnp.float32)
        for tp in range(4):
            acc += jnp.dot(
                ab[tp].reshape(2 * ROWS, 640),
                src[2 * tp : 2 * tp + 2, :, :, at : at + width].reshape(640, width),
                preferred_element_type=jnp.float32,
            )
        cs[i, :, :, :width] = acc.reshape(2, ROWS, width)
        send(
            cs.at[i, me.ty, :, pl.ds(0, width)], cr.at[i, :, pl.ds(0, width)],
            s_c.at[i], r_c.at[i], partner,
        )
    for i, (start, width) in enumerate(CHUNKS):
        arrived(cr.at[i, :, pl.ds(0, width)], r_c.at[i])
        un[:, start : start + width] = (cs[i, y, :, :width] + cr[i, :, :width]).astype(jnp.bfloat16)

    rows = jnp.concatenate([un[:, h * HD : (h + 1) * HD] for h in range(REPEAT)], axis=0)
    q_send[...] = jnp.dot(pick_send[...], rows, preferred_element_type=jnp.float32).astype(
        jnp.bfloat16
    ).reshape(N_ROLL, TILE, HD)

    def exchange(src, dst, s_sem, r_sem):
        def one(i, carry):
            peer = lax.rem(me.r + i, N_ROLL)
            pltpu.make_async_remote_copy(
                src_ref=src.at[peer], dst_ref=dst.at[me.r], send_sem=s_sem, recv_sem=r_sem,
                device_id={"roll": peer, "tp": t}, device_id_type=MESH,
            ).start()
            return carry

        lax.fori_loop(1, N_ROLL, one, 0)
        dst[me.r] = src[me.r]

    exchange(q_send, q_recv, s_q, r_q)

    def local_block(b, carry):
        at = pl.ds(pl.multiple_of(b * SB, SB), SB)
        queries = jnp.concatenate([un[at, h * HD : (h + 1) * HD] for h in range(REPEAT)], axis=0)
        own_k = un[at, REPEAT * HD : (REPEAT + 1) * HD].astype(jnp.float32)
        own_v = un[at, (REPEAT + 1) * HD :].astype(jnp.float32)
        own_k = jnp.concatenate([own_k] * REPEAT, axis=0)
        own_v = jnp.concatenate([own_v] * REPEAT, axis=0)
        keys = gathered[at, :, :, :HD].reshape(SB * KEYS, HD)
        values = gathered[at, :, :, HD:].reshape(SB * KEYS, HD)
        scores = lax.dot_general(
            queries, keys, (((1,), (1,)), ((), ())), preferred_element_type=jnp.float32
        ) * SCALE
        shape = (REPEAT * SB, SB * KEYS)
        mine = jnp.bitwise_and(iota(shape, 0), SB - 1) == lax.shift_right_logical(iota(shape, 1), 5)
        scores = jnp.where(mine, scores, MASKED)
        own = jnp.sum(queries.astype(jnp.float32) * own_k, axis=-1, keepdims=True) * SCALE
        top = jnp.maximum(jnp.max(scores, axis=-1, keepdims=True), own)
        e = jnp.exp(scores - top)
        e_own = jnp.exp(own - top)
        total = jnp.sum(e, axis=-1, keepdims=True) + e_own
        weights = (e / total).astype(jnp.bfloat16)
        w_own = (e_own / total).astype(jnp.bfloat16).astype(jnp.float32)
        res = jnp.dot(weights, values, preferred_element_type=jnp.float32) + w_own * own_v
        lse = jnp.broadcast_to(top + jnp.log(total), (REPEAT * SB, HD))
        for h in range(REPEAT):
            local_out[h, at, :] = res[h * SB : (h + 1) * SB]
            local_lse[h, at, :] = lse[h * SB : (h + 1) * SB]
        return carry

    lax.fori_loop(0, ROWS // SB, local_block, 0)

    load_prefix.wait()
    arrived(q_recv.at[pl.ds(0, N_ROLL - 1)], r_q)
    came = q_recv[...].reshape(N_ROLL * TILE, HD)
    outs, marks = [], []
    per = REPEAT * N_ROLL
    for j in range(2):
        queries = jnp.dot(
            pick_in[j * per : (j + 1) * per, :], came, preferred_element_type=jnp.float32
        ).astype(jnp.bfloat16)
        scores = lax.dot_general(
            queries, pref[j, :, :HD], (((1,), (1,)), ((), ())), preferred_element_type=jnp.float32
        ) * SCALE
        scores = jnp.where(iota(scores.shape, 1) < blocks[j] * BLOCK, scores, MASKED)
        top = jnp.max(scores, axis=-1, keepdims=True)
        e = jnp.exp(scores - top)
        total = jnp.sum(e, axis=-1, keepdims=True)
        weights = (e / total).astype(jnp.bfloat16)
        res = jnp.dot(weights, pref[j, :, HD:], preferred_element_type=jnp.float32)
        outs.append(res.astype(jnp.bfloat16))
        lse = jnp.broadcast_to(top + jnp.log(total), (per, HD))
        hi = lse.astype(jnp.bfloat16).astype(jnp.float32)
        mid = (lse - hi).astype(jnp.bfloat16).astype(jnp.float32)
        low = lse - hi - mid
        lane = iota((per, HD), 1)
        first = (lax.shift_right_logical(iota((per, HD), 0), 6) + j * REPEAT) * 3
        mark = jnp.where(lane == first, hi, jnp.where(lane == first + 1, mid, jnp.where(lane == first + 2, low, 0.0)))
        marks.append(mark.astype(jnp.bfloat16))
    stacked = jnp.concatenate(outs + marks, axis=0)
    o_send[...] = jnp.dot(pick_out[...], stacked, preferred_element_type=jnp.float32).astype(
        jnp.bfloat16
    ).reshape(N_ROLL, TILE, HD)
    exchange(o_send, o_recv, s_o, r_o)

    arrived(o_recv.at[pl.ds(0, N_ROLL - 1)], r_o)
    back = jnp.dot(
        pick_home[...], o_recv[...].reshape(N_ROLL * TILE, HD), preferred_element_type=jnp.float32
    )
    terms = back[REPEAT * ROWS :]
    second = jnp.bitwise_and(group_rows, 1) * REPEAT
    lane = iota((ROWS, HD), 1)
    for h in range(REPEAT):
        first = (second + h) * 3
        mine = jnp.where((lane >= first) & (lane < first + 3), terms, 0.0)
        p_lse = jnp.broadcast_to(jnp.sum(mine, axis=-1, keepdims=True), (ROWS, HD))
        l_lse = local_lse[h]
        top = jnp.maximum(p_lse, l_lse)
        ep = jnp.exp(p_lse - top)
        el = jnp.exp(l_lse - top)
        mixed = (ep * back[h * ROWS : (h + 1) * ROWS] + el * local_out[h]) / (ep + el)
        out[:, h * HD : (h + 1) * HD] = mixed.astype(jnp.bfloat16)

    arrived(q_send.at[pl.ds(0, N_ROLL - 1)], s_q)
    arrived(o_send.at[pl.ds(0, N_ROLL - 1)], s_o)
    send.finish()


def per_device(
    hidden_in, qkv_weight, sample_group, prefix_blocks, prefix_kv, page_table, suffix_pool
):
    dma = pltpu.SemaphoreType.DMA
    vmem = pl.BlockSpec(memory_space=pltpu.VMEM)
    smem = pl.BlockSpec(memory_space=pltpu.SMEM)
    hbm = pl.BlockSpec(memory_space=pl.ANY)
    bf16, f32 = jnp.bfloat16, jnp.float32
    sems = []
    for shape in ((4,), (3,), (4,), (4,), (8,), (4,), (8, 4), (4, 8)):
        sems += [dma(shape), dma(shape)]
    tiles = pltpu.VMEM((N_ROLL, TILE, HD), bf16)
    return pl.pallas_call(
        attend_kernel,
        out_shape=jax.ShapeDtypeStruct((ROWS, REPEAT * HD), bf16),
        in_specs=[hbm, hbm, hbm, smem, hbm, hbm, hbm],
        out_specs=vmem,
        scratch_shapes=[
            pltpu.VMEM((ROWS, 10 * HD), bf16),
            pltpu.VMEM((SHARD, XC + ZC), bf16),
            pltpu.VMEM((1, ROWS), jnp.int32),
            pltpu.SMEM((SPAGES, ROWS), jnp.int32),
            pltpu.VMEM((NZ, NX, SHARD, XC), bf16),
            pltpu.VMEM((NZ, NX, SHARD, ZC), bf16),
            pltpu.VMEM((4, 2, ROWS, 640), bf16),
            pltpu.VMEM((2, ROWS, 640), bf16),
            pltpu.VMEM((8, ROWS), f32),
            pltpu.VMEM((4, 8, ROWS), f32),
            pltpu.VMEM((4, 2, ROWS, 256), f32),
            pltpu.VMEM((4, ROWS, 256), f32),
            pltpu.VMEM((ROWS, XC + ZC), bf16),
            pltpu.VMEM(prefix_kv.shape, bf16),
            pltpu.VMEM(suffix_pool.shape, bf16),
            pltpu.VMEM((N_ROLL * TILE, REPEAT * ROWS), bf16),
            pltpu.VMEM((2 * REPEAT * N_ROLL, N_ROLL * TILE), bf16),
            pltpu.VMEM((N_ROLL * TILE, 2 * REPEAT * ROWS), bf16),
            pltpu.VMEM(((REPEAT + 1) * ROWS, N_ROLL * TILE), bf16),
            tiles, tiles, tiles, tiles,
            pltpu.VMEM((REPEAT, ROWS, HD), f32),
            pltpu.VMEM((REPEAT, ROWS, HD), f32),
            pltpu.VMEM((ROWS, SPAGES, PAGE, 2 * HD), bf16),
            *sems,
            dma((6,)), dma, dma, dma, dma,
        ],
        compiler_params=pltpu.CompilerParams(
            collective_id=0, has_side_effects=True, vmem_limit_bytes=62 * 1024 * 1024
        ),
    )(hidden_in, qkv_weight, sample_group.reshape(1, ROWS), prefix_blocks, prefix_kv, page_table.T, suffix_pool)


def solution(mesh):
    in_specs = (
        P("roll", "tp"),
        P("roll", "tp"),
        P("roll"),
        P("roll"),
        P("roll", None, "tp"),
        P("roll", None),
        P("roll", None, "tp"),
    )
    out_specs = P("roll", "tp")
    return jax.shard_map(
        per_device, mesh=mesh, in_specs=in_specs, out_specs=out_specs, check_vma=False
    )
```

```python
import math

import jax
import jax.numpy as jnp
from jax import lax
from jax.experimental import pallas as pl
from jax.experimental.pallas import tpu as pltpu
from jax.sharding import PartitionSpec as P

HEADS = 20
KV_HEADS = 4
HD = 128
BLOCK = 128
PAGE = 16
SPAGES = 2
D = 5120
NX, NY, NZ = 4, 2, 8
ROWS = 128
SHARD = 80
QX, QZ, KX, VZ = 384, 256, 128, 128
N_ROLL = NX * NY * NZ
REPEAT = HEADS // KV_HEADS
TILE = 16
SB = 16
KEYS = SPAGES * PAGE
SCALE = 1.0 / math.sqrt(HD)
MASKED = -1e30
MESH = pl.DeviceIdType.MESH
ORDER = (
    (
        514, 515, 2, 3, 770, 771, 258, 259, 516, 517, 818, 819,
    ),
    (
        370, 786, 787, 371, 274, 4, 5, 275, 260, 261, 772, 773, 372, 802, 803, 373, 820, 821,
        276,
    ),
    (
        788, 789, 355, 354, 6, 7, 291, 290, 774, 775, 277, 357, 804, 805, 356, 822,
    ),
    (
        823, 790, 791, 338, 339, 1027, 1282, 1283, 8, 1795, 1538, 1539, 1026, 9, 1794, 777, 776, 306,
        307, 807, 293, 806, 292, 825, 824, 340, 341, 793, 792, 1298, 1299, 1029, 1842, 1285, 1284, 1797,
        1810, 1843, 1028, 1811, 1796, 323, 322, 809, 1540, 1541, 808, 1394, 1395, 308, 1300, 1031, 309, 1844,
        1301, 1314, 1799, 1812, 1315, 1378, 1845, 1030, 1379, 1813, 1798, 325, 324,
    ),
    (
        1827, 1826, 1396, 1397, 1033, 1330, 1331, 1801, 1846, 1316, 1317, 1814, 1380, 1847, 1032, 1363, 1362, 1381,
        1800, 1815, 1829, 1828, 1332,
    ),
    (
        1333, 1848, 1816, 1849, 1346, 1347, 1364, 1817, 1365, 1831, 1830, 1349, 1348, 1833, 1832,
    ),
)


class Place:
    def __init__(self):
        self.r = lax.axis_index("roll")
        self.t = lax.axis_index("tp")
        self.x = lax.rem(self.r, NX)
        self.y = lax.rem(lax.div(self.r, NX), NY)
        self.z = lax.div(self.r, NX * NY)
        self.t1 = self.t + 1 - 2 * lax.rem(self.t, 2)
        self.t2 = lax.rem(self.t + 2, 4)
        self.t3 = lax.rem(self.t1 + 2, 4)
        self.ty = 1 - self.y

    def roll(self, z, y, x):
        return (z * NY + y) * NX + x

    def zn(self, k):
        return lax.rem(self.z + k + NZ, NZ)

    def xn(self, k):
        return lax.rem(self.x + k + NX, NX)

    def at_z(self, k):
        return {"roll": self.roll(self.zn(k), self.y, self.x), "tp": self.t}

    def at_x(self, k):
        return {"roll": self.roll(self.z, self.y, self.xn(k)), "tp": self.t}

    def other(self, flip_y, tp):
        y = self.ty if flip_y else self.y
        return {"roll": self.roll(self.z, y, self.x), "tp": tp}


class Sends:
    def __init__(self):
        self.copies = []

    def __call__(self, src, dst, send, recv, device):
        copy = pltpu.make_async_remote_copy(
            src_ref=src, dst_ref=dst, send_sem=send, recv_sem=recv,
            device_id=device, device_id_type=MESH,
        )
        copy.start()
        self.copies.append(copy)

    def finish(self):
        for copy in self.copies:
            copy.wait_send()


def arrived(ref, sem):
    pltpu.make_async_copy(ref, ref, sem).wait()


class Gather:
    def __init__(self, me, send, wx, wz, sems):
        self.me, self.send, self.wx, self.wz = me, send, wx, wz
        self.seen = set()
        self.s_xz, self.r_xz, self.s_zx, self.r_zx, self.s_xx, self.r_xx, self.s_zz, self.r_zz = sems

    def rows(self, last, way, parity):
        if not last:
            return pl.ds(0, SHARD)
        return pl.ds(0, 48) if (way + parity) % 2 == 0 else pl.ds(48, 32)

    def xz(self, step, way, wait):
        me, sign, i = self.me, 1 - 2 * way, way * 4 + step - 1
        ref = self.wx.at[me.zn(-sign * (step if wait else step - 1)), me.x, self.rows(step == 4, way, 0)]
        if wait:
            arrived(ref, self.r_xz.at[i])
        else:
            self.send(ref, ref, self.s_xz.at[i], self.r_xz.at[i], me.at_z(sign))

    def xx(self, d, step, way, wait):
        me, sign, i = self.me, 1 - 2 * way, way * 2 + step - 1
        ref = self.wx.at[me.zn(d), me.xn(-sign * (step if wait else step - 1)), self.rows(step == 2, way, d)]
        if wait:
            arrived(ref, self.r_xx.at[d, i])
        else:
            self.send(ref, ref, self.s_xx.at[d, i], self.r_xx.at[d, i], me.at_x(sign))

    def zx(self, step, way, wait):
        me, sign, i = self.me, 1 - 2 * way, way * 2 + step - 1
        ref = self.wz.at[me.z, me.xn(-sign * (step if wait else step - 1)), self.rows(step == 2, way, 1)]
        if wait:
            arrived(ref, self.r_zx.at[i])
        else:
            self.send(ref, ref, self.s_zx.at[i], self.r_zx.at[i], me.at_x(sign))

    def zz(self, j, step, way, wait):
        me, sign, i = self.me, 1 - 2 * way, way * 4 + step - 1
        ref = self.wz.at[me.zn(-sign * (step if wait else step - 1)), me.xn(j), self.rows(step == 4, way, j)]
        if wait:
            arrived(ref, self.r_zz.at[j, i])
        else:
            self.send(ref, ref, self.s_zz.at[j, i], self.r_zz.at[j, i], me.at_z(sign))

    def start(self):
        for way in (0, 1):
            self.xz(1, way, False)
            self.zx(1, way, False)
        for way in (0, 1):
            self.xx(0, 1, way, False)
            self.zz(0, 1, way, False)

    def event(self, kind, i, step, way):
        if kind == 0:
            self.xz(step, way, True)
            if step < 4:
                self.xz(step + 1, way, False)
                for out in (0, 1):
                    self.xx(step if way else NZ - step, 1, out, False)
        elif kind == 1:
            self.xx(i, step, way, True)
            if step == 1:
                self.xx(i, 2, way, False)
        elif kind == 2:
            self.zx(step, way, True)
            if step == 1:
                self.zx(2, way, False)
                for out in (0, 1):
                    self.zz(1 if way else 3, 1, out, False)
        else:
            self.zz(i, step, way, True)
            if step < 4:
                self.zz(i, step + 1, way, False)
        self.seen.add((kind, step, way))
        for both, ready in ((0, 4), (2, 2)):
            if kind == both and step == ready and (kind, step, 1 - way) in self.seen:
                for out in (0, 1):
                    if kind == 0:
                        self.xx(4, 1, out, False)
                    else:
                        self.zz(2, 1, out, False)


def onehot(hit):
    return jnp.where(hit, 1.0, 0.0).astype(jnp.bfloat16)


def iota(shape, axis):
    return lax.broadcasted_iota(jnp.int32, shape, axis)


def attend_kernel(
    hidden_hbm, w_hbm, group_hbm, blocks, prefix, table_hbm, pool, out,
    hidden, w, group, table,
    qx, qz, kx, vz, ab, nb, ssq_s, ssq_r, cs, cb, cr,
    un, pref, pages, pick_send, pick_in, pick_out, pick_home,
    q_send, q_recv, o_send, o_recv, local_out, local_lse, gathered,
    s_ss, r_ss, s_a, r_a, s_b, r_b, s_c, r_c,
    load_sem, s_q, r_q, s_o, r_o,
    *gather_sems,
):
    me = Place()
    send = Sends()
    x, y, z, t = me.x, me.y, me.z, me.t
    barrier = pltpu.get_barrier_semaphore()
    peers = [
        me.at_z(1), me.at_z(-1), me.at_x(1), me.at_x(-1),
        me.other(True, t), me.other(False, me.t2), me.other(True, me.t2),
        me.other(False, me.t1), me.other(False, me.t3),
    ]
    for peer in peers:
        pl.semaphore_signal(barrier, inc=1, device_id=peer, device_id_type=MESH)
    load_hidden = pltpu.make_async_copy(hidden_hbm, hidden, load_sem.at[2])
    load_w = pltpu.make_async_copy(w_hbm, w, load_sem.at[3])
    load_group = pltpu.make_async_copy(group_hbm, group, load_sem.at[4])
    load_table = pltpu.make_async_copy(table_hbm, table, load_sem.at[5])
    load_hidden.start()
    load_w.start()
    load_group.start()
    load_table.start()
    load_prefix = pltpu.make_async_copy(prefix, pref, load_sem.at[0])
    load_pages = pltpu.make_async_copy(pool, pages, load_sem.at[1])
    load_prefix.start()
    load_pages.start()

    load_w.wait()
    start = 0
    for part, width in ((qx, QX), (qz, QZ), (kx, KX), (vz, VZ)):
        part[z, x] = w[:, start : start + width]
        start += width
    q_recv[...] = jnp.zeros_like(q_recv)
    o_recv[...] = jnp.zeros_like(o_recv)
    pl.semaphore_wait(barrier, len(peers))

    g1 = Gather(me, send, qx, qz, gather_sems[:8])
    g2 = Gather(me, send, kx, vz, gather_sems[8:])
    g1.start()

    def run(stretch):
        for code in ORDER[stretch]:
            group_of, kind, i, step = code // 1024, code % 1024 // 256, code % 256 // 16, code % 16 // 2
            (g1, g2)[group_of].event(kind, i, step, code % 2)
            if group_of == 0 and (kind, step, code % 2) == (0, 3, 0):
                g2.start()

    load_hidden.wait()
    total = jnp.zeros((ROWS, HD), jnp.float32)
    for b in range(10):
        part = hidden[:, b * HD : (b + 1) * HD].astype(jnp.float32)
        total += part * part
    total = jnp.sum(total, axis=-1, keepdims=True)
    flat = jnp.broadcast_to(total, (ROWS, ROWS)).T[:8]
    ssq_s[...] = flat
    for k, tp in ((1, me.t1), (2, me.t2), (3, me.t3)):
        send(ssq_s, ssq_r.at[k], s_ss.at[k], r_ss.at[k], me.other(False, tp))
    load_group.wait()
    load_table.wait()
    slot = lax.shift_right_logical(group[...], 1) * TILE + jnp.bitwise_and(group[...], 1) * REPEAT
    slot_rows = jnp.broadcast_to(slot, (ROWS, ROWS)).T
    group_rows = jnp.broadcast_to(group[...], (ROWS, ROWS)).T

    def build_send():
        for h in range(REPEAT):
            pick_send[:, h * ROWS : (h + 1) * ROWS] = onehot(iota((N_ROLL * TILE, ROWS), 0) == slot + h)

    def build_in():
        for i in range(2 * REPEAT):
            target = iota((N_ROLL, N_ROLL * TILE), 0) * TILE + i
            pick_in[i * N_ROLL : (i + 1) * N_ROLL, :] = onehot(iota((N_ROLL, N_ROLL * TILE), 1) == target)

    def build_out():
        for i in range(2 * REPEAT):
            lane = iota((N_ROLL * TILE, ROWS), 1) + (i % REPEAT) * ROWS
            row = lax.shift_right_logical(lane, 6) if i < REPEAT else 2 * REPEAT
            target = jnp.bitwise_and(lane, N_ROLL - 1) * TILE + row
            pick_out[:, i * ROWS : (i + 1) * ROWS] = onehot(iota((N_ROLL * TILE, ROWS), 0) == target)

    def build_home():
        for b in range(N_ROLL * TILE // ROWS):
            column = iota((ROWS, ROWS), 1) + b * ROWS
            for h in range(REPEAT):
                pick_home[h * ROWS : (h + 1) * ROWS, b * ROWS : (b + 1) * ROWS] = onehot(column == slot_rows + h)
            target = lax.shift_right_logical(group_rows, 1) * TILE + 2 * REPEAT
            pick_home[REPEAT * ROWS :, b * ROWS : (b + 1) * ROWS] = onehot(column == target)

    def gather_pages():
        load_pages.wait()

        def one(s, carry):
            for j in range(SPAGES):
                gathered[s, j] = pages[table[j, s]]
            return carry

        lax.fori_loop(0, ROWS, one, 0, unroll=8)

    ssum = flat
    for k in (1, 2, 3):
        arrived(ssq_r.at[k], r_ss.at[k])
        ssum += ssq_r[k]
    scale = lax.rsqrt(ssum / D + 1e-06)
    scale = jnp.broadcast_to(scale[:1], (ROWS, ROWS)).T
    tiles = [hidden[:, b * HD : (b + 1) * HD].astype(jnp.float32) * scale for b in range(10)]
    turned = {b: pltpu.roll(tiles[b], HD // 2, 1) for b in range(2, 8)}
    low_half = iota((ROWS, HD), 1) < HD // 2

    def halves(first, second):
        return jnp.where(low_half, first, second)

    sides = (
        (tiles[0], tiles[1], halves(tiles[2], turned[5]), halves(turned[5], turned[6]), halves(turned[6], turned[7])),
        (halves(turned[2], turned[3]), halves(turned[3], turned[4]), halves(turned[4], tiles[7]), tiles[8], tiles[9]),
    )
    for side in range(2):
        for b in range(5):
            nb[side, :, b * HD : (b + 1) * HD] = sides[side][b].astype(jnp.bfloat16)
    ab[t, y] = nb[y]
    send(nb.at[me.ty], ab.at[t, y], s_a.at[0], r_a.at[0], me.other(True, t))
    send(nb.at[y], ab.at[t, y], s_a.at[1], r_a.at[1], me.other(False, me.t2))
    send(nb.at[me.ty], ab.at[t, y], s_a.at[2], r_a.at[2], me.other(True, me.t2))
    sibling = me.other(False, me.t1)
    send(nb.at[y], ab.at[t, y], s_b.at[3], r_b.at[3], sibling)

    def pass_rows():
        for i, (tp, yy) in enumerate(((t, me.ty), (me.t2, y), (me.t2, me.ty))):
            arrived(ab.at[tp, yy], r_a.at[i])
            send(ab.at[tp, yy], ab.at[tp, yy], s_b.at[i], r_b.at[i], sibling)

    partner = me.other(True, t)

    def product(i, src, at, width):
        acc = jnp.zeros((2 * ROWS, width), jnp.float32)
        for tp in range(4):
            acc += jnp.dot(
                ab[tp].reshape(2 * ROWS, 640),
                src[2 * tp : 2 * tp + 2, :, :, at : at + width].reshape(640, width),
                preferred_element_type=jnp.float32,
            )
        cs[i, :, :, :width] = acc.reshape(2, ROWS, width)
        cb[i, :, :width] = cs[i, me.ty, :, :width].astype(jnp.bfloat16)
        send(
            cb.at[i, :, pl.ds(0, width)], cr.at[i, :, pl.ds(0, width)],
            s_c.at[i], r_c.at[i], partner,
        )

    def total_of(i, start, width):
        arrived(cr.at[i, :, pl.ds(0, width)], r_c.at[i])
        un[:, start : start + width] = (cs[i, y, :, :width] + cr[i, :, :width].astype(jnp.float32)).astype(jnp.bfloat16)

    run(0)
    build_send()
    run(1)
    build_in()
    pass_rows()
    run(2)
    build_out()
    run(3)
    for i, (tp, yy) in enumerate(
        ((me.t1, me.ty), (me.t3, y), (me.t3, me.ty), (me.t1, y))
    ):
        arrived(ab.at[tp, yy], r_b.at[i])
    product(2, qz, 0, 256)
    product(0, qx, 0, 256)
    product(1, qx, 256, 128)
    build_home()
    gather_pages()
    run(4)
    total_of(2, 384, 256)
    total_of(0, 0, 256)
    total_of(1, 256, 128)

    rows = jnp.concatenate([un[:, h * HD : (h + 1) * HD] for h in range(REPEAT)], axis=0)
    q_send[...] = jnp.dot(pick_send[...], rows, preferred_element_type=jnp.float32).astype(
        jnp.bfloat16
    ).reshape(N_ROLL, TILE, HD)

    def exchange(src, dst, rows, s_sem, r_sem):
        here = y * NX + x
        for dz in (4, 3, 5, 2, 6, 1, 7, 0):

            def one(i, carry):
                peer = me.zn(dz) * (NX * NY) + lax.rem(here + i, NX * NY)
                pltpu.make_async_remote_copy(
                    src_ref=src.at[peer, pl.ds(0, rows)], dst_ref=dst.at[me.r, pl.ds(0, rows)],
                    send_sem=s_sem, recv_sem=r_sem,
                    device_id={"roll": peer, "tp": t}, device_id_type=MESH,
                ).start()
                return carry

            lax.fori_loop(1 if dz == 0 else 0, NX * NY, one, 0)
        dst[me.r] = src[me.r]

    def all_of(ref, rows, sem):
        arrived(ref.at[pl.ds(0, N_ROLL - 1), pl.ds(0, rows)], sem)

    exchange(q_send, q_recv, 10, s_q, r_q)
    run(5)
    product(3, kx, 0, 128)
    product(4, vz, 0, 128)

    def local_block(b, carry):
        at = pl.ds(pl.multiple_of(b * SB, SB), SB)
        queries = jnp.concatenate([un[at, h * HD : (h + 1) * HD] for h in range(REPEAT)], axis=0)
        own_k = un[at, REPEAT * HD : (REPEAT + 1) * HD].astype(jnp.float32)
        own_v = un[at, (REPEAT + 1) * HD :].astype(jnp.float32)
        own_k = jnp.concatenate([own_k] * REPEAT, axis=0)
        own_v = jnp.concatenate([own_v] * REPEAT, axis=0)
        keys = gathered[at, :, :, :HD].reshape(SB * KEYS, HD)
        values = gathered[at, :, :, HD:].reshape(SB * KEYS, HD)
        scores = lax.dot_general(
            queries, keys, (((1,), (1,)), ((), ())), preferred_element_type=jnp.float32
        ) * SCALE
        shape = (REPEAT * SB, SB * KEYS)
        mine = jnp.bitwise_and(iota(shape, 0), SB - 1) == lax.shift_right_logical(iota(shape, 1), 5)
        scores = jnp.where(mine, scores, MASKED)
        own = jnp.sum(queries.astype(jnp.float32) * own_k, axis=-1, keepdims=True) * SCALE
        top = jnp.maximum(jnp.max(scores, axis=-1, keepdims=True), own)
        e = jnp.exp(scores - top)
        e_own = jnp.exp(own - top)
        total = jnp.sum(e, axis=-1, keepdims=True) + e_own
        weights = (e / total).astype(jnp.bfloat16)
        w_own = (e_own / total).astype(jnp.bfloat16).astype(jnp.float32)
        res = jnp.dot(weights, values, preferred_element_type=jnp.float32) + w_own * own_v
        lse = jnp.broadcast_to(top + jnp.log(total), (REPEAT * SB, HD))
        for h in range(REPEAT):
            local_out[h, at, :] = res[h * SB : (h + 1) * SB]
            local_lse[h, at, :] = lse[h * SB : (h + 1) * SB]
        return carry

    load_prefix.wait()
    all_of(q_recv, 10, r_q)
    came = q_recv[...].reshape(N_ROLL * TILE, HD)
    outs, marks = [], []
    per = REPEAT * N_ROLL
    for j in range(2):
        queries = jnp.dot(
            pick_in[j * per : (j + 1) * per, :], came, preferred_element_type=jnp.float32
        ).astype(jnp.bfloat16)
        scores = lax.dot_general(
            queries, pref[j, :, :HD], (((1,), (1,)), ((), ())), preferred_element_type=jnp.float32
        ) * SCALE
        scores = jnp.where(iota(scores.shape, 1) < blocks[j] * BLOCK, scores, MASKED)
        top = jnp.max(scores, axis=-1, keepdims=True)
        e = jnp.exp(scores - top)
        total = jnp.sum(e, axis=-1, keepdims=True)
        weights = (e / total).astype(jnp.bfloat16)
        res = jnp.dot(weights, pref[j, :, HD:], preferred_element_type=jnp.float32)
        outs.append(res.astype(jnp.bfloat16))
        lse = jnp.broadcast_to(top + jnp.log(total), (per, HD))
        hi = lse.astype(jnp.bfloat16).astype(jnp.float32)
        mid = (lse - hi).astype(jnp.bfloat16).astype(jnp.float32)
        low = lse - hi - mid
        lane = iota((per, HD), 1)
        first = (lax.shift_right_logical(iota((per, HD), 0), 6) + j * REPEAT) * 3
        mark = jnp.where(lane == first, hi, jnp.where(lane == first + 1, mid, jnp.where(lane == first + 2, low, 0.0)))
        marks.append(mark.astype(jnp.bfloat16))
    stacked = jnp.concatenate(outs + marks, axis=0)
    o_send[...] = jnp.dot(pick_out[...], stacked, preferred_element_type=jnp.float32).astype(
        jnp.bfloat16
    ).reshape(N_ROLL, TILE, HD)
    exchange(o_send, o_recv, 12, s_o, r_o)
    total_of(3, 640, 128)
    total_of(4, 768, 128)
    lax.fori_loop(0, ROWS // SB, local_block, 0)
    all_of(o_recv, 12, r_o)
    back = jnp.dot(
        pick_home[...], o_recv[...].reshape(N_ROLL * TILE, HD), preferred_element_type=jnp.float32
    )
    terms = back[REPEAT * ROWS :]
    second = jnp.bitwise_and(group_rows, 1) * REPEAT
    lane = iota((ROWS, HD), 1)
    for h in range(REPEAT):
        first = (second + h) * 3
        mine = jnp.where((lane >= first) & (lane < first + 3), terms, 0.0)
        p_lse = jnp.broadcast_to(jnp.sum(mine, axis=-1, keepdims=True), (ROWS, HD))
        l_lse = local_lse[h]
        top = jnp.maximum(p_lse, l_lse)
        ep = jnp.exp(p_lse - top)
        el = jnp.exp(l_lse - top)
        mixed = (ep * back[h * ROWS : (h + 1) * ROWS] + el * local_out[h]) / (ep + el)
        out[:, h * HD : (h + 1) * HD] = mixed.astype(jnp.bfloat16)

    all_of(q_send, 10, s_q)
    all_of(o_send, 12, s_o)
    send.finish()


def per_device(
    hidden_in, qkv_weight, sample_group, prefix_blocks, prefix_kv, page_table, suffix_pool
):
    dma = pltpu.SemaphoreType.DMA
    vmem = pl.BlockSpec(memory_space=pltpu.VMEM)
    smem = pl.BlockSpec(memory_space=pltpu.SMEM)
    hbm = pl.BlockSpec(memory_space=pl.ANY)
    bf16, f32 = jnp.bfloat16, jnp.float32
    sems = []
    for shape in ((4,), (3,), (4,), (5,)):
        sems += [dma(shape), dma(shape)]
    gather_sems = []
    for shape in ((8,), (4,), (8, 4), (4, 8)) * 2:
        gather_sems += [dma(shape), dma(shape)]
    tiles = pltpu.VMEM((N_ROLL, TILE, HD), bf16)
    return pl.pallas_call(
        attend_kernel,
        out_shape=jax.ShapeDtypeStruct((ROWS, REPEAT * HD), bf16),
        in_specs=[hbm, hbm, hbm, smem, hbm, hbm, hbm],
        out_specs=vmem,
        scratch_shapes=[
            pltpu.VMEM((ROWS, 10 * HD), bf16),
            pltpu.VMEM((SHARD, QX + QZ + KX + VZ), bf16),
            pltpu.VMEM((1, ROWS), jnp.int32),
            pltpu.SMEM((SPAGES, ROWS), jnp.int32),
            *(pltpu.VMEM((NZ, NX, SHARD, width), bf16) for width in (QX, QZ, KX, VZ)),
            pltpu.VMEM((4, 2, ROWS, 640), bf16),
            pltpu.VMEM((2, ROWS, 640), bf16),
            pltpu.VMEM((8, ROWS), f32),
            pltpu.VMEM((4, 8, ROWS), f32),
            pltpu.VMEM((5, 2, ROWS, 256), f32),
            pltpu.VMEM((5, ROWS, 256), bf16),
            pltpu.VMEM((5, ROWS, 256), bf16),
            pltpu.VMEM((ROWS, QX + QZ + KX + VZ), bf16),
            pltpu.VMEM(prefix_kv.shape, bf16),
            pltpu.VMEM(suffix_pool.shape, bf16),
            pltpu.VMEM((N_ROLL * TILE, REPEAT * ROWS), bf16),
            pltpu.VMEM((2 * REPEAT * N_ROLL, N_ROLL * TILE), bf16),
            pltpu.VMEM((N_ROLL * TILE, 2 * REPEAT * ROWS), bf16),
            pltpu.VMEM(((REPEAT + 1) * ROWS, N_ROLL * TILE), bf16),
            tiles, tiles, tiles, tiles,
            pltpu.VMEM((REPEAT, ROWS, HD), f32),
            pltpu.VMEM((REPEAT, ROWS, HD), f32),
            pltpu.VMEM((ROWS, SPAGES, PAGE, 2 * HD), bf16),
            *sems,
            dma((6,)), dma, dma, dma, dma,
            *gather_sems,
        ],
        compiler_params=pltpu.CompilerParams(
            collective_id=0, has_side_effects=True, vmem_limit_bytes=62 * 1024 * 1024
        ),
    )(hidden_in, qkv_weight, sample_group.reshape(1, ROWS), prefix_blocks, prefix_kv, page_table.T, suffix_pool)


def solution(mesh):
    in_specs = (
        P("roll", "tp"),
        P("roll", "tp"),
        P("roll"),
        P("roll"),
        P("roll", None, "tp"),
        P("roll", None),
        P("roll", None, "tp"),
    )
    out_specs = P("roll", "tp")
    return jax.shard_map(
        per_device, mesh=mesh, in_specs=in_specs, out_specs=out_specs, check_vma=False
    )
```

```python
import math

import jax
import jax.numpy as jnp
from jax import lax
from jax.experimental import pallas as pl
from jax.experimental.pallas import tpu as pltpu
from jax.sharding import PartitionSpec as P

HEADS = 20
KV_HEADS = 4
HD = 128
BLOCK = 128
PAGE = 16
SPAGES = 2
D = 5120
NX, NY, NZ = 4, 2, 8
ROWS = 128
SHARD = 80
QX, QZ, KX, VZ = 384, 256, 128, 128
N_ROLL = NX * NY * NZ
REPEAT = HEADS // KV_HEADS
TILE = 16
SB = 16
KEYS = SPAGES * PAGE
SCALE = 1.0 / math.sqrt(HD)
MASKED = -1e30
MESH = pl.DeviceIdType.MESH
ORDER = (
    (
        16, 17, 528, 529, 272, 273, 784, 785,
    ),
    (
        1040, 1041, 1552, 1553, 1296, 1297, 1808, 1809, 2576, 2577, 522, 515, 880, 881, 2064, 2065, 496, 497,
        18, 19, 304, 305, 816, 817, 2320, 2321, 2832, 2833, 3088, 3089, 3600, 3601, 258, 267, 3344, 3345,
        3856, 3857,
    ),
    (
        1539, 1546, 1521, 786, 787, 1520, 2570, 2563, 848, 849, 1329, 2066, 2067, 464, 465, 20, 21, 336,
        337, 2928, 2929, 2864, 2865, 882, 883, 2544, 2545, 2352, 2353, 818, 819, 490,
    ),
    (
        2315, 483, 2306, 2896, 2897, 3594, 3587, 298, 850, 851, 1328, 291, 2834, 2835, 789, 788, 2068, 2069,
        432, 6, 15, 433, 368, 369, 2512, 2513, 2384, 2385, 450, 2538, 2930, 2931, 2866, 2867, 885, 884,
        821, 820, 459,
    ),
    (
        2346, 2531, 3568, 3569, 3376, 3377, 2898, 2899, 853, 852, 2339, 2054, 2063, 400, 401, 1043, 322, 331,
        1042, 1905, 1904, 2836, 2837, 783, 774, 1841, 1282, 1840, 2480, 2481, 2416, 2417, 419, 426, 362, 355,
        1514, 1507, 1322, 2498, 2507, 2932, 2933, 2868, 2869, 878, 871, 814, 807, 1873, 1872, 2900, 2901, 847,
        838, 1811, 2831, 1810, 2448, 2449, 386, 395, 2822, 1315, 1291, 2379, 3090, 3091, 1045, 1489, 1488, 1044,
        1361, 1360, 2370, 2474, 2467, 2926, 2919, 2410, 2862, 3330, 2855, 2403, 3562, 3952, 3953, 3888, 3889, 1906,
        1907, 1842, 1843, 3370, 3555, 2895, 2886, 2443, 2434,
    ),
    (
        3920, 3921, 1874, 1875, 3092, 3093, 1030, 1039, 1456, 1457, 1392, 1393, 3536, 3537, 3408, 3409, 3858, 3859,
        1474, 1483, 1355, 1346, 1812, 1813, 3363, 3339, 3954, 3955, 3890, 3891, 1908, 1909, 1844, 1845, 3922, 3923,
        1876, 1877, 3078, 3087, 1424, 1425,
    ),
    (
        3504, 3505, 3440, 3441, 3860, 3861, 1450, 1443, 1386, 1379, 1798, 1807, 3531, 3522, 3403, 3394, 3956, 3957,
        3892, 3893, 1902, 1895, 1838, 1831, 3472, 3473, 1410, 1419, 3924, 3925, 1862, 1871, 3498, 3855, 3491, 3846,
        3434, 3427, 3950, 3943, 3886, 3467, 3879, 3458, 3919, 3910,
    ),
)
PIECES = ((0, 48), (48, 32), (0, 80))


class Place:
    def __init__(self):
        self.r = lax.axis_index("roll")
        self.t = lax.axis_index("tp")
        self.x = lax.rem(self.r, NX)
        self.y = lax.rem(lax.div(self.r, NX), NY)
        self.z = lax.div(self.r, NX * NY)
        self.t1 = self.t + 1 - 2 * lax.rem(self.t, 2)
        self.t2 = lax.rem(self.t + 2, 4)
        self.t3 = lax.rem(self.t1 + 2, 4)
        self.ty = 1 - self.y

    def roll(self, z, y, x):
        return (z * NY + y) * NX + x

    def zn(self, k):
        return lax.rem(self.z + k + NZ, NZ)

    def xn(self, k):
        return lax.rem(self.x + k + NX, NX)

    def at_z(self, k):
        return {"roll": self.roll(self.zn(k), self.y, self.x), "tp": self.t}

    def at_x(self, k):
        return {"roll": self.roll(self.z, self.y, self.xn(k)), "tp": self.t}

    def other(self, flip_y, tp):
        y = self.ty if flip_y else self.y
        return {"roll": self.roll(self.z, y, self.x), "tp": tp}


def send(src, dst, s_sem, r_sem, device):
    pltpu.make_async_remote_copy(
        src_ref=src, dst_ref=dst, send_sem=s_sem, recv_sem=r_sem, device_id=device, device_id_type=MESH
    ).start()


def arrived(ref, sem):
    pltpu.make_async_copy(ref, ref, sem).wait()


class Gather:
    def __init__(self, me, wx, wz, s_sem, r_sem):
        self.me, self.wx, self.wz, self.s_sem, self.r_sem = me, wx, wz, s_sem, r_sem
        self.sems, self.waited = {}, set()

    def step(self, code):
        me, wait, key = self.me, code >= 2048, code % 1024
        kind, i, rows, hop, way = key >> 8, key >> 5 & 7, PIECES[key >> 3 & 3], (key >> 1 & 3) + 1, key & 1
        sign = 1 - 2 * way
        back = -sign * (hop if wait else hop - 1)
        ref, z, x = (
            (self.wx, me.zn(back), me.x),
            (self.wx, me.zn(i), me.xn(back)),
            (self.wz, me.z, me.xn(back)),
            (self.wz, me.zn(back), me.xn(i)),
        )[kind]
        ref = ref.at[z * NX + x, pl.ds(*rows)]
        shape = (kind, hop, (min(i, NZ - i), min(i, NX - i))[kind // 2])
        final = (1, 2, 0) if (kind, hop) == (1, 2) else (3, 4, 0) if (kind, hop) == (3, 4) else None
        sem = self.sems.setdefault(final or shape, len(self.sems))
        if not wait:
            to = me.at_z(sign) if kind in (0, 3) else me.at_x(sign)
            send(ref, ref, self.s_sem.at[kind // 2], self.r_sem.at[sem], to)
        elif not final and shape not in self.waited:
            self.waited.add(shape)
            count = 1 if (kind, hop) in ((0, 4), (2, 2)) else 4 if shape[2] and 2 * shape[2] != (NZ, NX)[kind // 2] else 2
            arrived((self.wx, self.wz)[kind // 2].at[pl.ds(0, count)], self.r_sem.at[sem])

    def finish(self):
        arrived(self.wx.at[pl.ds(0, NZ)], self.r_sem.at[self.sems[1, 2, 0]])
        arrived(self.wz.at[pl.ds(0, NX)], self.r_sem.at[self.sems[3, 4, 0]])

    def sent(self):
        arrived(self.wx.at[pl.ds(0, NZ * NX - 1)], self.s_sem.at[0])
        arrived(self.wz.at[pl.ds(0, NZ * NX - 1)], self.s_sem.at[1])


def onehot(hit):
    return jnp.where(hit, 1.0, 0.0).astype(jnp.bfloat16)


def iota(shape, axis):
    return lax.broadcasted_iota(jnp.int32, shape, axis)


def attend_kernel(
    hidden_hbm, w_hbm, group_hbm, blocks, prefix, table_hbm, pool, out,
    hidden, w, group, table,
    qx, qz, kx, vz, ab, nb, ssq_s, ssq_r, cs, cb, cr,
    un, pref, pages, pick_send, pick_in, pick_out, pick_home,
    q_send, q_recv, o_send, o_recv, local_out, local_lse, gathered,
    s_ss, r_ss, s_a, r_a, s_b, r_b, s_c, r_c,
    load_sem, s_q, r_q, s_o, r_o,
    *gather_sems,
):
    me = Place()
    x, y, z, t = me.x, me.y, me.z, me.t
    barrier = pltpu.get_barrier_semaphore()
    peers = [
        me.at_z(1), me.at_z(-1), me.at_x(1), me.at_x(-1),
        me.other(True, t), me.other(False, me.t2), me.other(True, me.t2),
        me.other(False, me.t1), me.other(False, me.t3),
    ]
    for peer in peers:
        pl.semaphore_signal(barrier, inc=1, device_id=peer, device_id_type=MESH)
    load_hidden = pltpu.make_async_copy(hidden_hbm, hidden, load_sem.at[2])
    load_w = pltpu.make_async_copy(w_hbm, w, load_sem.at[3])
    load_group = pltpu.make_async_copy(group_hbm, group, load_sem.at[4])
    load_table = pltpu.make_async_copy(table_hbm, table, load_sem.at[5])
    load_hidden.start()
    load_w.start()
    load_group.start()
    load_table.start()
    load_prefix = pltpu.make_async_copy(prefix, pref, load_sem.at[0])
    load_pages = pltpu.make_async_copy(pool, pages, load_sem.at[1])
    load_prefix.start()
    load_pages.start()

    load_w.wait()
    start = 0
    for part, width in ((qx, QX), (qz, QZ), (kx, KX), (vz, VZ)):
        part[z * NX + x] = w[:, start : start + width]
        start += width
    def build_in():
        for i in range(2 * REPEAT):
            target = iota((N_ROLL, N_ROLL * TILE), 0) * TILE + i
            pick_in[i * N_ROLL : (i + 1) * N_ROLL, :] = onehot(iota((N_ROLL, N_ROLL * TILE), 1) == target)

    def build_out():
        for i in range(2 * REPEAT):
            lane = iota((N_ROLL * TILE, ROWS), 1) + (i % REPEAT) * ROWS
            row = lax.shift_right_logical(lane, 6) if i < REPEAT else 2 * REPEAT
            target = jnp.bitwise_and(lane, N_ROLL - 1) * TILE + row
            pick_out[:, i * ROWS : (i + 1) * ROWS] = onehot(iota((N_ROLL * TILE, ROWS), 0) == target)

    build_in()
    build_out()
    q_recv[...] = jnp.zeros_like(q_recv)
    o_recv[...] = jnp.zeros_like(o_recv)
    pl.semaphore_wait(barrier, len(peers))

    g1 = Gather(me, qx, qz, *gather_sems[:2])
    g2 = Gather(me, kx, vz, *gather_sems[2:])

    def run(stretch):
        for code in ORDER[stretch]:
            (g1, g2)[code >> 10 & 1].step(code)

    run(0)
    load_hidden.wait()
    total = jnp.zeros((ROWS, HD), jnp.float32)
    for b in range(10):
        part = hidden[:, b * HD : (b + 1) * HD].astype(jnp.float32)
        total += part * part
    total = jnp.sum(total, axis=-1, keepdims=True)
    flat = jnp.broadcast_to(total, (ROWS, ROWS)).T[:8]
    ssq_s[...] = flat
    for k, tp in ((1, me.t1), (2, me.t2), (3, me.t3)):
        send(ssq_s, ssq_r.at[k], s_ss, r_ss, me.other(False, tp))
    load_group.wait()
    load_table.wait()
    slot = lax.shift_right_logical(group[...], 1) * TILE + jnp.bitwise_and(group[...], 1) * REPEAT
    slot_rows = jnp.broadcast_to(slot, (ROWS, ROWS)).T
    group_rows = jnp.broadcast_to(group[...], (ROWS, ROWS)).T

    def build_send():
        for h in range(REPEAT):
            pick_send[:, h * ROWS : (h + 1) * ROWS] = onehot(iota((N_ROLL * TILE, ROWS), 0) == slot + h)

    def build_home():
        for b in range(N_ROLL * TILE // ROWS):
            column = iota((ROWS, ROWS), 1) + b * ROWS
            for h in range(REPEAT):
                pick_home[h * ROWS : (h + 1) * ROWS, b * ROWS : (b + 1) * ROWS] = onehot(column == slot_rows + h)
            target = lax.shift_right_logical(group_rows, 1) * TILE + 2 * REPEAT
            pick_home[REPEAT * ROWS :, b * ROWS : (b + 1) * ROWS] = onehot(column == target)

    def gather_pages():
        load_pages.wait()

        def one(s, carry):
            for j in range(SPAGES):
                gathered[s, j] = pages[table[j, s]]
            return carry

        lax.fori_loop(0, ROWS, one, 0, unroll=8)

    ssum = flat
    arrived(ssq_r.at[pl.ds(1, 3)], r_ss)
    for k in (1, 2, 3):
        ssum += ssq_r[k]
    scale = lax.rsqrt(ssum / D + 1e-06)
    scale = jnp.broadcast_to(scale[:1], (ROWS, ROWS)).T
    tiles = [hidden[:, b * HD : (b + 1) * HD].astype(jnp.float32) * scale for b in range(10)]
    turned = {b: pltpu.roll(tiles[b], HD // 2, 1) for b in range(2, 8)}
    low_half = iota((ROWS, HD), 1) < HD // 2

    def halves(first, second):
        return jnp.where(low_half, first, second)

    sides = (
        (tiles[0], tiles[1], halves(tiles[2], turned[5]), halves(turned[5], turned[6]), halves(turned[6], turned[7])),
        (halves(turned[2], turned[3]), halves(turned[3], turned[4]), halves(turned[4], tiles[7]), tiles[8], tiles[9]),
    )
    for side in range(2):
        for b in range(5):
            nb[side, :, b * HD : (b + 1) * HD] = sides[side][b].astype(jnp.bfloat16)
    ab[2 * t + y] = nb[y]
    send(nb.at[me.ty], ab.at[2 * t + y], s_a, r_a, me.other(True, t))
    send(nb.at[y], ab.at[2 * t + y], s_a, r_a, me.other(False, me.t2))
    send(nb.at[me.ty], ab.at[2 * t + y], s_a, r_a, me.other(True, me.t2))
    sibling = me.other(False, me.t1)
    send(nb.at[y], ab.at[2 * t + y], s_b, r_b, sibling)

    def pass_rows():
        arrived(ab.at[pl.ds(0, 3)], r_a)
        for row in (2 * t + me.ty, 2 * me.t2 + y, 2 * me.t2 + me.ty):
            send(ab.at[row], ab.at[row], s_b, r_b, sibling)

    partner = me.other(True, t)

    def product(block, src, at, width, r_sem):
        acc = jnp.zeros((2 * ROWS, width), jnp.float32)
        for tp in range(4):
            acc += jnp.dot(
                ab[2 * tp : 2 * tp + 2].reshape(2 * ROWS, 640),
                src[8 * tp : 8 * tp + 8, :, at : at + width].reshape(640, width),
                preferred_element_type=jnp.float32,
            )
        blocks_of = pl.ds(block, width // HD)
        for b in range(width // HD):
            cs[block + b] = acc[:, b * HD : (b + 1) * HD].reshape(2, ROWS, HD)
            cb[block + b] = cs[block + b, me.ty].astype(jnp.bfloat16)
        send(cb.at[blocks_of], cr.at[blocks_of], s_c, r_sem, partner)

    def total_of(block, count, r_sem):
        arrived(cr.at[pl.ds(block, count)], r_sem)
        for b in range(block, block + count):
            un[:, b * HD : (b + 1) * HD] = (cs[b, y] + cr[b].astype(jnp.float32)).astype(jnp.bfloat16)

    run(1)
    run(2)
    run(3)
    build_send()
    pass_rows()
    run(4)
    g1.finish()
    arrived(ab.at[pl.ds(0, 4)], r_b)
    product(3, qz, 0, 256, r_c.at[0])
    product(0, qx, 0, 256, r_c.at[0])
    product(2, qx, 256, 128, r_c.at[0])
    build_home()
    gather_pages()
    run(5)
    total_of(0, 5, r_c.at[0])

    rows = jnp.concatenate([un[:, h * HD : (h + 1) * HD] for h in range(REPEAT)], axis=0)
    q_send[...] = jnp.dot(pick_send[...], rows, preferred_element_type=jnp.float32).astype(
        jnp.bfloat16
    ).reshape(N_ROLL, TILE, HD)

    def exchange(src, dst, rows, s_sem, r_sem):
        here = y * NX + x
        for dz in (4, 3, 5, 2, 6, 1, 7, 0):

            def one(i, carry):
                peer = me.zn(dz) * (NX * NY) + lax.rem(here + i, NX * NY)
                pltpu.make_async_remote_copy(
                    src_ref=src.at[peer, pl.ds(0, rows)], dst_ref=dst.at[me.r, pl.ds(0, rows)],
                    send_sem=s_sem, recv_sem=r_sem,
                    device_id={"roll": peer, "tp": t}, device_id_type=MESH,
                ).start()
                return carry

            lax.fori_loop(1 if dz == 0 else 0, NX * NY, one, 0)
        dst[me.r] = src[me.r]

    def all_of(ref, rows, sem):
        arrived(ref.at[pl.ds(0, N_ROLL - 1), pl.ds(0, rows)], sem)

    exchange(q_send, q_recv, 10, s_q, r_q)
    run(6)
    g2.finish()
    product(5, kx, 0, 128, r_c.at[1])
    product(6, vz, 0, 128, r_c.at[1])

    def local_block(b, carry):
        at = pl.ds(pl.multiple_of(b * SB, SB), SB)
        queries = jnp.concatenate([un[at, h * HD : (h + 1) * HD] for h in range(REPEAT)], axis=0)
        own_k = un[at, REPEAT * HD : (REPEAT + 1) * HD].astype(jnp.float32)
        own_v = un[at, (REPEAT + 1) * HD :].astype(jnp.float32)
        own_k = jnp.concatenate([own_k] * REPEAT, axis=0)
        own_v = jnp.concatenate([own_v] * REPEAT, axis=0)
        keys = gathered[at, :, :, :HD].reshape(SB * KEYS, HD)
        values = gathered[at, :, :, HD:].reshape(SB * KEYS, HD)
        scores = lax.dot_general(
            queries, keys, (((1,), (1,)), ((), ())), preferred_element_type=jnp.float32
        ) * SCALE
        shape = (REPEAT * SB, SB * KEYS)
        mine = jnp.bitwise_and(iota(shape, 0), SB - 1) == lax.shift_right_logical(iota(shape, 1), 5)
        scores = jnp.where(mine, scores, MASKED)
        own = jnp.sum(queries.astype(jnp.float32) * own_k, axis=-1, keepdims=True) * SCALE
        top = jnp.maximum(jnp.max(scores, axis=-1, keepdims=True), own)
        e = jnp.exp(scores - top)
        e_own = jnp.exp(own - top)
        total = jnp.sum(e, axis=-1, keepdims=True) + e_own
        weights = (e / total).astype(jnp.bfloat16)
        w_own = (e_own / total).astype(jnp.bfloat16).astype(jnp.float32)
        res = jnp.dot(weights, values, preferred_element_type=jnp.float32) + w_own * own_v
        lse = jnp.broadcast_to(top + jnp.log(total), (REPEAT * SB, HD))
        for h in range(REPEAT):
            local_out[h, at, :] = res[h * SB : (h + 1) * SB]
            local_lse[h, at, :] = lse[h * SB : (h + 1) * SB]
        return carry

    load_prefix.wait()
    all_of(q_recv, 10, r_q)
    came = q_recv[...].reshape(N_ROLL * TILE, HD)
    outs, marks = [], []
    per = REPEAT * N_ROLL
    for j in range(2):
        queries = jnp.dot(
            pick_in[j * per : (j + 1) * per, :], came, preferred_element_type=jnp.float32
        ).astype(jnp.bfloat16)
        scores = lax.dot_general(
            queries, pref[j, :, :HD], (((1,), (1,)), ((), ())), preferred_element_type=jnp.float32
        ) * SCALE
        scores = jnp.where(iota(scores.shape, 1) < blocks[j] * BLOCK, scores, MASKED)
        top = jnp.max(scores, axis=-1, keepdims=True)
        e = jnp.exp(scores - top)
        total = jnp.sum(e, axis=-1, keepdims=True)
        weights = (e / total).astype(jnp.bfloat16)
        res = jnp.dot(weights, pref[j, :, HD:], preferred_element_type=jnp.float32)
        outs.append(res.astype(jnp.bfloat16))
        lse = jnp.broadcast_to(top + jnp.log(total), (per, HD))
        hi = lse.astype(jnp.bfloat16).astype(jnp.float32)
        mid = (lse - hi).astype(jnp.bfloat16).astype(jnp.float32)
        low = lse - hi - mid
        lane = iota((per, HD), 1)
        first = (lax.shift_right_logical(iota((per, HD), 0), 6) + j * REPEAT) * 3
        mark = jnp.where(lane == first, hi, jnp.where(lane == first + 1, mid, jnp.where(lane == first + 2, low, 0.0)))
        marks.append(mark.astype(jnp.bfloat16))
    stacked = jnp.concatenate(outs + marks, axis=0)
    o_send[...] = jnp.dot(pick_out[...], stacked, preferred_element_type=jnp.float32).astype(
        jnp.bfloat16
    ).reshape(N_ROLL, TILE, HD)
    exchange(o_send, o_recv, 12, s_o, r_o)
    total_of(5, 2, r_c.at[1])
    lax.fori_loop(0, ROWS // SB, local_block, 0)
    all_of(o_recv, 12, r_o)
    back = jnp.dot(
        pick_home[...], o_recv[...].reshape(N_ROLL * TILE, HD), preferred_element_type=jnp.float32
    )
    terms = back[REPEAT * ROWS :]
    second = jnp.bitwise_and(group_rows, 1) * REPEAT
    lane = iota((ROWS, HD), 1)
    for h in range(REPEAT):
        first = (second + h) * 3
        mine = jnp.where((lane >= first) & (lane < first + 3), terms, 0.0)
        p_lse = jnp.broadcast_to(jnp.sum(mine, axis=-1, keepdims=True), (ROWS, HD))
        l_lse = local_lse[h]
        top = jnp.maximum(p_lse, l_lse)
        ep = jnp.exp(p_lse - top)
        el = jnp.exp(l_lse - top)
        mixed = (ep * back[h * ROWS : (h + 1) * ROWS] + el * local_out[h]) / (ep + el)
        out[:, h * HD : (h + 1) * HD] = mixed.astype(jnp.bfloat16)

    all_of(q_send, 10, s_q)
    all_of(o_send, 12, s_o)
    g1.sent()
    g2.sent()
    arrived(ssq_r.at[pl.ds(1, 3)], s_ss)
    arrived(ab.at[pl.ds(0, 3)], s_a)
    arrived(ab.at[pl.ds(0, 4)], s_b)
    arrived(cb.at[pl.ds(0, 7)], s_c)


def per_device(
    hidden_in, qkv_weight, sample_group, prefix_blocks, prefix_kv, page_table, suffix_pool
):
    dma = pltpu.SemaphoreType.DMA
    vmem = pl.BlockSpec(memory_space=pltpu.VMEM)
    smem = pl.BlockSpec(memory_space=pltpu.SMEM)
    hbm = pl.BlockSpec(memory_space=pl.ANY)
    bf16, f32 = jnp.bfloat16, jnp.float32
    sems = [dma] * 7 + [dma((2,))]
    gather_sems = []
    for _ in range(2):
        gather_sems += [dma((2,)), dma((22,))]
    tiles = pltpu.VMEM((N_ROLL, TILE, HD), bf16)
    return pl.pallas_call(
        attend_kernel,
        out_shape=jax.ShapeDtypeStruct((ROWS, REPEAT * HD), bf16),
        in_specs=[hbm, hbm, hbm, smem, hbm, hbm, hbm],
        out_specs=vmem,
        scratch_shapes=[
            pltpu.VMEM((ROWS, 10 * HD), bf16),
            pltpu.VMEM((SHARD, QX + QZ + KX + VZ), bf16),
            pltpu.VMEM((1, ROWS), jnp.int32),
            pltpu.SMEM((SPAGES, ROWS), jnp.int32),
            *(pltpu.VMEM((NZ * NX, SHARD, width), bf16) for width in (QX, QZ, KX, VZ)),
            pltpu.VMEM((8, ROWS, 640), bf16),
            pltpu.VMEM((2, ROWS, 640), bf16),
            pltpu.VMEM((8, ROWS), f32),
            pltpu.VMEM((4, 8, ROWS), f32),
            pltpu.VMEM((7, 2, ROWS, HD), f32),
            pltpu.VMEM((7, ROWS, HD), bf16),
            pltpu.VMEM((7, ROWS, HD), bf16),
            pltpu.VMEM((ROWS, QX + QZ + KX + VZ), bf16),
            pltpu.VMEM(prefix_kv.shape, bf16),
            pltpu.VMEM(suffix_pool.shape, bf16),
            pltpu.VMEM((N_ROLL * TILE, REPEAT * ROWS), bf16),
            pltpu.VMEM((2 * REPEAT * N_ROLL, N_ROLL * TILE), bf16),
            pltpu.VMEM((N_ROLL * TILE, 2 * REPEAT * ROWS), bf16),
            pltpu.VMEM(((REPEAT + 1) * ROWS, N_ROLL * TILE), bf16),
            tiles, tiles, tiles, tiles,
            pltpu.VMEM((REPEAT, ROWS, HD), f32),
            pltpu.VMEM((REPEAT, ROWS, HD), f32),
            pltpu.VMEM((ROWS, SPAGES, PAGE, 2 * HD), bf16),
            *sems,
            dma((6,)), dma, dma, dma, dma,
            *gather_sems,
        ],
        compiler_params=pltpu.CompilerParams(
            collective_id=0, has_side_effects=True, vmem_limit_bytes=62 * 1024 * 1024
        ),
    )(hidden_in, qkv_weight, sample_group.reshape(1, ROWS), prefix_blocks, prefix_kv, page_table.T, suffix_pool)


def solution(mesh):
    in_specs = (
        P("roll", "tp"),
        P("roll", "tp"),
        P("roll"),
        P("roll"),
        P("roll", None, "tp"),
        P("roll", None),
        P("roll", None, "tp"),
    )
    out_specs = P("roll", "tp")
    return jax.shard_map(
        per_device, mesh=mesh, in_specs=in_specs, out_specs=out_specs, check_vma=False
    )
```

```python
import math

import jax
import jax.numpy as jnp
from jax import lax
from jax.experimental import pallas as pl
from jax.experimental.pallas import tpu as pltpu
from jax.sharding import PartitionSpec as P

HEADS = 20
KV_HEADS = 4
HD = 128
BLOCK = 128
PAGE = 16
SPAGES = 2
D = 5120
NX, NY, NZ = 4, 2, 8
ROWS = 128
SHARD = 80
QX, QZ, KX, VZ = 384, 256, 128, 128
N_ROLL = NX * NY * NZ
REPEAT = HEADS // KV_HEADS
TILE = 16
SB = 16
KEYS = SPAGES * PAGE
SCALE = 1.0 / math.sqrt(HD)
MASKED = -1e30
MESH = pl.DeviceIdType.MESH
ORDER = (
    (
        16, 17, 528, 529, 272, 273, 784, 785,
    ),
    (
        1040, 1041, 1552, 1553, 1296, 1297, 1808, 1809, 2576, 2577, 522, 515, 880, 881, 2064, 2065, 496, 497,
        18, 19, 304, 305, 816, 817, 2320, 2321, 2832, 2833, 3088, 3089, 3600, 3601, 258, 786, 787,
    ),
    (
        267, 3344, 3345, 3856, 3857, 1539, 1546, 1521, 1520, 1329, 1328, 2570, 2563, 848, 849, 1291, 1042, 1043,
        2066, 2067, 464, 465, 20, 21, 336, 337,
    ),
    (
        2928, 2929, 2864, 2865, 882, 883, 2544, 2545, 2352, 2353, 818, 819, 490, 483, 2315, 2306, 2834, 2835,
        3594, 3587, 298, 291, 2896, 2897, 850, 851, 3568, 3569, 3376, 3377, 3339, 788, 789, 3090, 3091, 1488,
        1360, 1489, 1905, 2068, 2069, 432, 433, 6, 15, 368, 1904, 369, 2512, 2513, 2384, 2385, 450, 2538,
        459, 2930, 2931, 2866, 2867, 885, 884, 821, 820, 2531, 2346, 331, 322,
    ),
    (
        2898, 2899, 853, 852, 2339, 1361, 1841, 2836, 2837, 783, 774, 1840, 1873, 1872, 2054, 2063, 400, 401,
        1045, 1044, 1811, 1282, 2480, 2481, 2416, 2417, 426, 419, 362, 355, 1514, 1810, 1507, 2507, 1315, 2498,
        1322, 2932, 2933, 2868, 2869, 878, 871, 814, 807, 2379, 2370, 3536, 3537, 3408, 3409, 1474, 1346, 1483,
        1355, 2900, 2901, 847, 838, 2831, 2822, 3952, 3953, 3888, 3889, 1906, 1907, 1842, 1843, 2448, 2449, 386,
        395, 3920, 3921, 1874, 1875, 2474, 3092, 3093, 1457, 1456, 1030, 1039, 1393, 1392, 2467, 2410, 2926, 2919,
        3330, 2862, 3562, 2403, 3522, 2855, 3555, 3858, 3859, 1812, 1813, 3394, 2895, 3363, 3370, 3531, 2886, 3403,
        2443, 3954, 3955, 3890, 3891, 1908, 1909, 1844, 1845, 2434,
    ),
    (
        3922, 3923, 1876, 1877, 3078, 3087, 1424, 1425, 3504, 3505, 3440, 3441, 1450, 1443, 1386, 1379, 3860, 3861,
        1798, 1807, 3956, 3957, 3892, 3893, 1902, 1895, 1838, 1831,
    ),
    (
        3472, 3473, 1410, 1419, 3498, 3924, 3925, 1862, 1871, 3491, 3434, 3427, 3855, 3846, 3950, 3943, 3886, 3467,
        3458, 3879, 3910, 3919,
    ),
)
PIECES = ((0, 48), (48, 32), (0, 80))


class Place:
    def __init__(self):
        self.r = lax.axis_index("roll")
        self.t = lax.axis_index("tp")
        self.x = lax.rem(self.r, NX)
        self.y = lax.rem(lax.div(self.r, NX), NY)
        self.z = lax.div(self.r, NX * NY)
        self.t1 = self.t + 1 - 2 * lax.rem(self.t, 2)
        self.t2 = lax.rem(self.t + 2, 4)
        self.t3 = lax.rem(self.t1 + 2, 4)
        self.ty = 1 - self.y

    def roll(self, z, y, x):
        return (z * NY + y) * NX + x

    def zn(self, k):
        return lax.rem(self.z + k + NZ, NZ)

    def xn(self, k):
        return lax.rem(self.x + k + NX, NX)

    def at_z(self, k):
        return {"roll": self.roll(self.zn(k), self.y, self.x), "tp": self.t}

    def at_x(self, k):
        return {"roll": self.roll(self.z, self.y, self.xn(k)), "tp": self.t}

    def other(self, flip_y, tp):
        y = self.ty if flip_y else self.y
        return {"roll": self.roll(self.z, y, self.x), "tp": tp}


def send(src, dst, s_sem, r_sem, device):
    pltpu.make_async_remote_copy(
        src_ref=src, dst_ref=dst, send_sem=s_sem, recv_sem=r_sem, device_id=device, device_id_type=MESH
    ).start()


def arrived(ref, sem):
    pltpu.make_async_copy(ref, ref, sem).wait()


class Gather:
    def __init__(self, me, wx, wz, s_sem, r_sem):
        self.me, self.wx, self.wz, self.s_sem, self.r_sem = me, wx, wz, s_sem, r_sem
        self.sems, self.waited = {}, set()

    def step(self, code):
        me, wait, key = self.me, code >= 2048, code % 1024
        kind, i, rows, hop, way = key >> 8, key >> 5 & 7, PIECES[key >> 3 & 3], (key >> 1 & 3) + 1, key & 1
        sign = 1 - 2 * way
        back = -sign * (hop if wait else hop - 1)
        ref, z, x = (
            (self.wx, me.zn(back), me.x),
            (self.wx, me.zn(i), me.xn(back)),
            (self.wz, me.z, me.xn(back)),
            (self.wz, me.zn(back), me.xn(i)),
        )[kind]
        ref = ref.at[z * NX + x, pl.ds(*rows)]
        shape = (kind, hop, (min(i, NZ - i), min(i, NX - i))[kind // 2])
        final = (1, 2, 0) if (kind, hop) == (1, 2) else (3, 4, 0) if (kind, hop) == (3, 4) else None
        sem = self.sems.setdefault(final or shape, len(self.sems))
        if not wait:
            to = me.at_z(sign) if kind in (0, 3) else me.at_x(sign)
            send(ref, ref, self.s_sem.at[kind // 2], self.r_sem.at[sem], to)
        elif not final and shape not in self.waited:
            self.waited.add(shape)
            count = 1 if (kind, hop) in ((0, 4), (2, 2)) else 4 if shape[2] and 2 * shape[2] != (NZ, NX)[kind // 2] else 2
            arrived((self.wx, self.wz)[kind // 2].at[pl.ds(0, count)], self.r_sem.at[sem])

    def finish(self):
        arrived(self.wx.at[pl.ds(0, NZ)], self.r_sem.at[self.sems[1, 2, 0]])
        arrived(self.wz.at[pl.ds(0, NX)], self.r_sem.at[self.sems[3, 4, 0]])

    def sent(self):
        arrived(self.wx.at[pl.ds(0, NZ * NX - 1)], self.s_sem.at[0])
        arrived(self.wz.at[pl.ds(0, NZ * NX - 1)], self.s_sem.at[1])


def onehot(hit):
    return jnp.where(hit, 1.0, 0.0).astype(jnp.bfloat16)


def iota(shape, axis):
    return lax.broadcasted_iota(jnp.int32, shape, axis)


def attend_kernel(
    hidden_hbm, w_hbm, group_hbm, blocks, prefix, table_hbm, pool, out,
    hidden, w, group, table,
    qx, qz, kx, vz, ab, nb, ssq_s, ssq_r, cs, cb, cr,
    un, pref, pages, pick_send, pick_in, pick_out, pick_home,
    q_send, q_recv, o_send, o_recv, local_out, local_lse, gathered,
    s_ss, r_ss, s_a, r_a, s_b, r_b, s_c, r_c,
    load_sem, s_q, r_q, s_o, r_o,
    *gather_sems,
):
    me = Place()
    x, y, z, t = me.x, me.y, me.z, me.t
    barrier = pltpu.get_barrier_semaphore()
    peers = [
        me.at_z(1), me.at_z(-1), me.at_x(1), me.at_x(-1),
        me.other(True, t), me.other(False, me.t2), me.other(True, me.t2),
        me.other(False, me.t1), me.other(False, me.t3),
    ]
    for peer in peers:
        pl.semaphore_signal(barrier, inc=1, device_id=peer, device_id_type=MESH)
    load_hidden = pltpu.make_async_copy(hidden_hbm, hidden, load_sem.at[2])
    load_w = pltpu.make_async_copy(w_hbm, w, load_sem.at[3])
    load_group = pltpu.make_async_copy(group_hbm, group, load_sem.at[4])
    load_table = pltpu.make_async_copy(table_hbm, table, load_sem.at[5])
    load_hidden.start()
    load_w.start()
    load_group.start()
    load_table.start()
    load_prefix = pltpu.make_async_copy(prefix, pref, load_sem.at[0])
    load_pages = pltpu.make_async_copy(pool, pages, load_sem.at[1])
    load_prefix.start()
    load_pages.start()

    load_w.wait()
    start = 0
    for part, width in ((qx, QX), (qz, QZ), (kx, KX), (vz, VZ)):
        part[z * NX + x] = w[:, start : start + width]
        start += width
    def build_blocks():
        across = (jnp.bitwise_and(iota((256, 256), 0), 15) * TILE + lax.shift_right_logical(iota((256, 256), 0), 4))
        down = (jnp.bitwise_and(iota((256, 256), 1), 15) * TILE + lax.shift_right_logical(iota((256, 256), 1), 4))
        pick_in[...] = onehot(iota((256, 256), 1) == across)
        pick_out[...] = onehot(iota((256, 256), 0) == down)

    build_blocks()
    q_recv[...] = jnp.zeros_like(q_recv)
    o_recv[...] = jnp.zeros_like(o_recv)
    pl.semaphore_wait(barrier, len(peers))

    g1 = Gather(me, qx, qz, *gather_sems[:2])
    g2 = Gather(me, kx, vz, *gather_sems[2:])

    def run(stretch):
        for code in ORDER[stretch]:
            (g1, g2)[code >> 10 & 1].step(code)

    run(0)
    load_hidden.wait()
    total = jnp.zeros((ROWS, HD), jnp.float32)
    for b in range(10):
        part = hidden[:, b * HD : (b + 1) * HD].astype(jnp.float32)
        total += part * part
    total = jnp.sum(total, axis=-1, keepdims=True)
    flat = jnp.broadcast_to(total, (ROWS, ROWS)).T[:8]
    ssq_s[...] = flat
    for k, tp in ((1, me.t1), (2, me.t2), (3, me.t3)):
        send(ssq_s, ssq_r.at[k], s_ss, r_ss, me.other(False, tp))
    load_group.wait()
    load_table.wait()
    slot = lax.shift_right_logical(group[...], 1) * TILE + jnp.bitwise_and(group[...], 1) * REPEAT
    slot_rows = jnp.broadcast_to(slot, (ROWS, ROWS)).T
    group_rows = jnp.broadcast_to(group[...], (ROWS, ROWS)).T

    def build_send():
        for h in range(REPEAT):
            pick_send[:, h * ROWS : (h + 1) * ROWS] = onehot(iota((N_ROLL * TILE, ROWS), 0) == slot + h)

    def build_home():
        for b in range(N_ROLL * TILE // ROWS):
            column = iota((ROWS, ROWS), 1) + b * ROWS
            for h in range(REPEAT):
                pick_home[h * ROWS : (h + 1) * ROWS, b * ROWS : (b + 1) * ROWS] = onehot(column == slot_rows + h)
            target = lax.shift_right_logical(group_rows, 1) * TILE + 2 * REPEAT
            pick_home[REPEAT * ROWS :, b * ROWS : (b + 1) * ROWS] = onehot(column == target)

    def gather_pages():
        load_pages.wait()

        def one(s, carry):
            for j in range(SPAGES):
                gathered[s, j] = pages[table[j, s]]
            return carry

        lax.fori_loop(0, ROWS, one, 0, unroll=8)

    ssum = flat
    arrived(ssq_r.at[pl.ds(1, 3)], r_ss)
    for k in (1, 2, 3):
        ssum += ssq_r[k]
    scale = lax.rsqrt(ssum / D + 1e-06)
    scale = jnp.broadcast_to(scale[:1], (ROWS, ROWS)).T
    tiles = [hidden[:, b * HD : (b + 1) * HD].astype(jnp.float32) * scale for b in range(10)]
    turned = {b: pltpu.roll(tiles[b], HD // 2, 1) for b in range(2, 8)}
    low_half = iota((ROWS, HD), 1) < HD // 2

    def halves(first, second):
        return jnp.where(low_half, first, second)

    sides = (
        (tiles[0], tiles[1], halves(tiles[2], turned[5]), halves(turned[5], turned[6]), halves(turned[6], turned[7])),
        (halves(turned[2], turned[3]), halves(turned[3], turned[4]), halves(turned[4], tiles[7]), tiles[8], tiles[9]),
    )
    for side in range(2):
        for b in range(5):
            nb[side, :, b * HD : (b + 1) * HD] = sides[side][b].astype(jnp.bfloat16)
    ab[2 * t + y] = nb[y]
    send(nb.at[me.ty], ab.at[2 * t + y], s_a, r_a, me.other(True, t))
    send(nb.at[y], ab.at[2 * t + y], s_a, r_a, me.other(False, me.t2))
    send(nb.at[me.ty], ab.at[2 * t + y], s_a, r_a, me.other(True, me.t2))
    sibling = me.other(False, me.t1)
    send(nb.at[y], ab.at[2 * t + y], s_b, r_b, sibling)

    def pass_rows():
        arrived(ab.at[pl.ds(0, 3)], r_a)
        for row in (2 * t + me.ty, 2 * me.t2 + y, 2 * me.t2 + me.ty):
            send(ab.at[row], ab.at[row], s_b, r_b, sibling)

    partner = me.other(True, t)

    def product(block, src, at, width, r_sem):
        acc = jnp.zeros((2 * ROWS, width), jnp.float32)
        for tp in range(4):
            acc += jnp.dot(
                ab[2 * tp : 2 * tp + 2].reshape(2 * ROWS, 640),
                src[8 * tp : 8 * tp + 8, :, at : at + width].reshape(640, width),
                preferred_element_type=jnp.float32,
            )
        blocks_of = pl.ds(block, width // HD)
        for b in range(width // HD):
            cs[block + b] = acc[:, b * HD : (b + 1) * HD].reshape(2, ROWS, HD)
            cb[block + b] = cs[block + b, me.ty].astype(jnp.bfloat16)
        send(cb.at[blocks_of], cr.at[blocks_of], s_c, r_sem, partner)

    def total_of(block, count, r_sem):
        arrived(cr.at[pl.ds(block, count)], r_sem)
        for b in range(block, block + count):
            un[:, b * HD : (b + 1) * HD] = (cs[b, y] + cr[b].astype(jnp.float32)).astype(jnp.bfloat16)

    run(1)
    run(2)
    run(3)
    build_send()
    pass_rows()
    run(4)
    g1.finish()
    arrived(ab.at[pl.ds(0, 4)], r_b)
    product(3, qz, 0, 256, r_c.at[0])
    product(0, qx, 0, 256, r_c.at[0])
    product(2, qx, 256, 128, r_c.at[0])
    build_home()
    gather_pages()
    run(5)
    total_of(0, 5, r_c.at[0])

    rows = jnp.concatenate([un[:, h * HD : (h + 1) * HD] for h in range(REPEAT)], axis=0)
    q_send[...] = jnp.dot(pick_send[...], rows, preferred_element_type=jnp.float32).astype(
        jnp.bfloat16
    ).reshape(N_ROLL, TILE, HD)

    def exchange(src, dst, rows, s_sem, r_sem):
        here = y * NX + x
        for dz in (4, 3, 5, 2, 6, 1, 7, 0):

            def one(i, carry):
                peer = me.zn(dz) * (NX * NY) + lax.rem(here + i, NX * NY)
                pltpu.make_async_remote_copy(
                    src_ref=src.at[peer, pl.ds(0, rows)], dst_ref=dst.at[me.r, pl.ds(0, rows)],
                    send_sem=s_sem, recv_sem=r_sem,
                    device_id={"roll": peer, "tp": t}, device_id_type=MESH,
                ).start()
                return carry

            lax.fori_loop(1 if dz == 0 else 0, NX * NY, one, 0)
        dst[me.r] = src[me.r]

    def all_of(ref, rows, sem):
        arrived(ref.at[pl.ds(0, N_ROLL - 1), pl.ds(0, rows)], sem)

    exchange(q_send, q_recv, 10, s_q, r_q)
    run(6)
    g2.finish()
    product(5, kx, 0, 128, r_c.at[1])
    product(6, vz, 0, 128, r_c.at[1])

    def local_block(b, carry):
        at = pl.ds(pl.multiple_of(b * SB, SB), SB)
        queries = jnp.concatenate([un[at, h * HD : (h + 1) * HD] for h in range(REPEAT)], axis=0)
        own_k = un[at, REPEAT * HD : (REPEAT + 1) * HD].astype(jnp.float32)
        own_v = un[at, (REPEAT + 1) * HD :].astype(jnp.float32)
        own_k = jnp.concatenate([own_k] * REPEAT, axis=0)
        own_v = jnp.concatenate([own_v] * REPEAT, axis=0)
        keys = gathered[at, :, :, :HD].reshape(SB * KEYS, HD)
        values = gathered[at, :, :, HD:].reshape(SB * KEYS, HD)
        scores = lax.dot_general(
            queries, keys, (((1,), (1,)), ((), ())), preferred_element_type=jnp.float32
        ) * SCALE
        shape = (REPEAT * SB, SB * KEYS)
        mine = jnp.bitwise_and(iota(shape, 0), SB - 1) == lax.shift_right_logical(iota(shape, 1), 5)
        scores = jnp.where(mine, scores, MASKED)
        own = jnp.sum(queries.astype(jnp.float32) * own_k, axis=-1, keepdims=True) * SCALE
        top = jnp.maximum(jnp.max(scores, axis=-1, keepdims=True), own)
        e = jnp.exp(scores - top)
        e_own = jnp.exp(own - top)
        total = jnp.sum(e, axis=-1, keepdims=True) + e_own
        weights = (e / total).astype(jnp.bfloat16)
        w_own = (e_own / total).astype(jnp.bfloat16).astype(jnp.float32)
        res = jnp.dot(weights, values, preferred_element_type=jnp.float32) + w_own * own_v
        lse = jnp.broadcast_to(top + jnp.log(total), (REPEAT * SB, HD))
        for h in range(REPEAT):
            local_out[h, at, :] = res[h * SB : (h + 1) * SB]
            local_lse[h, at, :] = lse[h * SB : (h + 1) * SB]
        return carry

    load_prefix.wait()
    all_of(q_recv, 10, r_q)
    came = q_recv[...].reshape(N_ROLL * TILE, HD)
    per = REPEAT * N_ROLL
    part = REPEAT * TILE
    turned = [
        jnp.dot(
            pick_in[: 2 * part, :], came[b * 256 : (b + 1) * 256], preferred_element_type=jnp.float32
        ).astype(jnp.bfloat16)
        for b in range(4)
    ]
    outs, marks = [], [jnp.zeros((TILE, HD), jnp.float32)] * 4
    for j in range(2):
        queries = jnp.concatenate([q[j * part : (j + 1) * part] for q in turned], axis=0)
        scores = lax.dot_general(
            queries, pref[j, :, :HD], (((1,), (1,)), ((), ())), preferred_element_type=jnp.float32
        ) * SCALE
        scores = jnp.where(iota(scores.shape, 1) < blocks[j] * BLOCK, scores, MASKED)
        top = jnp.max(scores, axis=-1, keepdims=True)
        e = jnp.exp(scores - top)
        total = jnp.sum(e, axis=-1, keepdims=True)
        weights = (e / total).astype(jnp.bfloat16)
        res = jnp.dot(weights, pref[j, :, HD:], preferred_element_type=jnp.float32)
        outs.append(res.astype(jnp.bfloat16))
        lse = jnp.broadcast_to(top + jnp.log(total), (per, HD))
        hi = lse.astype(jnp.bfloat16).astype(jnp.float32)
        mid = (lse - hi).astype(jnp.bfloat16).astype(jnp.float32)
        low = lse - hi - mid
        lane = iota((TILE, HD), 1)
        for b in range(4):
            for h in range(REPEAT):
                first = (j * REPEAT + h) * 3
                at = slice(b * part + h * TILE, b * part + (h + 1) * TILE)
                marks[b] = jnp.where(
                    lane == first, hi[at], jnp.where(lane == first + 1, mid[at], jnp.where(lane == first + 2, low[at], marks[b]))
                )
    for b in range(4):
        rows = slice(b * part, (b + 1) * part)
        stacked = jnp.concatenate(
            [outs[0][rows], outs[1][rows], marks[b].astype(jnp.bfloat16), jnp.zeros((5 * TILE, HD), jnp.bfloat16)], axis=0
        )
        o_send[b * TILE : (b + 1) * TILE] = jnp.dot(
            pick_out[...], stacked, preferred_element_type=jnp.float32
        ).astype(jnp.bfloat16).reshape(TILE, TILE, HD)
    exchange(o_send, o_recv, 12, s_o, r_o)
    total_of(5, 2, r_c.at[1])
    lax.fori_loop(0, ROWS // SB, local_block, 0)
    all_of(o_recv, 12, r_o)
    back = jnp.dot(
        pick_home[...], o_recv[...].reshape(N_ROLL * TILE, HD), preferred_element_type=jnp.float32
    )
    terms = back[REPEAT * ROWS :]
    second = jnp.bitwise_and(group_rows, 1) * REPEAT
    lane = iota((ROWS, HD), 1)
    for h in range(REPEAT):
        first = (second + h) * 3
        mine = jnp.where((lane >= first) & (lane < first + 3), terms, 0.0)
        p_lse = jnp.broadcast_to(jnp.sum(mine, axis=-1, keepdims=True), (ROWS, HD))
        l_lse = local_lse[h]
        top = jnp.maximum(p_lse, l_lse)
        ep = jnp.exp(p_lse - top)
        el = jnp.exp(l_lse - top)
        mixed = (ep * back[h * ROWS : (h + 1) * ROWS] + el * local_out[h]) / (ep + el)
        out[:, h * HD : (h + 1) * HD] = mixed.astype(jnp.bfloat16)

    all_of(q_send, 10, s_q)
    all_of(o_send, 12, s_o)
    g1.sent()
    g2.sent()
    arrived(ssq_r.at[pl.ds(1, 3)], s_ss)
    arrived(ab.at[pl.ds(0, 3)], s_a)
    arrived(ab.at[pl.ds(0, 4)], s_b)
    arrived(cb.at[pl.ds(0, 7)], s_c)


def per_device(
    hidden_in, qkv_weight, sample_group, prefix_blocks, prefix_kv, page_table, suffix_pool
):
    dma = pltpu.SemaphoreType.DMA
    vmem = pl.BlockSpec(memory_space=pltpu.VMEM)
    smem = pl.BlockSpec(memory_space=pltpu.SMEM)
    hbm = pl.BlockSpec(memory_space=pl.ANY)
    bf16, f32 = jnp.bfloat16, jnp.float32
    sems = [dma] * 7 + [dma((2,))]
    gather_sems = []
    for _ in range(2):
        gather_sems += [dma((2,)), dma((22,))]
    tiles = pltpu.VMEM((N_ROLL, TILE, HD), bf16)
    return pl.pallas_call(
        attend_kernel,
        out_shape=jax.ShapeDtypeStruct((ROWS, REPEAT * HD), bf16),
        in_specs=[hbm, hbm, hbm, smem, hbm, hbm, hbm],
        out_specs=vmem,
        scratch_shapes=[
            pltpu.VMEM((ROWS, 10 * HD), bf16),
            pltpu.VMEM((SHARD, QX + QZ + KX + VZ), bf16),
            pltpu.VMEM((1, ROWS), jnp.int32),
            pltpu.SMEM((SPAGES, ROWS), jnp.int32),
            *(pltpu.VMEM((NZ * NX, SHARD, width), bf16) for width in (QX, QZ, KX, VZ)),
            pltpu.VMEM((8, ROWS, 640), bf16),
            pltpu.VMEM((2, ROWS, 640), bf16),
            pltpu.VMEM((8, ROWS), f32),
            pltpu.VMEM((4, 8, ROWS), f32),
            pltpu.VMEM((7, 2, ROWS, HD), f32),
            pltpu.VMEM((7, ROWS, HD), bf16),
            pltpu.VMEM((7, ROWS, HD), bf16),
            pltpu.VMEM((ROWS, QX + QZ + KX + VZ), bf16),
            pltpu.VMEM(prefix_kv.shape, bf16),
            pltpu.VMEM(suffix_pool.shape, bf16),
            pltpu.VMEM((N_ROLL * TILE, REPEAT * ROWS), bf16),
            pltpu.VMEM((256, 256), bf16),
            pltpu.VMEM((256, 256), bf16),
            pltpu.VMEM(((REPEAT + 1) * ROWS, N_ROLL * TILE), bf16),
            tiles, tiles, tiles, tiles,
            pltpu.VMEM((REPEAT, ROWS, HD), f32),
            pltpu.VMEM((REPEAT, ROWS, HD), f32),
            pltpu.VMEM((ROWS, SPAGES, PAGE, 2 * HD), bf16),
            *sems,
            dma((6,)), dma, dma, dma, dma,
            *gather_sems,
        ],
        compiler_params=pltpu.CompilerParams(
            collective_id=0, has_side_effects=True, vmem_limit_bytes=62 * 1024 * 1024
        ),
    )(hidden_in, qkv_weight, sample_group.reshape(1, ROWS), prefix_blocks, prefix_kv, page_table.T, suffix_pool)


def solution(mesh):
    in_specs = (
        P("roll", "tp"),
        P("roll", "tp"),
        P("roll"),
        P("roll"),
        P("roll", None, "tp"),
        P("roll", None),
        P("roll", None, "tp"),
    )
    out_specs = P("roll", "tp")
    return jax.shard_map(
        per_device, mesh=mesh, in_specs=in_specs, out_specs=out_specs, check_vma=False
    )
```

```python
import math

import jax
import jax.numpy as jnp
from jax import lax
from jax.experimental import pallas as pl
from jax.experimental.pallas import tpu as pltpu
from jax.sharding import PartitionSpec as P

HEADS = 20
KV_HEADS = 4
HD = 128
BLOCK = 128
PAGE = 16
SPAGES = 2
D = 5120
NX, NY, NZ = 4, 2, 8
ROWS = 128
SHARD = 80
QX, QZ, KX, VZ = 384, 256, 128, 128
N_ROLL = NX * NY * NZ
REPEAT = HEADS // KV_HEADS
TILE = 16
SB = 16
KEYS = SPAGES * PAGE
SCALE = 1.0 / math.sqrt(HD)
MASKED = -1e30
MESH = pl.DeviceIdType.MESH
ORDER = (
    (
        16, 17, 528, 529, 272, 273, 784, 785,
    ),
    (
        1040, 1041, 1552, 1553, 1296, 1297, 1808, 1809, 2576, 2577, 522, 515, 880, 881, 2064, 2065, 496, 497,
        18, 19, 304, 305, 816, 817, 2320, 2321, 2832, 2833, 3088, 3089, 3600, 3601, 258, 786, 787,
    ),
    (
        267, 3344, 3345, 3856, 3857, 1539, 1546, 1521, 1520, 1329, 1328, 2570, 2563, 848, 849, 1291, 1042, 1043,
        2066, 2067, 464, 465, 20, 21, 336, 337,
    ),
    (
        2928, 2929, 2864, 2865, 882, 883, 2544, 2545, 2352, 2353, 818, 819, 490, 483, 2315, 2306, 2834, 2835,
        3594, 3587, 298, 291, 2896, 2897, 850, 851, 3568, 3569, 3376, 3377, 3339, 788, 789, 3090, 3091, 1488,
        1360, 1489, 1905, 2068, 2069, 432, 433, 6, 15, 368, 1904, 369, 2512, 2513, 2384, 2385, 450, 2538,
        459, 2930, 2931, 2866, 2867, 885, 884, 821, 820, 2531, 2346, 331, 322,
    ),
    (
        2898, 2899, 853, 852, 2339, 1361, 1841, 2836, 2837, 783, 774, 1840, 1873, 1872, 2054, 2063, 400, 401,
        1045, 1044, 1811, 1282, 2480, 2481, 2416, 2417, 426, 419, 362, 355, 1514, 1810, 1507, 2507, 1315, 2498,
        1322, 2932, 2933, 2868, 2869, 878, 871, 814, 807, 2379, 2370, 3536, 3537, 3408, 3409, 1474, 1346, 1483,
        1355, 2900, 2901, 847, 838, 2831, 2822, 3952, 3953, 3888, 3889, 1906, 1907, 1842, 1843, 2448, 2449, 386,
        395, 3920, 3921, 1874, 1875, 2474, 3092, 3093, 1457, 1456, 1030, 1039, 1393, 1392, 2467, 2410, 2926, 2919,
        3330, 2862, 3562, 2403, 3522, 2855, 3555, 3858, 3859, 1812, 1813, 3394, 2895, 3363, 3370, 3531, 2886, 3403,
        2443, 3954, 3955, 3890, 3891, 1908, 1909, 1844, 1845, 2434,
    ),
    (
        3922, 3923, 1876, 1877, 3078, 3087, 1424, 1425, 3504, 3505, 3440, 3441, 1450, 1443, 1386, 1379, 3860, 3861,
        1798, 1807, 3956, 3957, 3892, 3893, 1902, 1895, 1838, 1831,
    ),
    (
        3472, 3473, 1410, 1419, 3498, 3924, 3925, 1862, 1871, 3491, 3434, 3427, 3855, 3846, 3950, 3943, 3886, 3467,
        3458, 3879, 3910, 3919,
    ),
)
PIECES = ((0, 48), (48, 32), (0, 80))


class Place:
    def __init__(self):
        self.r = lax.axis_index("roll")
        self.t = lax.axis_index("tp")
        self.x = lax.rem(self.r, NX)
        self.y = lax.rem(lax.div(self.r, NX), NY)
        self.z = lax.div(self.r, NX * NY)
        self.t1 = self.t + 1 - 2 * lax.rem(self.t, 2)
        self.t2 = lax.rem(self.t + 2, 4)
        self.t3 = lax.rem(self.t1 + 2, 4)
        self.ty = 1 - self.y

    def roll(self, z, y, x):
        return (z * NY + y) * NX + x

    def zn(self, k):
        return lax.rem(self.z + k + NZ, NZ)

    def xn(self, k):
        return lax.rem(self.x + k + NX, NX)

    def at_z(self, k):
        return {"roll": self.roll(self.zn(k), self.y, self.x), "tp": self.t}

    def at_x(self, k):
        return {"roll": self.roll(self.z, self.y, self.xn(k)), "tp": self.t}

    def other(self, flip_y, tp):
        y = self.ty if flip_y else self.y
        return {"roll": self.roll(self.z, y, self.x), "tp": tp}


def send(src, dst, s_sem, r_sem, device):
    pltpu.make_async_remote_copy(
        src_ref=src, dst_ref=dst, send_sem=s_sem, recv_sem=r_sem, device_id=device, device_id_type=MESH
    ).start()


def arrived(ref, sem):
    pltpu.make_async_copy(ref, ref, sem).wait()


class Gather:
    def __init__(self, me, wx, wz, s_sem, r_sem):
        self.me, self.wx, self.wz, self.s_sem, self.r_sem = me, wx, wz, s_sem, r_sem
        self.sems, self.waited = {}, set()

    def step(self, code):
        me, wait, key = self.me, code >= 2048, code % 1024
        kind, i, rows, hop, way = key >> 8, key >> 5 & 7, PIECES[key >> 3 & 3], (key >> 1 & 3) + 1, key & 1
        sign = 1 - 2 * way
        back = -sign * (hop if wait else hop - 1)
        ref, z, x = (
            (self.wx, me.zn(back), me.x),
            (self.wx, me.zn(i), me.xn(back)),
            (self.wz, me.z, me.xn(back)),
            (self.wz, me.zn(back), me.xn(i)),
        )[kind]
        ref = ref.at[z * NX + x, pl.ds(*rows)]
        shape = (kind, hop, (min(i, NZ - i), min(i, NX - i))[kind // 2])
        final = (1, 2, 0) if (kind, hop) == (1, 2) else (3, 4, 0) if (kind, hop) == (3, 4) else None
        sem = self.sems.setdefault(final or shape, len(self.sems))
        if not wait:
            to = me.at_z(sign) if kind in (0, 3) else me.at_x(sign)
            send(ref, ref, self.s_sem.at[kind // 2], self.r_sem.at[sem], to)
        elif not final and shape not in self.waited:
            self.waited.add(shape)
            count = 1 if (kind, hop) in ((0, 4), (2, 2)) else 4 if shape[2] and 2 * shape[2] != (NZ, NX)[kind // 2] else 2
            arrived((self.wx, self.wz)[kind // 2].at[pl.ds(0, count)], self.r_sem.at[sem])

    def finish(self):
        arrived(self.wx.at[pl.ds(0, NZ)], self.r_sem.at[self.sems[1, 2, 0]])
        arrived(self.wz.at[pl.ds(0, NX)], self.r_sem.at[self.sems[3, 4, 0]])

    def sent(self):
        arrived(self.wx.at[pl.ds(0, NZ * NX - 1)], self.s_sem.at[0])
        arrived(self.wz.at[pl.ds(0, NZ * NX - 1)], self.s_sem.at[1])


def onehot(hit):
    return jnp.where(hit, 1.0, 0.0).astype(jnp.bfloat16)


def iota(shape, axis):
    return lax.broadcasted_iota(jnp.int32, shape, axis)


def attend_kernel(
    hidden_hbm, w_hbm, group_hbm, blocks, prefix, table_hbm, pool, out,
    hidden, w, group, table, result,
    qx, qz, kx, vz, ab, nb, ssq_s, ssq_r, cs, cb, cr,
    un, pref, pages, pick_send, pick_in, pick_out, pick_home,
    q_send, q_recv, o_send, o_recv, local_out, local_lse, gathered,
    s_ss, r_ss, s_a, r_a, s_b, r_b, s_c, r_c,
    load_sem, s_q, r_q, s_o, r_o,
    *gather_sems,
):
    me = Place()
    x, y, z, t = me.x, me.y, me.z, me.t
    barrier = pltpu.get_barrier_semaphore()
    peers = [
        me.at_z(1), me.at_z(-1), me.at_x(1), me.at_x(-1),
        me.other(True, t), me.other(False, me.t2), me.other(True, me.t2),
        me.other(False, me.t1), me.other(False, me.t3),
    ]
    for peer in peers:
        pl.semaphore_signal(barrier, inc=1, device_id=peer, device_id_type=MESH)
    load_hidden = pltpu.make_async_copy(hidden_hbm, hidden, load_sem.at[2])
    load_w = pltpu.make_async_copy(w_hbm, w, load_sem.at[3])
    load_group = pltpu.make_async_copy(group_hbm, group, load_sem.at[4])
    load_table = pltpu.make_async_copy(table_hbm, table, load_sem.at[5])
    load_hidden.start()
    load_w.start()
    load_group.start()
    load_table.start()
    load_prefix = pltpu.make_async_copy(prefix, pref, load_sem.at[0])
    load_pages = pltpu.make_async_copy(pool, pages, load_sem.at[1])
    load_prefix.start()
    load_pages.start()

    load_w.wait()
    start = 0
    for part, width in ((qx, QX), (qz, QZ), (kx, KX), (vz, VZ)):
        part[z * NX + x] = w[:, start : start + width]
        start += width
    def build_blocks():
        across = (jnp.bitwise_and(iota((256, 256), 0), 15) * TILE + lax.shift_right_logical(iota((256, 256), 0), 4))
        down = (jnp.bitwise_and(iota((256, 256), 1), 15) * TILE + lax.shift_right_logical(iota((256, 256), 1), 4))
        pick_in[...] = onehot(iota((256, 256), 1) == across)
        pick_out[...] = onehot(iota((256, 256), 0) == down)

    build_blocks()
    q_recv[...] = jnp.zeros_like(q_recv)
    o_recv[...] = jnp.zeros_like(o_recv)
    pl.semaphore_wait(barrier, len(peers))

    g1 = Gather(me, qx, qz, *gather_sems[:2])
    g2 = Gather(me, kx, vz, *gather_sems[2:])

    def run(stretch):
        for code in ORDER[stretch]:
            (g1, g2)[code >> 10 & 1].step(code)

    run(0)
    load_hidden.wait()
    total = jnp.zeros((ROWS, HD), jnp.float32)
    for b in range(10):
        part = hidden[:, b * HD : (b + 1) * HD].astype(jnp.float32)
        total += part * part
    total = jnp.sum(total, axis=-1, keepdims=True)
    flat = jnp.broadcast_to(total, (ROWS, ROWS)).T[:8]
    ssq_s[...] = flat
    for k, tp in ((1, me.t1), (2, me.t2), (3, me.t3)):
        send(ssq_s, ssq_r.at[k], s_ss, r_ss, me.other(False, tp))
    load_group.wait()
    load_table.wait()
    group_rows = jnp.broadcast_to(group[...], (ROWS, ROWS)).T

    def build_picks():
        shape = (ROWS, ROWS)
        down = jnp.bitwise_and(iota(shape, 0), N_ROLL - 1) * 2 + lax.shift_right_logical(iota(shape, 0), 6)
        across = jnp.bitwise_and(iota(shape, 1), N_ROLL - 1) * 2 + lax.shift_right_logical(iota(shape, 1), 6)
        pick_send[...] = onehot(group[...] == down)
        pick_home[:, :ROWS] = onehot(group_rows == across)
        pick_home[:, ROWS:] = onehot(lax.shift_right_logical(group_rows, 1) == iota(shape, 1))

    def gather_pages():
        load_pages.wait()

        def one(s, carry):
            for j in range(SPAGES):
                gathered[s, j] = pages[table[j, s]]
            return carry

        lax.fori_loop(0, ROWS, one, 0, unroll=8)

    ssum = flat
    arrived(ssq_r.at[pl.ds(1, 3)], r_ss)
    for k in (1, 2, 3):
        ssum += ssq_r[k]
    scale = lax.rsqrt(ssum / D + 1e-06)
    scale = jnp.broadcast_to(scale[:1], (ROWS, ROWS)).T
    tiles = [hidden[:, b * HD : (b + 1) * HD].astype(jnp.float32) * scale for b in range(10)]
    turned = {b: pltpu.roll(tiles[b], HD // 2, 1) for b in range(2, 8)}
    low_half = iota((ROWS, HD), 1) < HD // 2

    def halves(first, second):
        return jnp.where(low_half, first, second)

    sides = (
        (tiles[0], tiles[1], halves(tiles[2], turned[5]), halves(turned[5], turned[6]), halves(turned[6], turned[7])),
        (halves(turned[2], turned[3]), halves(turned[3], turned[4]), halves(turned[4], tiles[7]), tiles[8], tiles[9]),
    )
    for side in range(2):
        for b in range(5):
            nb[side, :, b * HD : (b + 1) * HD] = sides[side][b].astype(jnp.bfloat16)
    ab[2 * t + y] = nb[y]
    send(nb.at[me.ty], ab.at[2 * t + y], s_a, r_a, me.other(True, t))
    send(nb.at[y], ab.at[2 * t + y], s_a, r_a, me.other(False, me.t2))
    send(nb.at[me.ty], ab.at[2 * t + y], s_a, r_a, me.other(True, me.t2))
    sibling = me.other(False, me.t1)
    send(nb.at[y], ab.at[2 * t + y], s_b, r_b, sibling)

    def pass_rows():
        arrived(ab.at[pl.ds(0, 3)], r_a)
        for row in (2 * t + me.ty, 2 * me.t2 + y, 2 * me.t2 + me.ty):
            send(ab.at[row], ab.at[row], s_b, r_b, sibling)

    partner = me.other(True, t)

    def product(block, src, at, width, r_sem):
        acc = jnp.zeros((2 * ROWS, width), jnp.float32)
        for tp in range(4):
            acc += jnp.dot(
                ab[2 * tp : 2 * tp + 2].reshape(2 * ROWS, 640),
                src[8 * tp : 8 * tp + 8, :, at : at + width].reshape(640, width),
                preferred_element_type=jnp.float32,
            )
        blocks_of = pl.ds(block, width // HD)
        for b in range(width // HD):
            cs[block + b] = acc[:, b * HD : (b + 1) * HD].reshape(2, ROWS, HD)
            cb[block + b] = cs[block + b, me.ty].astype(jnp.bfloat16)
        send(cb.at[blocks_of], cr.at[blocks_of], s_c, r_sem, partner)

    def total_of(block, count, r_sem):
        arrived(cr.at[pl.ds(block, count)], r_sem)
        for b in range(block, block + count):
            un[:, b * HD : (b + 1) * HD] = (cs[b, y] + cr[b].astype(jnp.float32)).astype(jnp.bfloat16)

    run(1)
    run(2)
    run(3)
    build_picks()
    pass_rows()
    run(4)
    g1.finish()
    arrived(ab.at[pl.ds(0, 4)], r_b)
    product(3, qz, 0, 256, r_c.at[0])
    product(0, qx, 0, 256, r_c.at[0])
    product(2, qx, 256, 128, r_c.at[0])
    run(5)
    total_of(0, 5, r_c.at[0])

    by_owner = jnp.dot(
        pick_send[...], un[:, : REPEAT * HD], preferred_element_type=jnp.float32
    ).astype(jnp.bfloat16)
    for b in range(4):
        parts = [
            by_owner[j * N_ROLL + b * TILE : j * N_ROLL + (b + 1) * TILE, h * HD : (h + 1) * HD]
            for j in range(2) for h in range(REPEAT)
        ]
        stacked = jnp.concatenate(parts + [jnp.zeros((6 * TILE, HD), jnp.bfloat16)], axis=0)
        q_send[b * TILE : (b + 1) * TILE] = jnp.dot(
            pick_out[...], stacked, preferred_element_type=jnp.float32
        ).astype(jnp.bfloat16).reshape(TILE, TILE, HD)

    def exchange(src, dst, rows, s_sem, r_sem):
        here = y * NX + x
        for dz in (4, 3, 5, 2, 6, 1, 7, 0):

            def one(i, carry):
                peer = me.zn(dz) * (NX * NY) + lax.rem(here + i, NX * NY)
                pltpu.make_async_remote_copy(
                    src_ref=src.at[peer, pl.ds(0, rows)], dst_ref=dst.at[me.r, pl.ds(0, rows)],
                    send_sem=s_sem, recv_sem=r_sem,
                    device_id={"roll": peer, "tp": t}, device_id_type=MESH,
                ).start()
                return carry

            lax.fori_loop(1 if dz == 0 else 0, NX * NY, one, 0)
        dst[me.r] = src[me.r]

    def all_of(ref, rows, sem):
        arrived(ref.at[pl.ds(0, N_ROLL - 1), pl.ds(0, rows)], sem)

    exchange(q_send, q_recv, 10, s_q, r_q)
    run(6)
    gather_pages()
    g2.finish()
    product(5, kx, 0, 128, r_c.at[1])
    product(6, vz, 0, 128, r_c.at[1])

    def local_block(b, carry):
        at = pl.ds(pl.multiple_of(b * SB, SB), SB)
        queries = jnp.concatenate([un[at, h * HD : (h + 1) * HD] for h in range(REPEAT)], axis=0)
        own_k = un[at, REPEAT * HD : (REPEAT + 1) * HD].astype(jnp.float32)
        own_v = un[at, (REPEAT + 1) * HD :].astype(jnp.float32)
        own_k = jnp.concatenate([own_k] * REPEAT, axis=0)
        own_v = jnp.concatenate([own_v] * REPEAT, axis=0)
        keys = gathered[at, :, :, :HD].reshape(SB * KEYS, HD)
        values = gathered[at, :, :, HD:].reshape(SB * KEYS, HD)
        scores = lax.dot_general(
            queries, keys, (((1,), (1,)), ((), ())), preferred_element_type=jnp.float32
        ) * SCALE
        shape = (REPEAT * SB, SB * KEYS)
        mine = jnp.bitwise_and(iota(shape, 0), SB - 1) == lax.shift_right_logical(iota(shape, 1), 5)
        scores = jnp.where(mine, scores, MASKED)
        own = jnp.sum(queries.astype(jnp.float32) * own_k, axis=-1, keepdims=True) * SCALE
        top = jnp.maximum(jnp.max(scores, axis=-1, keepdims=True), own)
        e = jnp.exp(scores - top)
        e_own = jnp.exp(own - top)
        total = jnp.sum(e, axis=-1, keepdims=True) + e_own
        weights = (e / total).astype(jnp.bfloat16)
        w_own = (e_own / total).astype(jnp.bfloat16).astype(jnp.float32)
        res = jnp.dot(weights, values, preferred_element_type=jnp.float32) + w_own * own_v
        lse = jnp.broadcast_to(top + jnp.log(total), (REPEAT * SB, HD))
        for h in range(REPEAT):
            local_out[h, at, :] = res[h * SB : (h + 1) * SB]
            local_lse[h, at, :] = lse[h * SB : (h + 1) * SB]
        return carry

    load_prefix.wait()
    all_of(q_recv, 10, r_q)
    came = q_recv[...].reshape(N_ROLL * TILE, HD)
    per = REPEAT * N_ROLL
    part = REPEAT * TILE
    turned = [
        jnp.dot(
            pick_in[: 2 * part, :], came[b * 256 : (b + 1) * 256], preferred_element_type=jnp.float32
        ).astype(jnp.bfloat16)
        for b in range(4)
    ]
    outs, marks = [], [jnp.zeros((TILE, HD), jnp.float32)] * 4
    for j in range(2):
        queries = jnp.concatenate([q[j * part : (j + 1) * part] for q in turned], axis=0)
        scores = lax.dot_general(
            queries, pref[j, :, :HD], (((1,), (1,)), ((), ())), preferred_element_type=jnp.float32
        ) * SCALE
        scores = jnp.where(iota(scores.shape, 1) < blocks[j] * BLOCK, scores, MASKED)
        top = jnp.max(scores, axis=-1, keepdims=True)
        e = jnp.exp(scores - top)
        total = jnp.sum(e, axis=-1, keepdims=True)
        weights = (e / total).astype(jnp.bfloat16)
        res = jnp.dot(weights, pref[j, :, HD:], preferred_element_type=jnp.float32)
        outs.append(res.astype(jnp.bfloat16))
        lse = jnp.broadcast_to(top + jnp.log(total), (per, HD))
        hi = lse.astype(jnp.bfloat16).astype(jnp.float32)
        mid = (lse - hi).astype(jnp.bfloat16).astype(jnp.float32)
        low = lse - hi - mid
        lane = iota((TILE, HD), 1)
        for b in range(4):
            for h in range(REPEAT):
                first = (j * REPEAT + h) * 3
                at = slice(b * part + h * TILE, b * part + (h + 1) * TILE)
                marks[b] = jnp.where(
                    lane == first, hi[at], jnp.where(lane == first + 1, mid[at], jnp.where(lane == first + 2, low[at], marks[b]))
                )
    for b in range(4):
        rows = slice(b * part, (b + 1) * part)
        stacked = jnp.concatenate(
            [outs[0][rows], outs[1][rows], marks[b].astype(jnp.bfloat16), jnp.zeros((5 * TILE, HD), jnp.bfloat16)], axis=0
        )
        o_send[b * TILE : (b + 1) * TILE] = jnp.dot(
            pick_out[...], stacked, preferred_element_type=jnp.float32
        ).astype(jnp.bfloat16).reshape(TILE, TILE, HD)
    exchange(o_send, o_recv, 12, s_o, r_o)
    total_of(5, 2, r_c.at[1])
    lax.fori_loop(0, ROWS // SB, local_block, 0)
    all_of(o_recv, 12, r_o)
    came = o_recv[...].reshape(N_ROLL * TILE, HD)
    turned = [
        jnp.dot(
            pick_in[: 11 * TILE, :], came[b * 256 : (b + 1) * 256], preferred_element_type=jnp.float32
        ).astype(jnp.bfloat16)
        for b in range(4)
    ]
    by_head = [
        jnp.concatenate(
            [turned[b][(j * REPEAT + h) * TILE : (j * REPEAT + h + 1) * TILE] for j in range(2) for b in range(4)], axis=0
        )
        for h in range(REPEAT)
    ]
    marks = [turned[b][10 * TILE : 11 * TILE] for b in range(4)] + [jnp.zeros((N_ROLL, HD), jnp.bfloat16)]
    terms = jnp.dot(
        pick_home[:, ROWS:], jnp.concatenate(marks, axis=0), preferred_element_type=jnp.float32
    )
    back = jnp.dot(
        pick_home[:, :ROWS], jnp.concatenate(by_head, axis=1), preferred_element_type=jnp.float32
    )
    second = jnp.bitwise_and(group_rows, 1) * REPEAT
    lane = iota((ROWS, HD), 1)
    for h in range(REPEAT):
        first = (second + h) * 3
        mine = jnp.where((lane >= first) & (lane < first + 3), terms, 0.0)
        p_lse = jnp.broadcast_to(jnp.sum(mine, axis=-1, keepdims=True), (ROWS, HD))
        l_lse = local_lse[h]
        top = jnp.maximum(p_lse, l_lse)
        ep = jnp.exp(p_lse - top)
        el = jnp.exp(l_lse - top)
        mixed = (ep * back[:, h * HD : (h + 1) * HD] + el * local_out[h]) / (ep + el)
        cols = slice(h * HD, (h + 1) * HD)
        result[:, cols] = mixed.astype(jnp.bfloat16)
        pltpu.make_async_copy(result.at[:, cols], out.at[:, cols], load_sem.at[6]).start()

    arrived(result, load_sem.at[6])
    all_of(q_send, 10, s_q)
    all_of(o_send, 12, s_o)
    g1.sent()
    g2.sent()
    arrived(ssq_r.at[pl.ds(1, 3)], s_ss)
    arrived(ab.at[pl.ds(0, 3)], s_a)
    arrived(ab.at[pl.ds(0, 4)], s_b)
    arrived(cb.at[pl.ds(0, 7)], s_c)


def per_device(
    hidden_in, qkv_weight, sample_group, prefix_blocks, prefix_kv, page_table, suffix_pool
):
    dma = pltpu.SemaphoreType.DMA
    vmem = pl.BlockSpec(memory_space=pltpu.VMEM)
    smem = pl.BlockSpec(memory_space=pltpu.SMEM)
    hbm = pl.BlockSpec(memory_space=pl.ANY)
    bf16, f32 = jnp.bfloat16, jnp.float32
    sems = [dma] * 7 + [dma((2,))]
    gather_sems = []
    for _ in range(2):
        gather_sems += [dma((2,)), dma((22,))]
    tiles = pltpu.VMEM((N_ROLL, TILE, HD), bf16)
    return pl.pallas_call(
        attend_kernel,
        out_shape=jax.ShapeDtypeStruct((ROWS, REPEAT * HD), bf16),
        in_specs=[hbm, hbm, hbm, smem, hbm, hbm, hbm],
        out_specs=hbm,
        scratch_shapes=[
            pltpu.VMEM((ROWS, 10 * HD), bf16),
            pltpu.VMEM((SHARD, QX + QZ + KX + VZ), bf16),
            pltpu.VMEM((1, ROWS), jnp.int32),
            pltpu.SMEM((SPAGES, ROWS), jnp.int32),
            pltpu.VMEM((ROWS, REPEAT * HD), bf16),
            *(pltpu.VMEM((NZ * NX, SHARD, width), bf16) for width in (QX, QZ, KX, VZ)),
            pltpu.VMEM((8, ROWS, 640), bf16),
            pltpu.VMEM((2, ROWS, 640), bf16),
            pltpu.VMEM((8, ROWS), f32),
            pltpu.VMEM((4, 8, ROWS), f32),
            pltpu.VMEM((7, 2, ROWS, HD), f32),
            pltpu.VMEM((7, ROWS, HD), bf16),
            pltpu.VMEM((7, ROWS, HD), bf16),
            pltpu.VMEM((ROWS, QX + QZ + KX + VZ), bf16),
            pltpu.VMEM(prefix_kv.shape, bf16),
            pltpu.VMEM(suffix_pool.shape, bf16),
            pltpu.VMEM((ROWS, ROWS), bf16),
            pltpu.VMEM((256, 256), bf16),
            pltpu.VMEM((256, 256), bf16),
            pltpu.VMEM((ROWS, 2 * ROWS), bf16),
            tiles, tiles, tiles, tiles,
            pltpu.VMEM((REPEAT, ROWS, HD), f32),
            pltpu.VMEM((REPEAT, ROWS, HD), f32),
            pltpu.VMEM((ROWS, SPAGES, PAGE, 2 * HD), bf16),
            *sems,
            dma((7,)), dma, dma, dma, dma,
            *gather_sems,
        ],
        compiler_params=pltpu.CompilerParams(
            collective_id=0, has_side_effects=True, vmem_limit_bytes=62 * 1024 * 1024
        ),
    )(hidden_in, qkv_weight, sample_group.reshape(1, ROWS), prefix_blocks, prefix_kv, page_table.T, suffix_pool)


def solution(mesh):
    in_specs = (
        P("roll", "tp"),
        P("roll", "tp"),
        P("roll"),
        P("roll"),
        P("roll", None, "tp"),
        P("roll", None),
        P("roll", None, "tp"),
    )
    out_specs = P("roll", "tp")
    return jax.shard_map(
        per_device, mesh=mesh, in_specs=in_specs, out_specs=out_specs, check_vma=False
    )
```

```python
import math

import jax
import jax.numpy as jnp
from jax import lax
from jax.experimental import pallas as pl
from jax.experimental.pallas import tpu as pltpu
from jax.sharding import PartitionSpec as P

HEADS = 20
KV_HEADS = 4
HD = 128
BLOCK = 128
PAGE = 16
SPAGES = 2
D = 5120
NX, NY, NZ = 4, 2, 8
ROWS = 128
SHARD = 80
QX, QZ, KX, VZ = 384, 256, 128, 128
N_ROLL = NX * NY * NZ
REPEAT = HEADS // KV_HEADS
TILE = 16
SB = 16
KEYS = SPAGES * PAGE
SCALE = 1.0 / math.sqrt(HD)
MASKED = -1e30
MESH = pl.DeviceIdType.MESH
ORDER = (
    (
        16, 17, 528, 529, 272, 273, 784, 785,
    ),
    (
        1040, 1041, 1552, 1553, 1296, 1297, 1808, 1809, 2576, 2577, 522, 515, 880, 881, 2064, 2065, 496, 497,
        18, 19, 304, 305, 816, 817, 2320, 2321, 2832, 2833, 3088, 3089, 3600, 3601, 258, 786, 787,
    ),
    (
        267, 3344, 3345, 3856, 3857, 1539, 1546, 1521, 1520, 1329, 1328, 2570, 2563, 848, 849, 1291, 1042, 1043,
        2066, 2067, 464, 465, 20, 21, 336, 337,
    ),
    (
        2928, 2929, 2864, 2865, 882, 883, 2544, 2545, 2352, 2353, 818, 819, 490, 483, 2315, 2306, 2834, 2835,
        3594, 3587, 298, 291, 2896, 2897, 850, 851, 3568, 3569, 3376, 3377, 3339, 788, 789, 3090, 3091, 1488,
        1360, 1489, 1905, 2068, 2069, 432, 433, 6, 15, 368, 1904, 369, 2512, 2513, 2384, 2385, 450, 2538,
        459, 2930, 2931, 2866, 2867, 885, 884, 821, 820, 2531, 2346, 331, 322,
    ),
    (
        2898, 2899, 853, 852, 2339, 1361, 1841, 2836, 2837, 783, 774, 1840, 1873, 1872, 2054, 2063, 400, 401,
        1045, 1044, 1811, 1282, 2480, 2481, 2416, 2417, 426, 419, 362, 355, 1514, 1810, 1507, 2507, 1315, 2498,
        1322, 2932, 2933, 2868, 2869, 878, 871, 814, 807, 2379, 2370, 3536, 3537, 3408, 3409, 1474, 1346, 1483,
        1355, 2900, 2901, 847, 838, 2831, 2822, 3952, 3953, 3888, 3889, 1906, 1907, 1842, 1843, 2448, 2449, 386,
        395, 3920, 3921, 1874, 1875, 2474, 3092, 3093, 1457, 1456, 1030, 1039, 1393, 1392, 2467, 2410, 2926, 2919,
        3330, 2862, 3562, 2403, 3522, 2855, 3555, 3858, 3859, 1812, 1813, 3394, 2895, 3363, 3370, 3531, 2886, 3403,
        2443, 3954, 3955, 3890, 3891, 1908, 1909, 1844, 1845, 2434,
    ),
    (
        3922, 3923, 1876, 1877, 3078, 3087, 1424, 1425, 3504, 3505, 3440, 3441, 1450, 1443, 1386, 1379, 3860, 3861,
        1798, 1807, 3956, 3957, 3892, 3893, 1902, 1895, 1838, 1831,
    ),
    (
        3472, 3473, 1410, 1419, 3498, 3924, 3925, 1862, 1871, 3491, 3434, 3427, 3855, 3846, 3950, 3943, 3886, 3467,
        3458, 3879, 3910, 3919,
    ),
)
PIECES = ((0, 48), (48, 32), (0, 80))


class Place:
    def __init__(self):
        self.r = lax.axis_index("roll")
        self.t = lax.axis_index("tp")
        self.x = lax.rem(self.r, NX)
        self.y = lax.rem(lax.div(self.r, NX), NY)
        self.z = lax.div(self.r, NX * NY)
        self.t1 = self.t + 1 - 2 * lax.rem(self.t, 2)
        self.t2 = lax.rem(self.t + 2, 4)
        self.t3 = lax.rem(self.t1 + 2, 4)
        self.ty = 1 - self.y

    def roll(self, z, y, x):
        return (z * NY + y) * NX + x

    def zn(self, k):
        return lax.rem(self.z + k + NZ, NZ)

    def xn(self, k):
        return lax.rem(self.x + k + NX, NX)

    def at_z(self, k):
        return {"roll": self.roll(self.zn(k), self.y, self.x), "tp": self.t}

    def at_x(self, k):
        return {"roll": self.roll(self.z, self.y, self.xn(k)), "tp": self.t}

    def other(self, flip_y, tp):
        y = self.ty if flip_y else self.y
        return {"roll": self.roll(self.z, y, self.x), "tp": tp}


def send(src, dst, s_sem, r_sem, device):
    pltpu.make_async_remote_copy(
        src_ref=src, dst_ref=dst, send_sem=s_sem, recv_sem=r_sem, device_id=device, device_id_type=MESH
    ).start()


def arrived(ref, sem):
    pltpu.make_async_copy(ref, ref, sem).wait()


class Gather:
    def __init__(self, me, wx, wz, s_sem, r_sem):
        self.me, self.wx, self.wz, self.s_sem, self.r_sem = me, wx, wz, s_sem, r_sem
        self.sems, self.waited = {}, set()

    def step(self, code):
        me, wait, key = self.me, code >= 2048, code % 1024
        kind, i, rows, hop, way = key >> 8, key >> 5 & 7, PIECES[key >> 3 & 3], (key >> 1 & 3) + 1, key & 1
        sign = 1 - 2 * way
        back = -sign * (hop if wait else hop - 1)
        ref, z, x = (
            (self.wx, me.zn(back), me.x),
            (self.wx, me.zn(i), me.xn(back)),
            (self.wz, me.z, me.xn(back)),
            (self.wz, me.zn(back), me.xn(i)),
        )[kind]
        ref = ref.at[z * NX + x, pl.ds(*rows)]
        shape = (kind, hop, (min(i, NZ - i), min(i, NX - i))[kind // 2])
        final = (1, 2, 0) if (kind, hop) == (1, 2) else (3, 4, 0) if (kind, hop) == (3, 4) else None
        sem = self.sems.setdefault(final or shape, len(self.sems))
        if not wait:
            to = me.at_z(sign) if kind in (0, 3) else me.at_x(sign)
            send(ref, ref, self.s_sem.at[kind // 2], self.r_sem.at[sem], to)
        elif not final and shape not in self.waited:
            self.waited.add(shape)
            count = 1 if (kind, hop) in ((0, 4), (2, 2)) else 4 if shape[2] and 2 * shape[2] != (NZ, NX)[kind // 2] else 2
            arrived((self.wx, self.wz)[kind // 2].at[pl.ds(0, count)], self.r_sem.at[sem])

    def finish(self):
        arrived(self.wx.at[pl.ds(0, NZ)], self.r_sem.at[self.sems[1, 2, 0]])
        arrived(self.wz.at[pl.ds(0, NX)], self.r_sem.at[self.sems[3, 4, 0]])

    def sent(self):
        arrived(self.wx.at[pl.ds(0, NZ * NX - 1)], self.s_sem.at[0])
        arrived(self.wz.at[pl.ds(0, NZ * NX - 1)], self.s_sem.at[1])


def onehot(hit):
    return jnp.where(hit, 1.0, 0.0).astype(jnp.bfloat16)


def iota(shape, axis):
    return lax.broadcasted_iota(jnp.int32, shape, axis)


def attend_kernel(
    hidden_hbm, w_hbm, group_hbm, blocks, prefix, table_hbm, pool, out,
    hidden, w, group, table, result,
    qx, qz, kx, vz, ab, nb, ssq_s, ssq_r, cs, cb, cr,
    un, pref, pages, pick_send, pick_in, pick_out, pick_home,
    q_send, q_recv, o_send, o_recv, local_out, local_lse, gathered,
    s_ss, r_ss, s_a, r_a, s_b, r_b, s_c, r_c,
    load_sem, s_q, r_q, s_o, r_o,
    *gather_sems,
):
    me = Place()
    x, y, z, t = me.x, me.y, me.z, me.t
    barrier = pltpu.get_barrier_semaphore()
    peers = [
        me.at_z(1), me.at_z(-1), me.at_x(1), me.at_x(-1),
        me.other(True, t), me.other(False, me.t2), me.other(True, me.t2),
        me.other(False, me.t1), me.other(False, me.t3),
    ]
    for peer in peers:
        pl.semaphore_signal(barrier, inc=1, device_id=peer, device_id_type=MESH)
    load_hidden = pltpu.make_async_copy(hidden_hbm, hidden, load_sem.at[2])
    load_w = pltpu.make_async_copy(w_hbm, w, load_sem.at[3])
    load_group = pltpu.make_async_copy(group_hbm, group, load_sem.at[4])
    load_table = pltpu.make_async_copy(table_hbm, table, load_sem.at[5])
    load_hidden.start()
    load_w.start()
    load_group.start()
    load_table.start()
    load_prefix = pltpu.make_async_copy(prefix, pref, load_sem.at[0])
    load_pages = pltpu.make_async_copy(pool, pages, load_sem.at[1])
    load_prefix.start()
    load_pages.start()

    load_w.wait()
    start = 0
    for part, width in ((qx, QX), (qz, QZ), (kx, KX), (vz, VZ)):
        part[z * NX + x] = w[:, start : start + width]
        start += width
    def build_blocks():
        across = (jnp.bitwise_and(iota((256, 256), 0), 15) * TILE + lax.shift_right_logical(iota((256, 256), 0), 4))
        down = (jnp.bitwise_and(iota((256, 256), 1), 15) * TILE + lax.shift_right_logical(iota((256, 256), 1), 4))
        pick_in[...] = onehot(iota((256, 256), 1) == across)
        pick_out[...] = onehot(iota((256, 256), 0) == down)

    build_blocks()
    q_recv[...] = jnp.zeros_like(q_recv)
    o_recv[...] = jnp.zeros_like(o_recv)
    pl.semaphore_wait(barrier, len(peers))

    g1 = Gather(me, qx, qz, *gather_sems[:2])
    g2 = Gather(me, kx, vz, *gather_sems[2:])

    def run(stretch):
        for code in ORDER[stretch]:
            (g1, g2)[code >> 10 & 1].step(code)

    run(0)
    load_hidden.wait()
    total = jnp.zeros((ROWS, HD), jnp.float32)
    for b in range(10):
        part = hidden[:, b * HD : (b + 1) * HD].astype(jnp.float32)
        total += part * part
    total = jnp.sum(total, axis=-1, keepdims=True)
    flat = jnp.broadcast_to(total, (ROWS, ROWS)).T[:8]
    ssq_s[...] = flat
    for k, tp in ((1, me.t1), (2, me.t2), (3, me.t3)):
        send(ssq_s, ssq_r.at[k], s_ss, r_ss, me.other(False, tp))
    load_group.wait()
    load_table.wait()
    group_rows = jnp.broadcast_to(group[...], (ROWS, ROWS)).T

    def build_picks():
        shape = (ROWS, ROWS)
        down = jnp.bitwise_and(iota(shape, 0), N_ROLL - 1) * 2 + lax.shift_right_logical(iota(shape, 0), 6)
        across = jnp.bitwise_and(iota(shape, 1), N_ROLL - 1) * 2 + lax.shift_right_logical(iota(shape, 1), 6)
        pick_send[...] = onehot(group[...] == down)
        pick_home[:, :ROWS] = onehot(group_rows == across)
        pick_home[:, ROWS:] = onehot(lax.shift_right_logical(group_rows, 1) == iota(shape, 1))

    def gather_pages():
        load_pages.wait()

        def one(s, carry):
            for j in range(SPAGES):
                gathered[s, j] = pages[table[j, s]]
            return carry

        lax.fori_loop(0, ROWS, one, 0, unroll=8)

    ssum = flat
    arrived(ssq_r.at[pl.ds(1, 3)], r_ss)
    for k in (1, 2, 3):
        ssum += ssq_r[k]
    scale = lax.rsqrt(ssum / D + 1e-06)
    scale = jnp.broadcast_to(scale[:1], (ROWS, ROWS)).T
    tiles = [hidden[:, b * HD : (b + 1) * HD].astype(jnp.float32) * scale for b in range(10)]
    turned = {b: pltpu.roll(tiles[b], HD // 2, 1) for b in range(2, 8)}
    low_half = iota((ROWS, HD), 1) < HD // 2

    def halves(first, second):
        return jnp.where(low_half, first, second)

    sides = (
        (tiles[0], tiles[1], halves(tiles[2], turned[5]), halves(turned[5], turned[6]), halves(turned[6], turned[7])),
        (halves(turned[2], turned[3]), halves(turned[3], turned[4]), halves(turned[4], tiles[7]), tiles[8], tiles[9]),
    )
    for side in range(2):
        for b in range(5):
            nb[side, :, b * HD : (b + 1) * HD] = sides[side][b].astype(jnp.bfloat16)
    ab[2 * t + y] = nb[y]
    send(nb.at[me.ty], ab.at[2 * t + y], s_a, r_a, me.other(True, t))
    send(nb.at[y], ab.at[2 * t + y], s_a, r_a, me.other(False, me.t2))
    send(nb.at[me.ty], ab.at[2 * t + y], s_a, r_a, me.other(True, me.t2))
    sibling = me.other(False, me.t1)
    send(nb.at[y], ab.at[2 * t + y], s_b, r_b, sibling)

    def pass_rows():
        arrived(ab.at[pl.ds(0, 3)], r_a)
        for row in (2 * t + me.ty, 2 * me.t2 + y, 2 * me.t2 + me.ty):
            send(ab.at[row], ab.at[row], s_b, r_b, sibling)

    partner = me.other(True, t)

    def product(block, src, at, width, r_sem):
        acc = jnp.zeros((2 * ROWS, width), jnp.float32)
        for tp in range(4):
            acc += jnp.dot(
                ab[2 * tp : 2 * tp + 2].reshape(2 * ROWS, 640),
                src[8 * tp : 8 * tp + 8, :, at : at + width].reshape(640, width),
                preferred_element_type=jnp.float32,
            )
        blocks_of = pl.ds(block, width // HD)
        for b in range(width // HD):
            cs[block + b] = acc[:, b * HD : (b + 1) * HD].reshape(2, ROWS, HD)
            cb[block + b] = cs[block + b, me.ty].astype(jnp.bfloat16)
        send(cb.at[blocks_of], cr.at[blocks_of], s_c, r_sem, partner)

    def total_of(block, count, r_sem):
        arrived(cr.at[pl.ds(block, count)], r_sem)
        for b in range(block, block + count):
            un[:, b * HD : (b + 1) * HD] = (cs[b, y] + cr[b].astype(jnp.float32)).astype(jnp.bfloat16)

    run(1)
    run(2)
    run(3)
    build_picks()
    pass_rows()
    run(4)
    g1.finish()
    arrived(ab.at[pl.ds(0, 4)], r_b)
    product(2, qx, 256, 128, r_c.at[0])
    product(3, qz, 0, 256, r_c.at[0])
    product(0, qx, 0, 256, r_c.at[0])
    run(5)
    total_of(0, 5, r_c.at[0])

    by_owner = jnp.dot(
        pick_send[...], un[:, : REPEAT * HD], preferred_element_type=jnp.float32
    ).astype(jnp.bfloat16)
    for b in range(4):
        parts = [
            by_owner[j * N_ROLL + b * TILE : j * N_ROLL + (b + 1) * TILE, h * HD : (h + 1) * HD]
            for j in range(2) for h in range(REPEAT)
        ]
        stacked = jnp.concatenate(parts + [jnp.zeros((6 * TILE, HD), jnp.bfloat16)], axis=0)
        q_send[b * TILE : (b + 1) * TILE] = jnp.dot(
            pick_out[...], stacked, preferred_element_type=jnp.float32
        ).astype(jnp.bfloat16).reshape(TILE, TILE, HD)

    def exchange(src, dst, rows, s_sem, r_sem):
        here = y * NX + x
        for dz in (4, 3, 5, 2, 6, 1, 7, 0):

            def one(i, carry):
                peer = me.zn(dz) * (NX * NY) + lax.rem(here + i, NX * NY)
                pltpu.make_async_remote_copy(
                    src_ref=src.at[peer, pl.ds(0, rows)], dst_ref=dst.at[me.r, pl.ds(0, rows)],
                    send_sem=s_sem, recv_sem=r_sem,
                    device_id={"roll": peer, "tp": t}, device_id_type=MESH,
                ).start()
                return carry

            lax.fori_loop(1 if dz == 0 else 0, NX * NY, one, 0)
        dst[me.r] = src[me.r]

    def all_of(ref, rows, sem):
        arrived(ref.at[pl.ds(0, N_ROLL - 1), pl.ds(0, rows)], sem)

    exchange(q_send, q_recv, 10, s_q, r_q)
    run(6)
    gather_pages()
    g2.finish()
    product(5, kx, 0, 128, r_c.at[1])
    product(6, vz, 0, 128, r_c.at[1])

    def local_block(b, carry):
        at = pl.ds(pl.multiple_of(b * SB, SB), SB)
        queries = jnp.concatenate([un[at, h * HD : (h + 1) * HD] for h in range(REPEAT)], axis=0)
        own_k = un[at, REPEAT * HD : (REPEAT + 1) * HD].astype(jnp.float32)
        own_v = un[at, (REPEAT + 1) * HD :].astype(jnp.float32)
        own_k = jnp.concatenate([own_k] * REPEAT, axis=0)
        own_v = jnp.concatenate([own_v] * REPEAT, axis=0)
        keys = gathered[at, :, :, :HD].reshape(SB * KEYS, HD)
        values = gathered[at, :, :, HD:].reshape(SB * KEYS, HD)
        scores = lax.dot_general(
            queries, keys, (((1,), (1,)), ((), ())), preferred_element_type=jnp.float32
        ) * SCALE
        shape = (REPEAT * SB, SB * KEYS)
        mine = jnp.bitwise_and(iota(shape, 0), SB - 1) == lax.shift_right_logical(iota(shape, 1), 5)
        scores = jnp.where(mine, scores, MASKED)
        own = jnp.sum(queries.astype(jnp.float32) * own_k, axis=-1, keepdims=True) * SCALE
        top = jnp.maximum(jnp.max(scores, axis=-1, keepdims=True), own)
        e = jnp.exp(scores - top)
        e_own = jnp.exp(own - top)
        total = jnp.sum(e, axis=-1, keepdims=True) + e_own
        weights = (e / total).astype(jnp.bfloat16)
        w_own = (e_own / total).astype(jnp.bfloat16).astype(jnp.float32)
        res = jnp.dot(weights, values, preferred_element_type=jnp.float32) + w_own * own_v
        lse = jnp.broadcast_to(top + jnp.log(total), (REPEAT * SB, HD))
        for h in range(REPEAT):
            local_out[h, at, :] = res[h * SB : (h + 1) * SB]
            local_lse[h, at, :] = lse[h * SB : (h + 1) * SB]
        return carry

    load_prefix.wait()
    all_of(q_recv, 10, r_q)
    came = q_recv[...].reshape(N_ROLL * TILE, HD)
    per = REPEAT * N_ROLL
    part = REPEAT * TILE
    turned = [
        jnp.dot(
            pick_in[: 2 * part, :], came[b * 256 : (b + 1) * 256], preferred_element_type=jnp.float32
        ).astype(jnp.bfloat16)
        for b in range(4)
    ]
    outs, marks = [], [jnp.zeros((TILE, HD), jnp.float32)] * 4
    for j in range(2):
        queries = jnp.concatenate([q[j * part : (j + 1) * part] for q in turned], axis=0)
        scores = lax.dot_general(
            queries, pref[j, :, :HD], (((1,), (1,)), ((), ())), preferred_element_type=jnp.float32
        ) * SCALE
        scores = jnp.where(iota(scores.shape, 1) < blocks[j] * BLOCK, scores, MASKED)
        top = jnp.max(scores, axis=-1, keepdims=True)
        e = jnp.exp(scores - top)
        total = jnp.sum(e, axis=-1, keepdims=True)
        weights = (e / total).astype(jnp.bfloat16)
        res = jnp.dot(weights, pref[j, :, HD:], preferred_element_type=jnp.float32)
        outs.append(res.astype(jnp.bfloat16))
        lse = jnp.broadcast_to(top + jnp.log(total), (per, HD))
        hi = lse.astype(jnp.bfloat16).astype(jnp.float32)
        mid = (lse - hi).astype(jnp.bfloat16).astype(jnp.float32)
        low = lse - hi - mid
        lane = iota((TILE, HD), 1)
        for b in range(4):
            for h in range(REPEAT):
                first = (j * REPEAT + h) * 3
                at = slice(b * part + h * TILE, b * part + (h + 1) * TILE)
                marks[b] = jnp.where(
                    lane == first, hi[at], jnp.where(lane == first + 1, mid[at], jnp.where(lane == first + 2, low[at], marks[b]))
                )
    for b in range(4):
        rows = slice(b * part, (b + 1) * part)
        stacked = jnp.concatenate(
            [outs[0][rows], outs[1][rows], marks[b].astype(jnp.bfloat16), jnp.zeros((5 * TILE, HD), jnp.bfloat16)], axis=0
        )
        o_send[b * TILE : (b + 1) * TILE] = jnp.dot(
            pick_out[...], stacked, preferred_element_type=jnp.float32
        ).astype(jnp.bfloat16).reshape(TILE, TILE, HD)
    exchange(o_send, o_recv, 12, s_o, r_o)
    total_of(5, 2, r_c.at[1])
    lax.fori_loop(0, ROWS // SB, local_block, 0)
    all_of(o_recv, 12, r_o)
    came = o_recv[...].reshape(N_ROLL * TILE, HD)
    turned = [
        jnp.dot(
            pick_in[: 11 * TILE, :], came[b * 256 : (b + 1) * 256], preferred_element_type=jnp.float32
        ).astype(jnp.bfloat16)
        for b in range(4)
    ]
    by_head = [
        jnp.concatenate(
            [turned[b][(j * REPEAT + h) * TILE : (j * REPEAT + h + 1) * TILE] for j in range(2) for b in range(4)], axis=0
        )
        for h in range(REPEAT)
    ]
    marks = [turned[b][10 * TILE : 11 * TILE] for b in range(4)] + [jnp.zeros((N_ROLL, HD), jnp.bfloat16)]
    terms = jnp.dot(
        pick_home[:, ROWS:], jnp.concatenate(marks, axis=0), preferred_element_type=jnp.float32
    )
    back = jnp.dot(
        pick_home[:, :ROWS], jnp.concatenate(by_head, axis=1), preferred_element_type=jnp.float32
    )
    second = jnp.bitwise_and(group_rows, 1) * REPEAT
    lane = iota((ROWS, HD), 1)
    for h in range(REPEAT):
        first = (second + h) * 3
        mine = jnp.where((lane >= first) & (lane < first + 3), terms, 0.0)
        p_lse = jnp.broadcast_to(jnp.sum(mine, axis=-1, keepdims=True), (ROWS, HD))
        l_lse = local_lse[h]
        top = jnp.maximum(p_lse, l_lse)
        ep = jnp.exp(p_lse - top)
        el = jnp.exp(l_lse - top)
        mixed = (ep * back[:, h * HD : (h + 1) * HD] + el * local_out[h]) / (ep + el)
        cols = slice(h * HD, (h + 1) * HD)
        result[:, cols] = mixed.astype(jnp.bfloat16)
        pltpu.make_async_copy(result.at[:, cols], out.at[:, cols], load_sem.at[6]).start()

    arrived(result, load_sem.at[6])
    all_of(q_send, 10, s_q)
    all_of(o_send, 12, s_o)
    g1.sent()
    g2.sent()
    arrived(ssq_r.at[pl.ds(1, 3)], s_ss)
    arrived(ab.at[pl.ds(0, 3)], s_a)
    arrived(ab.at[pl.ds(0, 4)], s_b)
    arrived(cb.at[pl.ds(0, 7)], s_c)


def per_device(
    hidden_in, qkv_weight, sample_group, prefix_blocks, prefix_kv, page_table, suffix_pool
):
    dma = pltpu.SemaphoreType.DMA
    vmem = pl.BlockSpec(memory_space=pltpu.VMEM)
    smem = pl.BlockSpec(memory_space=pltpu.SMEM)
    hbm = pl.BlockSpec(memory_space=pl.ANY)
    bf16, f32 = jnp.bfloat16, jnp.float32
    sems = [dma] * 7 + [dma((2,))]
    gather_sems = []
    for _ in range(2):
        gather_sems += [dma((2,)), dma((22,))]
    tiles = pltpu.VMEM((N_ROLL, TILE, HD), bf16)
    return pl.pallas_call(
        attend_kernel,
        out_shape=jax.ShapeDtypeStruct((ROWS, REPEAT * HD), bf16),
        in_specs=[hbm, hbm, hbm, smem, hbm, hbm, hbm],
        out_specs=hbm,
        scratch_shapes=[
            pltpu.VMEM((ROWS, 10 * HD), bf16),
            pltpu.VMEM((SHARD, QX + QZ + KX + VZ), bf16),
            pltpu.VMEM((1, ROWS), jnp.int32),
            pltpu.SMEM((SPAGES, ROWS), jnp.int32),
            pltpu.VMEM((ROWS, REPEAT * HD), bf16),
            *(pltpu.VMEM((NZ * NX, SHARD, width), bf16) for width in (QX, QZ, KX, VZ)),
            pltpu.VMEM((8, ROWS, 640), bf16),
            pltpu.VMEM((2, ROWS, 640), bf16),
            pltpu.VMEM((8, ROWS), f32),
            pltpu.VMEM((4, 8, ROWS), f32),
            pltpu.VMEM((7, 2, ROWS, HD), f32),
            pltpu.VMEM((7, ROWS, HD), bf16),
            pltpu.VMEM((7, ROWS, HD), bf16),
            pltpu.VMEM((ROWS, QX + QZ + KX + VZ), bf16),
            pltpu.VMEM(prefix_kv.shape, bf16),
            pltpu.VMEM(suffix_pool.shape, bf16),
            pltpu.VMEM((ROWS, ROWS), bf16),
            pltpu.VMEM((256, 256), bf16),
            pltpu.VMEM((256, 256), bf16),
            pltpu.VMEM((ROWS, 2 * ROWS), bf16),
            tiles, tiles, tiles, tiles,
            pltpu.VMEM((REPEAT, ROWS, HD), f32),
            pltpu.VMEM((REPEAT, ROWS, HD), f32),
            pltpu.VMEM((ROWS, SPAGES, PAGE, 2 * HD), bf16),
            *sems,
            dma((7,)), dma, dma, dma, dma,
            *gather_sems,
        ],
        compiler_params=pltpu.CompilerParams(
            collective_id=0, has_side_effects=True, vmem_limit_bytes=62 * 1024 * 1024
        ),
    )(hidden_in, qkv_weight, sample_group.reshape(1, ROWS), prefix_blocks, prefix_kv, page_table.T, suffix_pool)


def solution(mesh):
    in_specs = (
        P("roll", "tp"),
        P("roll", "tp"),
        P("roll"),
        P("roll"),
        P("roll", None, "tp"),
        P("roll", None),
        P("roll", None, "tp"),
    )
    out_specs = P("roll", "tp")
    return jax.shard_map(
        per_device, mesh=mesh, in_specs=in_specs, out_specs=out_specs, check_vma=False
    )
```
